32 devices in a mesh: groups: 2 (over y), src: 4 (over x, core), tgt: 4 (over z).
Axes of the slice: x: 2, y: 2, z: 4, core: 2. Of those that a mesh axis runs over, the one named last changes fastest.
Arguments:
- tokens: bfloat16 [8192, 1024], P(('groups', 'src', 'tgt')), parts along dimension 0, may hold values from -6 to 6
- sentence_ids: int32 [32, 256], P(('groups', 'src', 'tgt')), parts along dimension 0, may hold values from 0 to 31, never falling along the last dimension, each value on 1 to 32 neighbouring positions
- inner_weight: bfloat16 [4096, 1024], P(('src', 'tgt')), may hold values from -0.1875 to 0.1875
- outer_weight: bfloat16 [4096, 1024], P(('src', 'tgt')), may hold values from -0.09375 to 0.09375
- grid_rows: int32 [1024], P(('groups', 'src', 'tgt')), parts along dimension 0, may hold values from 0 to 511, as said below
- candidates: int32 [8, 16], P(('groups', 'src')), parts along dimension 0, may hold values from 0 to 63, as said below
- targets: bfloat16 [32768, 1024], P(('groups', 'tgt')), parts along dimension 0, may hold values from -6 to 6
Outputs:
- matched: bfloat16 [1024, 1024], P(('groups', 'src', 'tgt')), parts along dimension 0
- log_mass: float32 [1024], P(('groups', 'src', 'tgt')), parts along dimension 0
The draws below stay inside these ranges and needn't reach their ends.
There are 2 independent parts, one for each index of `groups`. The reference program is written for one: setup_inputs(seed, part) draws one part's arguments, and reference() takes and returns one part's arrays. A program takes and returns all parts, laid end to end along the dimension named above; an argument that names none is the same for every part. Nothing has to cross between parts.
Inputs may be any that keep to these rules, and one draw needn't show every extreme that they name: `grid_rows`: A permutation of the 512 source rows. The sentences of the device at index d along src+tgt take exactly 8 rows of every aligned run of 128 rows, rows d * 8 to d * 8 + 7 of that run. `candidates`: row b lists 16 distinct target blocks for the source rows b * 128 to b * 128 + 127. Block g lies in grid column g // 16. A row names at most 4 blocks of one column, and exactly 4 blocks of some column.
All inputs are finite; a program needn't handle non-finite values.
Results may differ from the reference program's by a relative error of at most 0.0082.
Values may be sent and summed in bfloat16 or wider, within the bound.
A program may use at most 128 MiB of HBM per device.

```python
import math
import jax
import jax.numpy as jnp
import numpy as np
from jax import lax

D = 1024
FF = 4096
TOK_DEV = 256
SENT_DEV = 32
MAXLEN = 32
TBLK = 256
TB_COL = 16
K = 16
MOST = 4
PDEV = 16
SPB = 8
SBLK = 128
NSB = 4
NS = 512
TOKENS = 4096
NTB = 64
NT = 16384
N_SRC = 4
N_TGT = 4


def draw_grid_rows(key, part):
    subkeys = jax.random.split(key, PDEV)
    orders = jax.vmap(lambda subkey: jax.random.permutation(subkey, SENT_DEV))(subkeys).astype(jnp.int32)
    ranks = jnp.argsort(orders, axis=1, stable=True).astype(jnp.int32)
    device = jnp.arange(PDEV, dtype=jnp.int32)[:, None]
    rows = ranks // SPB * SBLK + device * SPB + ranks % SPB
    return rows.reshape(-1).astype(jnp.int32)


def draw_candidates(key, part):
    heavy_key, order_key, local_key, final_key = jax.random.split(jax.random.fold_in(key, 7), 4)
    heavy = jax.random.randint(heavy_key, (N_SRC,), 0, N_TGT)
    tickets = N_TGT * MOST
    orders = jax.vmap(lambda subkey: jax.random.permutation(subkey, tickets))(jax.random.split(order_key, N_SRC)).astype(jnp.int32)
    columns = orders // MOST
    light = (columns != heavy[:, None]).astype(jnp.int32)
    arrange = jnp.argsort(light, axis=1, stable=True)
    chosen = jnp.take_along_axis(columns, arrange, axis=1)[:, :K]
    same = chosen[:, :, None] == chosen[:, None, :]
    lower = jnp.arange(K)[None, :] < jnp.arange(K)[:, None]
    ranks = jnp.sum((same & lower[None, :, :]).astype(jnp.int32), axis=2)
    local_orders = jax.vmap(lambda subkey: jax.random.permutation(subkey, TB_COL))(jax.random.split(local_key, N_SRC * N_TGT)).astype(jnp.int32)
    local_orders = local_orders.reshape(N_SRC, N_TGT, TB_COL)
    source_index = jnp.arange(N_SRC, dtype=jnp.int32)[:, None]
    local = local_orders[source_index, chosen, ranks]
    blocks = chosen * TB_COL + local
    shuffle = jax.vmap(lambda subkey: jax.random.permutation(subkey, K))(jax.random.split(final_key, N_SRC)).astype(jnp.int32)
    return jnp.take_along_axis(blocks, shuffle, axis=1).astype(jnp.int32)


def level_of(stream_key, dims, pieces, smallest, largest):
    loudness = 1.0
    for position, blocks in pieces:
        draws = jax.random.uniform(jax.random.fold_in(jax.random.fold_in(stream_key, 6), position), (blocks,), jnp.float32, smallest / len(pieces), largest / len(pieces))
        loudness = loudness * jnp.repeat(jnp.exp(draws), dims[position] // blocks).reshape((-1,) + (1,) * (len(dims) - 1 - position))
    return loudness


def length_profile(count, total, limit, lean):
    loads = [(1 << 20) // math.isqrt(standing ** lean) + 1 for standing in range(2, count + 1)]
    rest, given = total - limit - (count - 1), [1] * (count - 1)
    while rest > 0:
        free = [i for i in range(count - 1) if given[i] < limit]
        whole, remaining = sum([loads[i] for i in free]), rest
        for i in free:
            extra = min(limit - given[i], max(1, remaining * loads[i] // whole), rest)
            given[i] = given[i] + extra
            rest = rest - extra
    return np.array([limit] + given)


def uneven(own_key, count, total, bound, slope):
    if count == 2:
        one = jax.random.randint(own_key, (), max(1, total - bound), min(bound, total - 1) + 1)
        return jnp.stack([one, total - one])
    tallies = jnp.asarray(length_profile(count, total, bound, slope), jnp.int32)
    twos = (count - 1) // 2
    donor, receiver = tallies[1:1 + 2 * twos:2], tallies[2:2 + 2 * twos:2]
    margin = jnp.minimum(donor - 1, bound - receiver)
    shifted = jax.random.randint(jax.random.fold_in(own_key, 1), (twos,), 0, 1 << 20) % (margin + 1)
    tallies = tallies.at[1:1 + 2 * twos:2].set(donor - shifted).at[2:2 + 2 * twos:2].set(receiver + shifted)
    return tallies[jax.random.permutation(jax.random.fold_in(own_key, 2), count)]


def normal_values(stream_key, shape, deviation, limit, shards=(), kind=jnp.bfloat16):
    result = deviation * jax.random.normal(stream_key, shape, jnp.float32)
    if shards:
        result = result * level_of(stream_key, shape, shards, -0.22, 0.18)
    return jnp.clip(result, -limit, limit).astype(kind)


def setup_inputs(seed: int = 0, part: int = 0) -> dict:
    key_list = jax.random.split(jax.random.key(seed), 8)
    part_keys = jax.random.split(jax.random.fold_in(key_list[7], part), 8)
    tokens = normal_values(part_keys[0], (TOKENS, D), 1.0, 6.0, ((0, 16),))
    sentence_ids = jax.vmap(lambda own: jnp.searchsorted(jnp.cumsum(uneven(own, SENT_DEV, TOK_DEV, MAXLEN, 2)), jnp.arange(TOK_DEV), side="right"))(jax.random.split(part_keys[1], PDEV)).reshape((PDEV, TOK_DEV)).astype(jnp.int32)
    inner_weight = normal_values(key_list[2], (FF, D), D ** -0.5, 0.1875, ((0, 16),))
    outer_weight = normal_values(key_list[3], (FF, D), FF ** -0.5, 0.09375, ((0, 16),))
    grid_rows = draw_grid_rows(jax.random.fold_in(jax.random.fold_in(key_list[7], part), 71), part)
    candidates = draw_candidates(jax.random.fold_in(jax.random.fold_in(key_list[7], part), 71), part)
    targets = normal_values(part_keys[6], (NT, D), 1.0, 6.0, ((0, 4),))
    return dict(tokens=tokens, sentence_ids=sentence_ids, inner_weight=inner_weight, outer_weight=outer_weight, grid_rows=grid_rows, candidates=candidates, targets=targets)


SCORE_SCALE = 32.0

def unit_rows(values):
    floats = values.astype(jnp.float32)
    square = lax.optimization_barrier(jnp.mean(floats * floats, axis=-1, keepdims=True))
    return (floats * lax.rsqrt(square + 1e-06) * (1.0 / math.sqrt(values.shape[-1]))).astype(jnp.bfloat16)

def inner_units(rows, inner):
    product = lax.dot_general(rows, inner, (((1,), (1,)), ((), ())), preferred_element_type=jnp.float32)
    return jax.nn.gelu(product, approximate=False).astype(jnp.bfloat16)

def layer_norm(summed):
    center = lax.optimization_barrier(jnp.mean(summed, axis=-1, keepdims=True))
    spread = lax.optimization_barrier(jnp.mean((summed - center) * (summed - center), axis=-1, keepdims=True))
    return (summed - center) * lax.rsqrt(spread + 1e-05)

def pool_units(normed, identity):
    members = (identity[None, :] == jnp.arange(SENT_DEV, dtype=jnp.int32)[:, None]).astype(jnp.float32)
    sums = jnp.dot(members, normed, precision=lax.Precision.HIGHEST)
    pooled = sums / lax.optimization_barrier(jnp.sum(members, axis=1, keepdims=True))
    return unit_rows(pooled)

def reference(tokens, sentence_ids, inner_weight, outer_weight, grid_rows, candidates, targets):

    def encode(pair):
        rows, identity = pair
        projected = jnp.dot(inner_units(rows, inner_weight), outer_weight, preferred_element_type=jnp.float32)
        normed = layer_norm(rows.astype(jnp.float32) + projected)
        return pool_units(normed, identity)
    units = lax.map(encode, (tokens.reshape(PDEV, TOK_DEV, D), sentence_ids)).reshape(NS, D)
    sources = jnp.zeros((NS, D), jnp.bfloat16).at[grid_rows].set(units)
    blocks = targets.reshape(NTB, TBLK, D)

    def listed(index):
        block = lax.dynamic_slice_in_dim(sources, index * SBLK, SBLK)
        target_units = unit_rows(blocks[candidates[index]]).reshape(K * TBLK, D)
        scores = lax.dot_general(block, target_units, (((1,), (1,)), ((), ())), preferred_element_type=jnp.float32)
        return (target_units, jnp.exp(SCORE_SCALE * scores))

    def first_pass(index):
        target_units, expo = listed(index)
        return (lax.optimization_barrier(jnp.sum(expo, axis=1)), lax.optimization_barrier(jnp.sum(expo, axis=0)).reshape(K, TBLK))
    indices = jnp.arange(NSB, dtype=jnp.int32)
    row_total, column_parts = lax.map(first_pass, indices)
    column_total = jnp.zeros((NTB, TBLK), jnp.float32).at[candidates.reshape(-1)].add(column_parts.reshape(NSB * K, TBLK))

    def second_pass(index):
        target_units, expo = listed(index)
        divisor = column_total[candidates[index]].reshape(-1)
        mutual = expo * (expo / divisor[None, :])
        numer = jnp.dot(mutual.astype(jnp.bfloat16), target_units, preferred_element_type=jnp.float32)
        mass = lax.optimization_barrier(jnp.sum(mutual, axis=1))
        square = lax.optimization_barrier(jnp.mean(numer * numer, axis=-1, keepdims=True))
        matched = (numer * lax.rsqrt(square + 1e-06)).astype(jnp.bfloat16)
        return (matched, jnp.log(mass / row_total[index]))
    matched, log_mass = lax.map(second_pass, indices)
    return (matched.reshape(NS, D), log_mass.reshape(NS))
```

```python
import math

import jax
import jax.numpy as jnp
from jax import lax
from jax.experimental import pallas as pl
from jax.experimental.pallas import tpu as pltpu
from jax.sharding import PartitionSpec as P

SENT_DEV = 32
TBLK = 256
MOST = 4


SCORE_SCALE = 32.0


def unit_rows(values):
    floats = values.astype(jnp.float32)
    square = jnp.mean(floats * floats, axis=-1, keepdims=True)
    return (floats * lax.rsqrt(square + 1e-06) * (1.0 / math.sqrt(values.shape[-1]))).astype(
        jnp.bfloat16
    )


def inner_units(rows, inner):
    product = lax.dot_general(
        rows, inner, (((1,), (1,)), ((), ())), preferred_element_type=jnp.float32
    )
    return jax.nn.gelu(product, approximate=False).astype(jnp.bfloat16)


def layer_norm(summed):
    center = jnp.mean(summed, axis=-1, keepdims=True)
    spread = jnp.mean((summed - center) * (summed - center), axis=-1, keepdims=True)
    return (summed - center) * lax.rsqrt(spread + 1e-05)


def on_device(tokens, sentence_ids, inner_weight, outer_weight, grid_rows, candidates, targets):
    features = tokens.shape[1]
    projected = jnp.dot(
        inner_units(tokens, lax.all_gather(inner_weight, ("src", "tgt"), axis=0, tiled=True)),
        lax.all_gather(outer_weight, ("src", "tgt"), axis=0, tiled=True),
        preferred_element_type=jnp.float32,
    )
    normed = layer_norm(tokens.astype(jnp.float32) + projected)
    members = (sentence_ids[0][None, :] == jnp.arange(SENT_DEV, dtype=jnp.int32)[:, None]).astype(
        jnp.float32
    )
    sums = jnp.dot(members, normed, precision=lax.Precision.HIGHEST)
    unit = unit_rows(sums / jnp.sum(members, axis=1, keepdims=True))
    src_count = lax.axis_size("src")
    tgt_count = lax.axis_size("tgt")
    per_block = SENT_DEV // src_count
    block_rows = tgt_count * SENT_DEV
    order_key = grid_rows // block_rows * per_block + grid_rows % per_block
    reorder = (order_key[None, :] == jnp.arange(SENT_DEV, dtype=jnp.int32)[:, None]).astype(
        jnp.bfloat16
    )
    sorted_units = jnp.dot(reorder, unit, preferred_element_type=jnp.float32).astype(jnp.bfloat16)
    relayed = lax.all_to_all(
        sorted_units.reshape(src_count, per_block, features),
        "src",
        split_axis=0,
        concat_axis=0,
        tiled=True,
    )
    block = lax.all_gather(relayed, "tgt", axis=1, tiled=True).reshape(block_rows, features)
    column_index = lax.axis_index("tgt")
    column_blocks = targets.shape[0] // TBLK
    cand_row = candidates[0]
    listed = (cand_row // column_blocks == column_index).astype(jnp.int32)
    places = jnp.arange(cand_row.shape[0], dtype=jnp.int32)
    ranks = jnp.sum(listed[None, :] * (places[None, :] <= places[:, None]), axis=1) - 1
    chosen = (
        (listed[None, :] == 1) & (ranks[None, :] == jnp.arange(MOST, dtype=jnp.int32)[:, None])
    ).astype(jnp.int32)
    slot_block = jnp.sum(chosen * (cand_row % column_blocks)[None, :], axis=1)
    valid = jnp.sum(chosen, axis=1).astype(jnp.float32)
    tiles = jnp.stack(
        [lax.dynamic_slice_in_dim(targets, slot_block[m] * TBLK, TBLK) for m in range(MOST)]
    )
    target_units = unit_rows(tiles).reshape(MOST * TBLK, features)
    scores = lax.dot_general(
        block, target_units, (((1,), (1,)), ((), ())), preferred_element_type=jnp.float32
    )
    column_valid = jnp.repeat(valid, TBLK)
    expo = jnp.exp(SCORE_SCALE * scores) * column_valid[None, :]
    row_part = jnp.sum(expo, axis=1)
    column_part = jnp.sum(expo, axis=0).reshape(MOST, TBLK)
    picker = (slot_block[:, None] == jnp.arange(column_blocks, dtype=jnp.int32)[None, :]).astype(
        jnp.float32
    )
    column_local = jnp.dot(
        (picker * valid[:, None]).T, column_part, precision=lax.Precision.HIGHEST
    )
    column_total = lax.psum(column_local, "src")
    picked = jnp.dot(picker, column_total, precision=lax.Precision.HIGHEST)
    divisor = jnp.where(valid[:, None] > 0, picked, 1.0).reshape(-1)
    mutual = expo * (expo / divisor[None, :])
    numer = jnp.dot(mutual.astype(jnp.bfloat16), target_units, preferred_element_type=jnp.float32)
    mass_part = jnp.sum(mutual, axis=1)
    row_total = lax.psum(row_part, "tgt")
    numer_rows, mass_rows = (
        lax.psum_scatter(numer, "tgt", scatter_dimension=0, tiled=True),
        lax.psum_scatter(mass_part, "tgt", scatter_dimension=0, tiled=True),
    )
    total_rows = lax.dynamic_slice_in_dim(row_total, column_index * SENT_DEV, SENT_DEV)
    square = jnp.mean(numer_rows * numer_rows, axis=-1, keepdims=True)
    matched = (numer_rows * lax.rsqrt(square + 1e-06)).astype(jnp.bfloat16)
    log_mass = jnp.log(mass_rows / total_rows)
    return (matched, log_mass)


NP = 4
HALF = 0.7071067811865476


def remote(source, target, send, recv, /, **device):
    return pltpu.make_async_remote_copy(
        src_ref=source,
        dst_ref=target,
        send_sem=send,
        recv_sem=recv,
        device_id=device,
        device_id_type=pl.DeviceIdType.MESH,
    )


def fused_kernel(
    tok_any, sid_any, win_any, wout_any, grid_any, cand_any, tgt_any,
    matched_ref, log_ref,
    sid_ref, grid_ref, cand_ref, tok, w, acc, tgt, tu, part_send, part_recv, su, blk, num_send, num_recv,
    stat_send, stat_recv, col_send, col_recv,
    local_sem, own_send, fwd_send, y_send, z_recv, y_recv, tok_send, tok_recv,
    part_ssem, part_rsem, unit_ssem, unit_rsem, col_ssem, col_rsem, num_ssem, num_rsem,
):
    g = lax.axis_index("groups")
    s = lax.axis_index("src")
    z = lax.axis_index("tgt")
    f32, bf16 = jnp.float32, jnp.bfloat16
    features = tok.shape[2]
    mate = s + 1 - 2 * lax.rem(s, 2)
    peer = lax.rem(s + 2, 4)

    locals_ = [
        pltpu.make_async_copy(tok_any, tok.at[0], local_sem.at[0]),
        pltpu.make_async_copy(win_any, w.at[0, z], local_sem.at[1]),
        pltpu.make_async_copy(wout_any, w.at[1, z], local_sem.at[2]),
        pltpu.make_async_copy(tgt_any, tgt, local_sem.at[3]),
        pltpu.make_async_copy(sid_any, sid_ref, local_sem.at[4]),
        pltpu.make_async_copy(grid_any, grid_ref, local_sem.at[5]),
        pltpu.make_async_copy(cand_any, cand_ref, local_sem.at[6]),
    ]
    for copy in locals_[:3]:
        copy.start()

    barrier = pltpu.get_barrier_semaphore()
    others = [(a, b) for a in range(4) for b in range(4) if a or b]

    def greet(**device):
        pl.semaphore_signal(
            barrier, inc=1, device_id=device, device_id_type=pl.DeviceIdType.MESH
        )

    pl.when(z > 0)(lambda: greet(tgt=z - 1))
    pl.when(z < 3)(lambda: greet(tgt=z + 1))
    greet(groups=1 - g)
    greet(src=mate)
    greet(src=peer)
    pl.semaphore_wait(barrier, 3 + (z > 0).astype(jnp.int32) + (z < 3).astype(jnp.int32))

    def piece(origin, p, half):
        row = pl.multiple_of(half * 128 + (p // 2) * 64, 64)
        return w.at[lax.rem(p, 2), origin, pl.ds(row, 64)]

    def own_copy(direction, p):
        row = pl.multiple_of(g * 128 + (p // 2) * 64, 64)
        return remote(
            (win_any, wout_any)[p % 2].at[pl.ds(row, 64)], piece(z, p, g),
            own_send.at[direction, p], z_recv.at[z, p],
            tgt=z + 1 if direction == 0 else z - 1,
        )

    for p in range(NP):
        pl.when(z < 3)(own_copy(0, p).start)
        pl.when(z > 0)(own_copy(1, p).start)

    to_mate = remote(tok_any, tok.at[1], tok_send.at[0], tok_recv.at[1], src=mate)
    to_peer = remote(tok_any, tok.at[2], tok_send.at[1], tok_recv.at[2], src=peer)
    to_diag = remote(tok.at[2], tok.at[3], tok_send.at[2], tok_recv.at[3], src=mate)
    to_mate.start()
    to_peer.start()

    first = 1 + lax.rem(z, 2)
    third = jnp.where(z < 2, 3, 0)
    second = 6 - z - first - third

    def origin_of(j):
        return jnp.where(j == 0, z, jnp.where(j == 1, first, jnp.where(j == 2, second, third)))

    def z_copy(j, p):
        origin = origin_of(j)
        ref = piece(origin, p, g)
        from_left = origin < z
        following = jnp.where(from_left, z + 1, z - 1)
        valid = jnp.where(from_left, (z < 3).astype(jnp.int32), (z > 0).astype(jnp.int32)) == 1
        return (
            remote(ref, ref, fwd_send.at[j - 1, p], z_recv.at[origin, p], tgt=following),
            valid,
        )

    def y_copy(j, p):
        origin = origin_of(j)
        ref = piece(origin, p, g)
        return remote(ref, ref, y_send.at[j - 1, p], y_recv.at[origin, p], groups=1 - g)

    def y_wait(j):
        origin = origin_of(j)
        for p in range(NP):
            ref = piece(origin, p, 1 - g)
            remote(ref, ref, y_send.at[0, p], y_recv.at[origin, p], groups=1 - g).wait_recv()

    for copy in locals_[3:]:
        copy.start()
    for copy in locals_[:3] + locals_[4:]:
        copy.wait()

    def compute(j, r):
        origin = origin_of(j)
        product = lax.dot_general(
            tok[r], w[0, origin], (((1,), (1,)), ((), ())), preferred_element_type=f32
        )
        hidden = (0.5 * product * (1.0 + lax.erf(product * HALF))).astype(bf16)
        term = jnp.dot(hidden, w[1, origin], preferred_element_type=f32)

        @pl.when(j == 0)
        def _():
            acc[r] = term

        @pl.when(j > 0)
        def _():
            acc[r] += term

    count = jnp.int32(0)
    slots = [jnp.int32(0)] * MOST
    valids = [jnp.int32(0)] * MOST
    column_blocks = tgt.shape[0] // TBLK
    for k in range(cand_ref.shape[1]):
        c = cand_ref[0, k]
        hit = (c // column_blocks == z).astype(jnp.int32)
        for m in range(MOST):
            take = hit * (count == m).astype(jnp.int32) == 1
            slots[m] = jnp.where(take, lax.rem(c, column_blocks), slots[m])
            valids[m] = jnp.where(take, 1, valids[m])
        count = count + hit

    def target_unit(p):
        def some(i, carry):
            row = pl.multiple_of(p * 64 + i * 16, 16)
            tiles = [jnp.zeros((16, features), bf16)] * MOST
            for b in range(column_blocks):
                values = tgt[pl.ds(b * TBLK + row, 16), :]
                for m in range(MOST):
                    keep = jnp.full((16, features), (slots[m] == b).astype(f32), f32)
                    tiles[m] = tiles[m] + values * keep.astype(bf16)
            for m in range(MOST):
                tu[pl.ds(m * TBLK + row, 16), :] = unit_rows(tiles[m])
            return carry

        lax.fori_loop(0, 4, some, 0)

    def step(i, carry):
        j = i // NP
        p = lax.rem(i, NP)
        ref = piece(origin_of(j + 1), p, g)
        remote(
            ref, ref, own_send.at[0, p], z_recv.at[origin_of(j + 1), p], groups=1 - g
        ).wait_recv()
        forward, valid = z_copy(j + 1, p)
        pl.when(valid)(forward.start)
        y_copy(j + 1, p).start()

        @pl.when((j == 0) & (p == 1))
        def _():
            to_mate.wait_recv()

        @pl.when((j == 0) & (p == 2))
        def _():
            to_peer.wait_recv()
            to_diag.start()

        @pl.when((j == 0) & (p == 3))
        def _():
            to_diag.wait_recv()

        @pl.when((j == 2) & (p == 0))
        def _():
            y_wait(1)

        @pl.when(j != 1)
        def _():
            compute(j // 2, p)

        @pl.when(i == NP)
        def _():
            locals_[3].wait()

        @pl.when(j == 1)
        def _():
            target_unit(p)

        return carry

    lax.fori_loop(0, 3 * NP, step, 0)

    y_wait(2)

    def behind(p, carry):
        compute(2, p)
        return carry

    lax.fori_loop(0, 4, behind, 0)
    y_wait(3)

    to_a = remote(part_send.at[0], part_recv.at[0], part_ssem.at[0], part_rsem.at[0], src=mate)
    to_c = remote(part_send.at[1], part_recv.at[1], part_ssem.at[1], part_rsem.at[1], src=mate)

    def to_b(q):
        rows = pl.ds(q * 64, 64)
        return remote(
            part_send.at[2, rows], part_recv.at[2, rows],
            part_ssem.at[2 + q], part_rsem.at[2 + q], src=peer,
        )

    def last(i, carry):
        r = 3 - i
        compute(3, r)

        @pl.when(i == 0)
        def _():
            part_send[0] = acc[3].astype(bf16)
            to_a.start()

        @pl.when(i == 1)
        def _():
            to_a.wait_recv()
            for q in range(4):
                rows = pl.ds(q * 64, 64)
                part_send[2, rows] = (acc[2, rows] + part_recv[0, rows].astype(f32)).astype(bf16)
                to_b(q).start()

        @pl.when(i == 2)
        def _():
            part_send[1] = acc[1].astype(bf16)
            to_c.start()

        return carry

    lax.fori_loop(0, 4, last, 0)

    to_c.wait_recv()
    sums = jnp.zeros((SENT_DEV, features), f32)
    counts = jnp.zeros((SENT_DEV, 1), f32)
    for q in range(4):
        rows = pl.ds(q * 64, 64)
        to_b(q).wait_recv()
        summed = tok[0, rows].astype(f32) + (
            acc[0, rows] + part_recv[1, rows].astype(f32) + part_recv[2, rows].astype(f32)
        )
        normed = layer_norm(summed)
        high = normed.astype(bf16)
        low = (normed - high.astype(f32)).astype(bf16)
        ids = sid_ref[:, q * 64:(q + 1) * 64]
        members = (ids == lax.broadcasted_iota(jnp.int32, (SENT_DEV, 64), 0)).astype(f32)
        counts = counts + jnp.sum(members, axis=1, keepdims=True)
        members = members.astype(bf16)
        sums = sums + (
            jnp.dot(members, high, preferred_element_type=f32)
            + jnp.dot(members, low, preferred_element_type=f32)
        )
    unit = unit_rows(sums / counts)
    grid = grid_ref[...]
    order_key = grid // 128 * 8 + lax.rem(grid, 8)
    reorder = (order_key == lax.broadcasted_iota(jnp.int32, (SENT_DEV, SENT_DEV), 0)).astype(f32)
    ordered = jnp.dot(reorder.astype(bf16), unit, preferred_element_type=f32)
    for b in range(4):
        su[b] = ordered[b * 8:(b + 1) * 8].astype(bf16)

    me = s * 4 + z

    def unit_copy(n):
        a, b = others[n]
        return remote(
            su.at[lax.rem(s + a, 4)], blk.at[me], unit_ssem.at[n], unit_rsem.at[n],
            src=lax.rem(s + a, 4), tgt=lax.rem(z + b, 4),
        )

    for n in range(len(others)):
        unit_copy(n).start()
    blk[me] = su[s]
    for n in range(len(others)):
        a, b = others[n]
        origin = lax.rem(s + 4 - a, 4) * 4 + lax.rem(z + 4 - b, 4)
        remote(
            su.at[0], blk.at[origin], unit_ssem.at[n], unit_rsem.at[n],
            src=lax.rem(s + a, 4), tgt=lax.rem(z + b, 4),
        ).wait_recv()

    block = jnp.concatenate([blk[d].astype(f32) for d in range(16)], axis=0).astype(bf16)
    row_ids = lax.broadcasted_iota(jnp.int32, (column_blocks, TBLK), 0)
    expos = []
    row_part = jnp.zeros((128, 1), f32)
    dense = jnp.zeros((column_blocks, TBLK), f32)
    for m in range(MOST):
        scores = lax.dot_general(
            block, tu[m * TBLK:(m + 1) * TBLK, :], (((1,), (1,)), ((), ())),
            preferred_element_type=f32,
        )
        expo = jnp.exp(SCORE_SCALE * scores) * valids[m].astype(f32)
        expos.append(expo)
        row_part = row_part + jnp.sum(expo, axis=1, keepdims=True)
        dense = dense + jnp.where(row_ids == slots[m], jnp.sum(expo, axis=0, keepdims=True), 0.0)
    col_send[...] = dense

    def col_copy(a):
        return remote(
            col_send, col_recv.at[a - 1], col_ssem.at[a - 1], col_rsem.at[a - 1],
            src=lax.rem(s + a, 4),
        )

    for a in range(1, 4):
        col_copy(a).start()
    for a in range(1, 4):
        col_copy(a).wait_recv()
    total = dense + col_recv[0] + col_recv[1] + col_recv[2]
    numer = jnp.zeros((128, features), f32)
    mass = jnp.zeros((128, 1), f32)
    for m in range(MOST):
        picked = jnp.sum(jnp.where(row_ids == slots[m], total, 0.0), axis=0, keepdims=True)
        divisor = jnp.where(valids[m] > 0, picked, 1.0)
        mutual = expos[m] * (expos[m] / divisor)
        mass = mass + jnp.sum(mutual, axis=1, keepdims=True)
        numer = numer + jnp.dot(
            mutual.astype(bf16), tu[m * TBLK:(m + 1) * TBLK, :], preferred_element_type=f32
        )
    lanes = lax.broadcasted_iota(jnp.int32, (128, 128), 1)
    stats = jnp.where(lanes == 0, mass, jnp.where(lanes == 1, row_part, 0.0))
    for t in range(4):
        num_send[t] = numer[t * 32:(t + 1) * 32].astype(bf16)
        stat_send[t] = stats[t * 32:(t + 1) * 32]

    def num_copies(b):
        to = lax.rem(z + b, 4)
        return (
            remote(
                num_send.at[to], num_recv.at[b - 1], num_ssem.at[0, b - 1], num_rsem.at[0, b - 1],
                tgt=to,
            ),
            remote(
                stat_send.at[to], stat_recv.at[b - 1], num_ssem.at[1, b - 1],
                num_rsem.at[1, b - 1], tgt=to,
            ),
        )

    for b in range(1, 4):
        for copy in num_copies(b):
            copy.start()
    for b in range(1, 4):
        for copy in num_copies(b):
            copy.wait_recv()
    rows = num_send[z].astype(f32)
    stat = stat_send[z]
    for b in range(3):
        rows = rows + num_recv[b].astype(f32)
        stat = stat + stat_recv[b]
    square = jnp.mean(rows * rows, axis=-1, keepdims=True)
    matched_ref[...] = (rows * lax.rsqrt(square + 1e-06)).astype(bf16)
    logs = jnp.log(stat[:, 0:1] / stat[:, 1:2])
    eye = lax.broadcasted_iota(jnp.int32, (32, 32), 0) == lax.broadcasted_iota(
        jnp.int32, (32, 32), 1
    )
    log_ref[...] = jnp.sum(jnp.where(eye, logs, 0.0), axis=0, keepdims=True)

    for p in range(NP):
        pl.when(z < 3)(own_copy(0, p).wait_send)
        pl.when(z > 0)(own_copy(1, p).wait_send)
    to_mate.wait_send()
    to_peer.wait_send()
    to_diag.wait_send()

    def drain(i, carry):
        j = i // NP + 1
        p = lax.rem(i, NP)
        forward, valid = z_copy(j, p)
        pl.when(valid)(forward.wait_send)
        y_copy(j, p).wait_send()
        return carry

    lax.fori_loop(0, 3 * NP, drain, 0)
    to_a.wait_send()
    to_c.wait_send()
    for q in range(4):
        to_b(q).wait_send()
    for n in range(len(others)):
        unit_copy(n).wait_send()
    for a in range(1, 4):
        col_copy(a).wait_send()
    for b in range(1, 4):
        for copy in num_copies(b):
            copy.wait_send()


def fused(tokens, sentence_ids, inner_weight, outer_weight, grid_rows, candidates, targets):
    f32, bf16 = jnp.float32, jnp.bfloat16
    features = tokens.shape[1]
    dma = pltpu.SemaphoreType.DMA
    any_spec = pl.BlockSpec(memory_space=pltpu.HBM)
    vmem = pl.BlockSpec(memory_space=pltpu.VMEM)
    matched, logs = pl.pallas_call(
        fused_kernel,
        out_shape=(
            jax.ShapeDtypeStruct((SENT_DEV, features), bf16),
            jax.ShapeDtypeStruct((1, SENT_DEV), f32),
        ),
        in_specs=[
            any_spec,
        ] * 7,
        out_specs=(vmem, vmem),
        scratch_shapes=[
            pltpu.VMEM((1, 256), jnp.int32),
            pltpu.VMEM((1, SENT_DEV), jnp.int32),
            pltpu.SMEM(candidates.shape, jnp.int32),
            pltpu.VMEM((4, 256, features), bf16),
            pltpu.VMEM((2, 4, 256, features), bf16),
            pltpu.VMEM((4, 256, features), f32),
            pltpu.VMEM(targets.shape, bf16),
            pltpu.VMEM((MOST * TBLK, features), bf16),
            pltpu.VMEM((3, 256, features), bf16),
            pltpu.VMEM((3, 256, features), bf16),
            pltpu.VMEM((4, 8, features), bf16),
            pltpu.VMEM((16, 8, features), bf16),
            pltpu.VMEM((4, 32, features), bf16),
            pltpu.VMEM((3, 32, features), bf16),
            pltpu.VMEM((4, 32, 128), f32),
            pltpu.VMEM((3, 32, 128), f32),
            pltpu.VMEM((targets.shape[0] // TBLK, TBLK), f32),
            pltpu.VMEM((3, targets.shape[0] // TBLK, TBLK), f32),
            dma((7,)),
            dma((2, NP)),
            dma((3, NP)),
            dma((3, NP)),
            dma((4, NP)),
            dma((4, NP)),
            dma((3,)),
            dma((4,)),
            dma((6,)),
            dma((6,)),
            dma((15,)),
            dma((15,)),
            dma((3,)),
            dma((3,)),
            dma((2, 3)),
            dma((2, 3)),
        ],
        compiler_params=pltpu.CompilerParams(
            collective_id=0, has_side_effects=True, vmem_limit_bytes=64 * 1024 * 1024 - 65536
        ),
    )(
        tokens, sentence_ids, inner_weight, outer_weight,
        grid_rows.reshape(1, SENT_DEV), candidates, targets,
    )
    return matched, logs.reshape(SENT_DEV)


def solution(mesh):
    in_specs = (
        P(("groups", "src", "tgt"), None),
        P(("groups", "src", "tgt"), None),
        P(("src", "tgt"), None),
        P(("src", "tgt"), None),
        P(("groups", "src", "tgt")),
        P(("groups", "src"), None),
        P(("groups", "tgt"), None),
    )
    out_specs = (P(("groups", "src", "tgt"), None), P(("groups", "src", "tgt")))
    sizes = tuple(mesh.shape[name] for name in ("groups", "src", "tgt"))
    body = fused if sizes == (2, 4, 4) else on_device
    return jax.shard_map(
        body, mesh=mesh, in_specs=in_specs, out_specs=out_specs, check_vma=False
    )
```

```python
import math

import jax
import jax.numpy as jnp
from jax import lax
from jax.experimental import pallas as pl
from jax.experimental.pallas import tpu as pltpu
from jax.sharding import PartitionSpec as P

SENT_DEV = 32
TBLK = 256
MOST = 4


SCORE_SCALE = 32.0


def unit_rows(values):
    floats = values.astype(jnp.float32)
    square = jnp.mean(floats * floats, axis=-1, keepdims=True)
    return (floats * lax.rsqrt(square + 1e-06) * (1.0 / math.sqrt(values.shape[-1]))).astype(
        jnp.bfloat16
    )


def inner_units(rows, inner):
    product = lax.dot_general(
        rows, inner, (((1,), (1,)), ((), ())), preferred_element_type=jnp.float32
    )
    return jax.nn.gelu(product, approximate=False).astype(jnp.bfloat16)


def layer_norm(summed):
    center = jnp.mean(summed, axis=-1, keepdims=True)
    spread = jnp.mean((summed - center) * (summed - center), axis=-1, keepdims=True)
    return (summed - center) * lax.rsqrt(spread + 1e-05)


def on_device(tokens, sentence_ids, inner_weight, outer_weight, grid_rows, candidates, targets):
    features = tokens.shape[1]
    projected = jnp.dot(
        inner_units(tokens, lax.all_gather(inner_weight, ("src", "tgt"), axis=0, tiled=True)),
        lax.all_gather(outer_weight, ("src", "tgt"), axis=0, tiled=True),
        preferred_element_type=jnp.float32,
    )
    normed = layer_norm(tokens.astype(jnp.float32) + projected)
    members = (sentence_ids[0][None, :] == jnp.arange(SENT_DEV, dtype=jnp.int32)[:, None]).astype(
        jnp.float32
    )
    sums = jnp.dot(members, normed, precision=lax.Precision.HIGHEST)
    unit = unit_rows(sums / jnp.sum(members, axis=1, keepdims=True))
    src_count = lax.axis_size("src")
    tgt_count = lax.axis_size("tgt")
    per_block = SENT_DEV // src_count
    block_rows = tgt_count * SENT_DEV
    order_key = grid_rows // block_rows * per_block + grid_rows % per_block
    reorder = (order_key[None, :] == jnp.arange(SENT_DEV, dtype=jnp.int32)[:, None]).astype(
        jnp.bfloat16
    )
    sorted_units = jnp.dot(reorder, unit, preferred_element_type=jnp.float32).astype(jnp.bfloat16)
    relayed = lax.all_to_all(
        sorted_units.reshape(src_count, per_block, features),
        "src",
        split_axis=0,
        concat_axis=0,
        tiled=True,
    )
    block = lax.all_gather(relayed, "tgt", axis=1, tiled=True).reshape(block_rows, features)
    column_index = lax.axis_index("tgt")
    column_blocks = targets.shape[0] // TBLK
    cand_row = candidates[0]
    listed = (cand_row // column_blocks == column_index).astype(jnp.int32)
    places = jnp.arange(cand_row.shape[0], dtype=jnp.int32)
    ranks = jnp.sum(listed[None, :] * (places[None, :] <= places[:, None]), axis=1) - 1
    chosen = (
        (listed[None, :] == 1) & (ranks[None, :] == jnp.arange(MOST, dtype=jnp.int32)[:, None])
    ).astype(jnp.int32)
    slot_block = jnp.sum(chosen * (cand_row % column_blocks)[None, :], axis=1)
    valid = jnp.sum(chosen, axis=1).astype(jnp.float32)
    tiles = jnp.stack(
        [lax.dynamic_slice_in_dim(targets, slot_block[m] * TBLK, TBLK) for m in range(MOST)]
    )
    target_units = unit_rows(tiles).reshape(MOST * TBLK, features)
    scores = lax.dot_general(
        block, target_units, (((1,), (1,)), ((), ())), preferred_element_type=jnp.float32
    )
    column_valid = jnp.repeat(valid, TBLK)
    expo = jnp.exp(SCORE_SCALE * scores) * column_valid[None, :]
    row_part = jnp.sum(expo, axis=1)
    column_part = jnp.sum(expo, axis=0).reshape(MOST, TBLK)
    picker = (slot_block[:, None] == jnp.arange(column_blocks, dtype=jnp.int32)[None, :]).astype(
        jnp.float32
    )
    column_local = jnp.dot(
        (picker * valid[:, None]).T, column_part, precision=lax.Precision.HIGHEST
    )
    column_total = lax.psum(column_local, "src")
    picked = jnp.dot(picker, column_total, precision=lax.Precision.HIGHEST)
    divisor = jnp.where(valid[:, None] > 0, picked, 1.0).reshape(-1)
    mutual = expo * (expo / divisor[None, :])
    numer = jnp.dot(mutual.astype(jnp.bfloat16), target_units, preferred_element_type=jnp.float32)
    mass_part = jnp.sum(mutual, axis=1)
    row_total = lax.psum(row_part, "tgt")
    numer_rows, mass_rows = (
        lax.psum_scatter(numer, "tgt", scatter_dimension=0, tiled=True),
        lax.psum_scatter(mass_part, "tgt", scatter_dimension=0, tiled=True),
    )
    total_rows = lax.dynamic_slice_in_dim(row_total, column_index * SENT_DEV, SENT_DEV)
    square = jnp.mean(numer_rows * numer_rows, axis=-1, keepdims=True)
    matched = (numer_rows * lax.rsqrt(square + 1e-06)).astype(jnp.bfloat16)
    log_mass = jnp.log(mass_rows / total_rows)
    return (matched, log_mass)


PIECES = ((0, 0), (0, 64), (1, 0), (1, 64))
PROWS = 64
NP = len(PIECES)
HALF = 0.7071067811865476


def remote(source, target, send, recv, /, **device):
    return pltpu.make_async_remote_copy(
        src_ref=source,
        dst_ref=target,
        send_sem=send,
        recv_sem=recv,
        device_id=device,
        device_id_type=pl.DeviceIdType.MESH,
    )


def gelu(product):
    return (0.5 * product * (1.0 + lax.erf(product * HALF))).astype(jnp.bfloat16)


def fused_kernel(
    tok_any, sid_any, win_any, wout_any, grid_any, cand_any, tgt_any,
    matched_ref, log_ref,
    sid_ref, grid_ref, cand_ref, tok, w, acc, hid, tgt, tu, part_send, part_recv, su, blk,
    num_send, num_recv, num_relay, stat_send, stat_recv, col_send, col_recv,
    local_sem, own_send, fwd_send, y_send, z_recv, y_recv, tok_send, tok_recv,
    part_ssem, part_rsem, unit_ssem, unit_rsem, relay_ssem, col_ssem, col_rsem,
    num_ssem, num_rsem, stat_ssem, stat_rsem,
):
    g = lax.axis_index("groups")
    s = lax.axis_index("src")
    z = lax.axis_index("tgt")
    f32, bf16 = jnp.float32, jnp.bfloat16
    features = tok.shape[2]
    mate = s + 1 - 2 * lax.rem(s, 2)
    peer = lax.rem(s + 2, 4)
    mid = (z == 1) | (z == 2)
    end = (z == 0) | (z == 3)

    locals_ = [
        pltpu.make_async_copy(tok_any, tok.at[0], local_sem.at[0]),
        pltpu.make_async_copy(win_any, w.at[0, z], local_sem.at[1]),
        pltpu.make_async_copy(wout_any, w.at[1, z], local_sem.at[2]),
        pltpu.make_async_copy(tgt_any, tgt, local_sem.at[3]),
        pltpu.make_async_copy(sid_any, sid_ref, local_sem.at[4]),
        pltpu.make_async_copy(grid_any, grid_ref, local_sem.at[5]),
        pltpu.make_async_copy(cand_any, cand_ref, local_sem.at[6]),
    ]

    barrier = pltpu.get_barrier_semaphore()

    def greet(**device):
        pl.semaphore_signal(
            barrier, inc=1, device_id=device, device_id_type=pl.DeviceIdType.MESH
        )

    pl.when(z > 0)(lambda: greet(tgt=z - 1))
    pl.when(z < 3)(lambda: greet(tgt=z + 1))
    greet(groups=1 - g)
    greet(src=mate)
    greet(src=peer)
    for copy in locals_[:3]:
        copy.start()
    pl.semaphore_wait(barrier, 4 + mid.astype(jnp.int32))

    def place(u, half):
        if isinstance(u, int):
            matrix, row = PIECES[u]
        else:
            matrix, row = u // 2, lax.rem(u, 2) * PROWS
        return matrix, pl.multiple_of(half * 128 + row, PROWS)

    def piece(origin, u, half):
        matrix, row = place(u, half)
        return w.at[matrix, origin, pl.ds(row, PROWS)]

    def unit_of(origin, u):
        if isinstance(u, int) and u == NP:
            return piece(origin, NP - 1, 1 - g)
        return piece(origin, u, g)

    def own_copy(direction, u):
        half = 1 - g if u == NP else g
        matrix, row = place(min(u, NP - 1), half)
        return remote(
            (win_any, wout_any)[matrix].at[pl.ds(row, PROWS)], unit_of(z, u),
            own_send.at[direction, u], z_recv.at[z, u],
            tgt=z + 1 if direction == 0 else z - 1,
        )

    def own_copies(method):
        for u in range(NP + 1):
            pl.when(z < 3 if u < NP else z == 0)(lambda u=u: method(own_copy(0, u)))
            pl.when(z > 0 if u < NP else z == 3)(lambda u=u: method(own_copy(1, u)))

    own_copies(lambda copy: copy.start())

    to_mate = remote(tok_any, tok.at[1], tok_send.at[0], tok_recv.at[1], src=mate)
    to_peer = remote(tok_any, tok.at[2], tok_send.at[1], tok_recv.at[2], src=peer)
    to_diag = remote(tok.at[2], tok.at[3], tok_send.at[2], tok_recv.at[3], src=mate)
    to_mate.start()
    to_peer.start()
    for copy in locals_[3:]:
        copy.start()

    first = 1 + lax.rem(z, 2)
    third = jnp.where(z < 2, 3, 0)
    second = 6 - z - first - third

    def origin_of(j):
        return jnp.where(j == 0, z, jnp.where(j == 1, first, jnp.where(j == 2, second, third)))

    def z_copy(j, u):
        origin = origin_of(j)
        ref = unit_of(origin, u)
        from_left = origin < z
        following = jnp.where(from_left, z + 1, z - 1)
        valid = jnp.where(from_left, (z < 3).astype(jnp.int32), (z > 0).astype(jnp.int32)) == 1
        return (
            remote(ref, ref, fwd_send.at[j - 1, u], z_recv.at[origin, u], tgt=following),
            valid,
        )

    def y_copy(j, u):
        origin = origin_of(j)
        ref = piece(origin, u, g)
        return remote(ref, ref, y_send.at[j - 1, u], y_recv.at[origin, u], groups=1 - g)

    def has_y(j, u):
        return (u < NP - 1) | (j == 1) | ((j == 2) & end)

    def y_wait(j, us=range(NP)):
        origin = origin_of(j)
        for u in us:
            ref = piece(origin, u, 1 - g)

            def wait(u=u, ref=ref):
                remote(ref, ref, y_send.at[0, u], y_recv.at[origin, u], groups=1 - g).wait_recv()

            if j == 2 and u == NP - 1:
                pl.when(end)(wait)
            elif j < 3 or u < NP - 1:
                wait()

    def take(j, u):
        ref = unit_of(origin_of(j), u)
        remote(
            ref, ref, own_send.at[0, u], z_recv.at[origin_of(j), u], groups=1 - g
        ).wait_recv()
        forward, valid = z_copy(j, u)
        pl.when(valid)(forward.start)

    for copy in locals_[:3] + locals_[4:]:
        copy.wait()

    def hidden_of(j, r):
        product = lax.dot_general(
            tok[r], w[0, origin_of(j)], (((1,), (1,)), ((), ())), preferred_element_type=f32
        )
        return gelu(product)

    def compute(j, r):
        term = jnp.dot(hidden_of(j, r), w[1, origin_of(j)], preferred_element_type=f32)

        @pl.when(j == 0)
        def _():
            acc[r] = term

        @pl.when(j > 0)
        def _():
            acc[r] += term

    count = jnp.int32(0)
    slots = [jnp.int32(0)] * MOST
    valids = [jnp.int32(0)] * MOST
    column_blocks = tgt.shape[0] // TBLK
    for k in range(cand_ref.shape[1]):
        c = cand_ref[0, k]
        hit = (c // column_blocks == z).astype(jnp.int32)
        for m in range(MOST):
            take_it = hit * (count == m).astype(jnp.int32) == 1
            slots[m] = jnp.where(take_it, lax.rem(c, column_blocks), slots[m])
            valids[m] = jnp.where(take_it, 1, valids[m])
        count = count + hit

    def target_unit(p):
        def some(i, carry):
            row = pl.multiple_of(p * 64 + i * 16, 16)
            tiles = [jnp.zeros((16, features), bf16)] * MOST
            for b in range(column_blocks):
                values = tgt[pl.ds(b * TBLK + row, 16), :]
                for m in range(MOST):
                    keep = jnp.full((16, features), (slots[m] == b).astype(f32), f32)
                    tiles[m] = tiles[m] + values * keep.astype(bf16)
            for m in range(MOST):
                tu[pl.ds(m * TBLK + row, 16), :] = unit_rows(tiles[m])
            return carry

        lax.fori_loop(0, 4, some, 0)

    def step(i, carry):
        j = i // NP + 1
        p = lax.rem(i, NP)
        take(j, p)
        pl.when(has_y(j, p))(lambda: y_copy(j, p).start())
        pl.when((p == NP - 1) & (j > 1) & mid)(lambda: take(j, NP))

        @pl.when(i == 1)
        def _():
            to_mate.wait_recv()

        @pl.when(i == 2)
        def _():
            locals_[3].wait()

        @pl.when((i >= 2) & (i < 6))
        def _():
            target_unit(i - 2)

        @pl.when(i == 6)
        def _():
            to_peer.wait_recv()
            to_diag.start()

        @pl.when(i == 7)
        def _():
            to_diag.wait_recv()

        @pl.when(i == 8)
        def _():
            y_wait(1)

        @pl.when(i == 10)
        def _():
            y_wait(2)

        start = jnp.where(i < 2, i, jnp.where(i < 8, i - 4, 2 * i - 12))
        number = jnp.where(i < 2, 1, jnp.where(i < 6, 0, jnp.where(i < 8, 1, 2)))

        def block(k, carry):
            compute((start + k) // 4, lax.rem(start + k, 4))
            return carry

        lax.fori_loop(0, number, block, 0)
        return carry

    lax.fori_loop(0, 3 * NP, step, 0)

    y_wait(3, (0, 1))

    def inner(r, carry):
        hid[r] = hidden_of(3, r)
        return carry

    lax.fori_loop(0, 4, inner, 0)
    pl.when(end)(lambda: take(3, NP))
    y_wait(3, (2,))

    def to_a(h):
        rows = pl.ds(h * 128, 128)
        return remote(
            part_send.at[0, rows], part_recv.at[0, rows], part_ssem.at[h], part_rsem.at[h],
            src=mate,
        )

    to_c = remote(part_send.at[1], part_recv.at[1], part_ssem.at[2], part_rsem.at[2], src=mate)

    def to_b(q):
        rows = pl.ds(q * 64, 64)
        return remote(
            part_send.at[2, rows], part_recv.at[2, rows],
            part_ssem.at[3 + q], part_rsem.at[3 + q], src=peer,
        )

    def last(i, carry):
        r = 3 - i
        acc[r] += jnp.dot(hid[r], w[1, third], preferred_element_type=f32)

        @pl.when(i == 0)
        def _():
            for h in range(2):
                rows = pl.ds(h * 128, 128)
                part_send[0, rows] = acc[3, rows].astype(bf16)
                to_a(h).start()

        @pl.when(i == 1)
        def _():
            for q in range(4):
                if q % 2 == 0:
                    to_a(q // 2).wait_recv()
                rows = pl.ds(q * 64, 64)
                part_send[2, rows] = (acc[2, rows] + part_recv[0, rows].astype(f32)).astype(bf16)
                to_b(q).start()

        @pl.when(i == 2)
        def _():
            part_send[1] = acc[1].astype(bf16)
            to_c.start()

        return carry

    lax.fori_loop(0, 4, last, 0)

    to_c.wait_recv()
    sums = jnp.zeros((SENT_DEV, features), f32)
    counts = jnp.zeros((SENT_DEV, 1), f32)
    for q in range(4):
        rows = pl.ds(q * 64, 64)
        to_b(q).wait_recv()
        summed = tok[0, rows].astype(f32) + (
            acc[0, rows] + part_recv[1, rows].astype(f32) + part_recv[2, rows].astype(f32)
        )
        normed = layer_norm(summed)
        high = normed.astype(bf16)
        low = (normed - high.astype(f32)).astype(bf16)
        ids = sid_ref[:, q * 64:(q + 1) * 64]
        members = (ids == lax.broadcasted_iota(jnp.int32, (SENT_DEV, 64), 0)).astype(f32)
        counts = counts + jnp.sum(members, axis=1, keepdims=True)
        members = members.astype(bf16)
        sums = sums + (
            jnp.dot(members, high, preferred_element_type=f32)
            + jnp.dot(members, low, preferred_element_type=f32)
        )
    unit = unit_rows(sums / counts)
    grid = grid_ref[...]
    order_key = grid // 128 * 8 + lax.rem(grid, 8)
    reorder = (order_key == lax.broadcasted_iota(jnp.int32, (SENT_DEV, SENT_DEV), 0)).astype(f32)
    ordered = jnp.dot(reorder.astype(bf16), unit, preferred_element_type=f32)
    for b in range(4):
        su[b] = ordered[b * 8:(b + 1) * 8].astype(bf16)

    me = s * 4 + z

    def unit_copy(a, to):
        n = a * 4 + lax.rem(to - z + 4, 4)
        return remote(
            su.at[lax.rem(s + a, 4)], blk.at[me], unit_ssem.at[n], unit_rsem.at[n],
            src=lax.rem(s + a, 4), tgt=to,
        )

    across = 3 - z
    near_end = jnp.where(z < 2, 0, 3)
    next_one = jnp.where(mid, near_end, jnp.where(z == 0, 2, 1))
    inward = jnp.where(z == 0, 1, 2)

    def unit_copies(method):
        for a in range(4):
            method(unit_copy(a, across))
        for a in range(4):
            method(unit_copy(a, next_one))
        pl.when(end)(lambda: [method(unit_copy(a, inward)) for a in range(4)] and None)
        for a in range(1, 4):
            method(unit_copy(a, z))

    def unit_wait(a, b):
        origin = lax.rem(s + 4 - a, 4) * 4 + lax.rem(z + 4 - b, 4)
        remote(
            su.at[0], blk.at[origin], unit_ssem.at[a * 4 + b], unit_rsem.at[a * 4 + b],
            groups=1 - g,
        ).wait_recv()

    def unit_relay(a):
        origin = lax.rem(s + 4 - a, 4) * 4 + across
        return remote(
            blk.at[origin], blk.at[origin], relay_ssem.at[a], unit_rsem.at[a * 4 + 2],
            tgt=near_end,
        )

    unit_copies(lambda copy: copy.start())
    blk[me] = su[s]
    back = lax.rem(4 + z - across, 4)

    @pl.when(mid)
    def _():
        for a in range(4):
            unit_wait(a, back)
            unit_relay(a).start()
        for a in range(4):
            unit_wait(a, lax.rem(back + 2, 4))
            unit_wait(a, 2)

    @pl.when(end)
    def _():
        for a in range(4):
            for b in range(1, 4):
                unit_wait(a, b)

    for a in range(1, 4):
        unit_wait(a, 0)

    block = jnp.concatenate([blk[d].astype(f32) for d in range(16)], axis=0).astype(bf16)
    row_ids = lax.broadcasted_iota(jnp.int32, (column_blocks, TBLK), 0)
    expos = []
    row_part = jnp.zeros((128, 1), f32)
    dense = jnp.zeros((column_blocks, TBLK), f32)
    for m in range(MOST):
        scores = lax.dot_general(
            block, tu[m * TBLK:(m + 1) * TBLK, :], (((1,), (1,)), ((), ())),
            preferred_element_type=f32,
        )
        expo = jnp.exp(SCORE_SCALE * scores) * valids[m].astype(f32)
        expos.append(expo)
        row_part = row_part + jnp.sum(expo, axis=1, keepdims=True)
        dense = dense + jnp.where(row_ids == slots[m], jnp.sum(expo, axis=0, keepdims=True), 0.0)
    col_send[...] = dense

    def col_copy(a):
        return remote(
            col_send, col_recv.at[a - 1], col_ssem.at[a - 1], col_rsem.at[a - 1],
            src=lax.rem(s + a, 4),
        )

    for a in range(1, 4):
        col_copy(a).start()
    for a in range(1, 4):
        col_copy(a).wait_recv()
    total = dense + col_recv[0] + col_recv[1] + col_recv[2]
    numer = jnp.zeros((128, features), f32)
    mass = jnp.zeros((128, 1), f32)
    for m in range(MOST):
        picked = jnp.sum(jnp.where(row_ids == slots[m], total, 0.0), axis=0, keepdims=True)
        divisor = jnp.where(valids[m] > 0, picked, 1.0)
        mutual = expos[m] * (expos[m] / divisor)
        mass = mass + jnp.sum(mutual, axis=1, keepdims=True)
        numer = numer + jnp.dot(
            mutual.astype(bf16), tu[m * TBLK:(m + 1) * TBLK, :], preferred_element_type=f32
        )
    for t in range(4):
        num_send[t] = numer[t * 32:(t + 1) * 32].astype(bf16)

    far_end = 3 - near_end

    def num_copy(to, slot, k):
        return remote(
            num_send.at[to], num_recv.at[slot], num_ssem.at[k], num_rsem.at[slot], tgt=to
        )

    def relay_copy(h):
        rows = pl.ds(h * 16, 16)
        return remote(
            num_send.at[far_end, rows], num_relay.at[rows],
            num_ssem.at[h], num_rsem.at[3 + h], tgt=inward,
        )

    def summed_copy(h):
        rows = pl.ds(h * 16, 16)
        return remote(
            num_relay.at[rows], num_recv.at[1, rows],
            num_ssem.at[2 + h], num_rsem.at[5 + h], tgt=far_end,
        )

    def stat_copy(b):
        return remote(
            stat_send, stat_recv.at[b - 1], stat_ssem.at[b - 1], stat_rsem.at[b - 1],
            tgt=lax.rem(z + b, 4),
        )

    @pl.when(end)
    def _():
        relay_copy(0).start()
        relay_copy(1).start()
        num_copy(next_one, 2, 2).start()
        num_copy(inward, 0, 3).start()
        num_recv[2] = jnp.zeros((32, features), bf16)

    @pl.when(mid)
    def _():
        num_copy(across, 1, 0).start()
        num_copy(near_end, 0, 1).start()

    square_eye = lax.broadcasted_iota(jnp.int32, (128, 128), 0) == lax.broadcasted_iota(
        jnp.int32, (128, 128), 1
    )

    def as_row(column):
        return jnp.sum(jnp.where(square_eye, column, 0.0), axis=0, keepdims=True)

    eights = lax.broadcasted_iota(jnp.int32, (8, 128), 0)
    stat_send[...] = jnp.where(
        eights == 0, as_row(mass), jnp.where(eights == 1, as_row(row_part), 0.0)
    )
    for b in range(1, 4):
        stat_copy(b).start()

    @pl.when(mid)
    def _():
        for h in range(2):
            rows = pl.ds(h * 16, 16)
            remote(
                num_send.at[far_end, rows], num_relay.at[rows],
                num_ssem.at[h], num_rsem.at[3 + h], tgt=far_end,
            ).wait_recv()
            num_relay[rows] = (
                num_relay[rows].astype(f32) + num_send[far_end, rows].astype(f32)
            ).astype(bf16)
            summed_copy(h).start()
        num_copy(across, 1, 0).wait_recv()
        num_copy(across, 2, 0).wait_recv()

    @pl.when(end)
    def _():
        for h in range(2):
            rows = pl.ds(h * 16, 16)
            remote(
                num_relay.at[rows], num_recv.at[1, rows],
                num_ssem.at[2 + h], num_rsem.at[5 + h], tgt=far_end,
            ).wait_recv()

    num_copy(across, 0, 0).wait_recv()
    for b in range(1, 4):
        stat_copy(b).wait_recv()
    rows = num_send[z].astype(f32)
    stat = stat_send[...]
    for b in range(3):
        rows = rows + num_recv[b].astype(f32)
        stat = stat + stat_recv[b]
    square = jnp.mean(rows * rows, axis=-1, keepdims=True)
    matched_ref[...] = (rows * lax.rsqrt(square + 1e-06)).astype(bf16)
    logs = jnp.log(stat[0:1] / stat[1:2])
    chosen = (
        lax.broadcasted_iota(jnp.int32, (128, 32), 0)
        == z * 32 + lax.broadcasted_iota(jnp.int32, (128, 32), 1)
    )
    log_ref[...] = jnp.sum(
        jnp.where(chosen, jnp.sum(jnp.where(square_eye, logs, 0.0), axis=1, keepdims=True), 0.0),
        axis=0, keepdims=True,
    )

    own_copies(lambda copy: copy.wait_send())
    to_mate.wait_send()
    to_peer.wait_send()
    to_diag.wait_send()

    def drain(i, carry):
        j = i // NP + 1
        p = lax.rem(i, NP)
        forward, valid = z_copy(j, p)
        pl.when(valid)(forward.wait_send)
        pl.when(has_y(j, p))(lambda: y_copy(j, p).wait_send())
        return carry

    lax.fori_loop(0, 3 * NP, drain, 0)
    for j in (2, 3):
        forward, valid = z_copy(j, NP)
        pl.when(valid & (mid if j == 2 else True))(forward.wait_send)
    to_a(0).wait_send()
    to_a(1).wait_send()
    to_c.wait_send()
    for q in range(4):
        to_b(q).wait_send()
    unit_copies(lambda copy: copy.wait_send())
    pl.when(mid)(lambda: [unit_relay(a).wait_send() for a in range(4)] and None)
    for a in range(1, 4):
        col_copy(a).wait_send()

    @pl.when(end)
    def _():
        relay_copy(0).wait_send()
        relay_copy(1).wait_send()
        num_copy(next_one, 2, 2).wait_send()
        num_copy(inward, 0, 3).wait_send()

    @pl.when(mid)
    def _():
        num_copy(across, 1, 0).wait_send()
        num_copy(near_end, 0, 1).wait_send()
        summed_copy(0).wait_send()
        summed_copy(1).wait_send()

    for b in range(1, 4):
        stat_copy(b).wait_send()


def fused(tokens, sentence_ids, inner_weight, outer_weight, grid_rows, candidates, targets):
    f32, bf16 = jnp.float32, jnp.bfloat16
    features = tokens.shape[1]
    dma = pltpu.SemaphoreType.DMA
    any_spec = pl.BlockSpec(memory_space=pltpu.HBM)
    vmem = pl.BlockSpec(memory_space=pltpu.VMEM)
    matched, logs = pl.pallas_call(
        fused_kernel,
        out_shape=(
            jax.ShapeDtypeStruct((SENT_DEV, features), bf16),
            jax.ShapeDtypeStruct((1, SENT_DEV), f32),
        ),
        in_specs=[
            any_spec,
        ] * 7,
        out_specs=(vmem, vmem),
        scratch_shapes=[
            pltpu.VMEM((1, 256), jnp.int32),
            pltpu.VMEM((1, SENT_DEV), jnp.int32),
            pltpu.SMEM(candidates.shape, jnp.int32),
            pltpu.VMEM((4, 256, features), bf16),
            pltpu.VMEM((2, 4, 256, features), bf16),
            pltpu.VMEM((4, 256, features), f32),
            pltpu.VMEM((4, 256, 256), bf16),
            pltpu.VMEM(targets.shape, bf16),
            pltpu.VMEM((MOST * TBLK, features), bf16),
            pltpu.VMEM((3, 256, features), bf16),
            pltpu.VMEM((3, 256, features), bf16),
            pltpu.VMEM((4, 8, features), bf16),
            pltpu.VMEM((16, 8, features), bf16),
            pltpu.VMEM((4, 32, features), bf16),
            pltpu.VMEM((3, 32, features), bf16),
            pltpu.VMEM((32, features), bf16),
            pltpu.VMEM((8, 128), f32),
            pltpu.VMEM((3, 8, 128), f32),
            pltpu.VMEM((targets.shape[0] // TBLK, TBLK), f32),
            pltpu.VMEM((3, targets.shape[0] // TBLK, TBLK), f32),
            dma((7,)),
            dma((2, NP + 1)),
            dma((3, NP + 1)),
            dma((3, NP)),
            dma((4, NP + 1)),
            dma((4, NP)),
            dma((3,)),
            dma((4,)),
            dma((7,)),
            dma((7,)),
            dma((16,)),
            dma((16,)),
            dma((4,)),
            dma((3,)),
            dma((3,)),
            dma((4,)),
            dma((7,)),
            dma((3,)),
            dma((3,)),
        ],
        compiler_params=pltpu.CompilerParams(
            collective_id=0, has_side_effects=True, vmem_limit_bytes=64 * 1024 * 1024 - 65536
        ),
    )(
        tokens, sentence_ids, inner_weight, outer_weight,
        grid_rows.reshape(1, SENT_DEV), candidates, targets,
    )
    return matched, logs.reshape(SENT_DEV)


def solution(mesh):
    in_specs = (
        P(("groups", "src", "tgt"), None),
        P(("groups", "src", "tgt"), None),
        P(("src", "tgt"), None),
        P(("src", "tgt"), None),
        P(("groups", "src", "tgt")),
        P(("groups", "src"), None),
        P(("groups", "tgt"), None),
    )
    out_specs = (P(("groups", "src", "tgt"), None), P(("groups", "src", "tgt")))
    sizes = tuple(mesh.shape[name] for name in ("groups", "src", "tgt"))
    body = fused if sizes == (2, 4, 4) else on_device
    return jax.shard_map(
        body, mesh=mesh, in_specs=in_specs, out_specs=out_specs, check_vma=False
    )
```

```python
import math

import jax
import jax.numpy as jnp
from jax import lax
from jax.experimental import pallas as pl
from jax.experimental.pallas import tpu as pltpu
from jax.sharding import PartitionSpec as P

SENT_DEV = 32
TBLK = 256
MOST = 4


SCORE_SCALE = 32.0


def unit_rows(values):
    floats = values.astype(jnp.float32)
    square = jnp.mean(floats * floats, axis=-1, keepdims=True)
    return (floats * lax.rsqrt(square + 1e-06) * (1.0 / math.sqrt(values.shape[-1]))).astype(
        jnp.bfloat16
    )


def inner_units(rows, inner):
    product = lax.dot_general(
        rows, inner, (((1,), (1,)), ((), ())), preferred_element_type=jnp.float32
    )
    return jax.nn.gelu(product, approximate=False).astype(jnp.bfloat16)


def layer_norm(summed):
    center = jnp.mean(summed, axis=-1, keepdims=True)
    spread = jnp.mean((summed - center) * (summed - center), axis=-1, keepdims=True)
    return (summed - center) * lax.rsqrt(spread + 1e-05)


def on_device(tokens, sentence_ids, inner_weight, outer_weight, grid_rows, candidates, targets):
    features = tokens.shape[1]
    projected = jnp.dot(
        inner_units(tokens, lax.all_gather(inner_weight, ("src", "tgt"), axis=0, tiled=True)),
        lax.all_gather(outer_weight, ("src", "tgt"), axis=0, tiled=True),
        preferred_element_type=jnp.float32,
    )
    normed = layer_norm(tokens.astype(jnp.float32) + projected)
    members = (sentence_ids[0][None, :] == jnp.arange(SENT_DEV, dtype=jnp.int32)[:, None]).astype(
        jnp.float32
    )
    sums = jnp.dot(members, normed, precision=lax.Precision.HIGHEST)
    unit = unit_rows(sums / jnp.sum(members, axis=1, keepdims=True))
    src_count = lax.axis_size("src")
    tgt_count = lax.axis_size("tgt")
    per_block = SENT_DEV // src_count
    block_rows = tgt_count * SENT_DEV
    order_key = grid_rows // block_rows * per_block + grid_rows % per_block
    reorder = (order_key[None, :] == jnp.arange(SENT_DEV, dtype=jnp.int32)[:, None]).astype(
        jnp.bfloat16
    )
    sorted_units = jnp.dot(reorder, unit, preferred_element_type=jnp.float32).astype(jnp.bfloat16)
    relayed = lax.all_to_all(
        sorted_units.reshape(src_count, per_block, features),
        "src",
        split_axis=0,
        concat_axis=0,
        tiled=True,
    )
    block = lax.all_gather(relayed, "tgt", axis=1, tiled=True).reshape(block_rows, features)
    column_index = lax.axis_index("tgt")
    column_blocks = targets.shape[0] // TBLK
    cand_row = candidates[0]
    listed = (cand_row // column_blocks == column_index).astype(jnp.int32)
    places = jnp.arange(cand_row.shape[0], dtype=jnp.int32)
    ranks = jnp.sum(listed[None, :] * (places[None, :] <= places[:, None]), axis=1) - 1
    chosen = (
        (listed[None, :] == 1) & (ranks[None, :] == jnp.arange(MOST, dtype=jnp.int32)[:, None])
    ).astype(jnp.int32)
    slot_block = jnp.sum(chosen * (cand_row % column_blocks)[None, :], axis=1)
    valid = jnp.sum(chosen, axis=1).astype(jnp.float32)
    tiles = jnp.stack(
        [lax.dynamic_slice_in_dim(targets, slot_block[m] * TBLK, TBLK) for m in range(MOST)]
    )
    target_units = unit_rows(tiles).reshape(MOST * TBLK, features)
    scores = lax.dot_general(
        block, target_units, (((1,), (1,)), ((), ())), preferred_element_type=jnp.float32
    )
    column_valid = jnp.repeat(valid, TBLK)
    expo = jnp.exp(SCORE_SCALE * scores) * column_valid[None, :]
    row_part = jnp.sum(expo, axis=1)
    column_part = jnp.sum(expo, axis=0).reshape(MOST, TBLK)
    picker = (slot_block[:, None] == jnp.arange(column_blocks, dtype=jnp.int32)[None, :]).astype(
        jnp.float32
    )
    column_local = jnp.dot(
        (picker * valid[:, None]).T, column_part, precision=lax.Precision.HIGHEST
    )
    column_total = lax.psum(column_local, "src")
    picked = jnp.dot(picker, column_total, precision=lax.Precision.HIGHEST)
    divisor = jnp.where(valid[:, None] > 0, picked, 1.0).reshape(-1)
    mutual = expo * (expo / divisor[None, :])
    numer = jnp.dot(mutual.astype(jnp.bfloat16), target_units, preferred_element_type=jnp.float32)
    mass_part = jnp.sum(mutual, axis=1)
    row_total = lax.psum(row_part, "tgt")
    numer_rows, mass_rows = (
        lax.psum_scatter(numer, "tgt", scatter_dimension=0, tiled=True),
        lax.psum_scatter(mass_part, "tgt", scatter_dimension=0, tiled=True),
    )
    total_rows = lax.dynamic_slice_in_dim(row_total, column_index * SENT_DEV, SENT_DEV)
    square = jnp.mean(numer_rows * numer_rows, axis=-1, keepdims=True)
    matched = (numer_rows * lax.rsqrt(square + 1e-06)).astype(jnp.bfloat16)
    log_mass = jnp.log(mass_rows / total_rows)
    return (matched, log_mass)


PIECES = ((0, 0), (0, 64), (1, 0), (1, 64))
PROWS = 64
NP = len(PIECES)
HALF = 0.7071067811865476


def remote(source, target, send, recv, /, **device):
    return pltpu.make_async_remote_copy(
        src_ref=source,
        dst_ref=target,
        send_sem=send,
        recv_sem=recv,
        device_id=device,
        device_id_type=pl.DeviceIdType.MESH,
    )


def gelu(product):
    return (0.5 * product * (1.0 + lax.erf(product * HALF))).astype(jnp.bfloat16)


def fused_kernel(
    tok_any, sid_any, win_any, wout_any, grid_any, cand_any, tgt_any,
    matched_ref, log_ref,
    sid_ref, grid_ref, cand_ref, tok, w, acc, hid, tgt, tu, part_send, part_recv, su, blk,
    num_send, num_recv, stat_send, stat_recv, col_send, col_recv,
    local_sem, own_send, fwd_send, y_send, z_recv, y_recv, tok_send, tok_recv,
    part_ssem, part_rsem, unit_ssem, unit_rsem, relay_ssem, col_ssem, col_rsem,
    num_ssem, num_rsem, stat_ssem, stat_rsem,
):
    g = lax.axis_index("groups")
    s = lax.axis_index("src")
    z = lax.axis_index("tgt")
    f32, bf16 = jnp.float32, jnp.bfloat16
    features = tok.shape[2]
    mate = s + 1 - 2 * lax.rem(s, 2)
    peer = lax.rem(s + 2, 4)
    mid = (z == 1) | (z == 2)
    end = (z == 0) | (z == 3)

    locals_ = [
        pltpu.make_async_copy(tok_any, tok.at[0], local_sem.at[0]),
        pltpu.make_async_copy(win_any, w.at[0, z], local_sem.at[1]),
        pltpu.make_async_copy(wout_any, w.at[1, z], local_sem.at[2]),
        pltpu.make_async_copy(tgt_any, tgt, local_sem.at[3]),
        pltpu.make_async_copy(sid_any, sid_ref, local_sem.at[4]),
        pltpu.make_async_copy(grid_any, grid_ref, local_sem.at[5]),
        pltpu.make_async_copy(cand_any, cand_ref, local_sem.at[6]),
    ]

    barrier = pltpu.get_barrier_semaphore()

    def greet(**device):
        pl.semaphore_signal(
            barrier, inc=1, device_id=device, device_id_type=pl.DeviceIdType.MESH
        )

    pl.when(z > 0)(lambda: greet(tgt=z - 1))
    pl.when(z < 3)(lambda: greet(tgt=z + 1))
    greet(groups=1 - g)
    greet(src=mate)
    greet(src=peer)
    for copy in locals_[:3]:
        copy.start()
    pl.semaphore_wait(barrier, 4 + mid.astype(jnp.int32))

    def place(u, half):
        if isinstance(u, int):
            matrix, row = PIECES[u]
        else:
            matrix, row = u // 2, lax.rem(u, 2) * PROWS
        return matrix, pl.multiple_of(half * 128 + row, PROWS)

    def piece(origin, u, half):
        matrix, row = place(u, half)
        return w.at[matrix, origin, pl.ds(row, PROWS)]

    def unit_of(origin, u):
        if isinstance(u, int) and u == NP:
            return piece(origin, NP - 1, 1 - g)
        return piece(origin, u, g)

    def own_copy(direction, u):
        half = 1 - g if u == NP else g
        matrix, row = place(min(u, NP - 1), half)
        return remote(
            (win_any, wout_any)[matrix].at[pl.ds(row, PROWS)], unit_of(z, u),
            own_send.at[direction, u], z_recv.at[z, u],
            tgt=z + 1 if direction == 0 else z - 1,
        )

    def own_copies(method):
        for u in range(NP + 1):
            pl.when(z < 3 if u < NP else z == 0)(lambda u=u: method(own_copy(0, u)))
            pl.when(z > 0 if u < NP else z == 3)(lambda u=u: method(own_copy(1, u)))

    own_copies(lambda copy: copy.start())

    to_mate = remote(tok_any, tok.at[1], tok_send.at[0], tok_recv.at[1], src=mate)
    to_peer = remote(tok_any, tok.at[2], tok_send.at[1], tok_recv.at[2], src=peer)
    to_diag = remote(tok.at[2], tok.at[3], tok_send.at[2], tok_recv.at[3], src=mate)
    to_mate.start()
    to_peer.start()
    for copy in locals_[3:]:
        copy.start()

    first = 1 + lax.rem(z, 2)
    third = jnp.where(z < 2, 3, 0)
    second = 6 - z - first - third

    def origin_of(j):
        return jnp.where(j == 0, z, jnp.where(j == 1, first, jnp.where(j == 2, second, third)))

    def z_copy(j, u):
        origin = origin_of(j)
        ref = unit_of(origin, u)
        from_left = origin < z
        following = jnp.where(from_left, z + 1, z - 1)
        valid = jnp.where(from_left, (z < 3).astype(jnp.int32), (z > 0).astype(jnp.int32)) == 1
        return (
            remote(ref, ref, fwd_send.at[j - 1, u], z_recv.at[origin, u], tgt=following),
            valid,
        )

    def y_copy(j, u):
        origin = origin_of(j)
        ref = piece(origin, u, g)
        return remote(ref, ref, y_send.at[j - 1, u], y_recv.at[origin, u], groups=1 - g)

    def has_y(j, u):
        return (u < NP - 1) | (j == 1) | ((j == 2) & end)

    def y_wait(j, us=range(NP)):
        origin = origin_of(j)
        for u in us:
            ref = piece(origin, u, 1 - g)

            def wait(u=u, ref=ref):
                remote(ref, ref, y_send.at[0, u], y_recv.at[origin, u], groups=1 - g).wait_recv()

            if j == 2 and u == NP - 1:
                pl.when(end)(wait)
            elif j < 3 or u < NP - 1:
                wait()

    def take(j, u):
        ref = unit_of(origin_of(j), u)
        remote(
            ref, ref, own_send.at[0, u], z_recv.at[origin_of(j), u], groups=1 - g
        ).wait_recv()
        forward, valid = z_copy(j, u)
        pl.when(valid)(forward.start)

    for copy in locals_[:3] + locals_[4:]:
        copy.wait()

    def hidden_of(j, r):
        product = lax.dot_general(
            tok[r], w[0, origin_of(j)], (((1,), (1,)), ((), ())), preferred_element_type=f32
        )
        return gelu(product)

    def compute(j, r):
        term = jnp.dot(hidden_of(j, r), w[1, origin_of(j)], preferred_element_type=f32)

        @pl.when(j == 0)
        def _():
            acc[r] = term

        @pl.when(j > 0)
        def _():
            acc[r] += term

    count = jnp.int32(0)
    slots = [jnp.int32(0)] * MOST
    valids = [jnp.int32(0)] * MOST
    column_blocks = tgt.shape[0] // TBLK
    for k in range(cand_ref.shape[1]):
        c = cand_ref[0, k]
        hit = (c // column_blocks == z).astype(jnp.int32)
        for m in range(MOST):
            take_it = hit * (count == m).astype(jnp.int32) == 1
            slots[m] = jnp.where(take_it, lax.rem(c, column_blocks), slots[m])
            valids[m] = jnp.where(take_it, 1, valids[m])
        count = count + hit

    def target_unit(p):
        def some(i, carry):
            row = pl.multiple_of(p * 64 + i * 16, 16)
            tiles = [jnp.zeros((16, features), bf16)] * MOST
            for b in range(column_blocks):
                values = tgt[pl.ds(b * TBLK + row, 16), :]
                for m in range(MOST):
                    keep = jnp.full((16, features), (slots[m] == b).astype(f32), f32)
                    tiles[m] = tiles[m] + values * keep.astype(bf16)
            for m in range(MOST):
                tu[pl.ds(m * TBLK + row, 16), :] = unit_rows(tiles[m])
            return carry

        lax.fori_loop(0, 4, some, 0)

    def step(i, carry):
        j = i // NP + 1
        p = lax.rem(i, NP)
        take(j, p)
        pl.when(has_y(j, p))(lambda: y_copy(j, p).start())
        pl.when((p == NP - 1) & (j > 1) & mid)(lambda: take(j, NP))

        @pl.when(i == 1)
        def _():
            to_mate.wait_recv()

        @pl.when(i == 2)
        def _():
            locals_[3].wait()

        @pl.when((i >= 2) & (i < 6))
        def _():
            target_unit(i - 2)

        @pl.when(i == 6)
        def _():
            to_peer.wait_recv()
            to_diag.start()

        @pl.when(i == 7)
        def _():
            to_diag.wait_recv()

        @pl.when(i == 8)
        def _():
            y_wait(1)

        @pl.when(i == 10)
        def _():
            y_wait(2)

        start = jnp.where(i < 2, i, jnp.where(i < 8, i - 4, 2 * i - 12))
        number = jnp.where(i < 2, 1, jnp.where(i < 6, 0, jnp.where(i < 8, 1, 2)))

        def block(k, carry):
            compute((start + k) // 4, lax.rem(start + k, 4))
            return carry

        lax.fori_loop(0, number, block, 0)
        return carry

    lax.fori_loop(0, 3 * NP, step, 0)

    y_wait(3, (0, 1))

    def inner(r, carry):
        hid[r] = hidden_of(3, r)
        return carry

    lax.fori_loop(0, 4, inner, 0)
    pl.when(end)(lambda: take(3, NP))
    y_wait(3, (2,))

    def to_a(h):
        rows = pl.ds(h * 128, 128)
        return remote(
            part_send.at[0, rows], part_recv.at[0, rows], part_ssem.at[h], part_rsem.at[h],
            src=mate,
        )

    to_c = remote(part_send.at[1], part_recv.at[1], part_ssem.at[2], part_rsem.at[2], src=mate)

    def to_b(q):
        rows = pl.ds(q * 64, 64)
        return remote(
            part_send.at[2, rows], part_recv.at[2, rows],
            part_ssem.at[3 + q], part_rsem.at[3 + q], src=peer,
        )

    def last(i, carry):
        r = 3 - i
        acc[r] += jnp.dot(hid[r], w[1, third], preferred_element_type=f32)

        @pl.when(i == 0)
        def _():
            for h in range(2):
                rows = pl.ds(h * 128, 128)
                part_send[0, rows] = acc[3, rows].astype(bf16)
                to_a(h).start()

        @pl.when(i == 1)
        def _():
            for q in range(4):
                if q % 2 == 0:
                    to_a(q // 2).wait_recv()
                rows = pl.ds(q * 64, 64)
                part_send[2, rows] = (acc[2, rows] + part_recv[0, rows].astype(f32)).astype(bf16)
                to_b(q).start()

        @pl.when(i == 2)
        def _():
            part_send[1] = acc[1].astype(bf16)
            to_c.start()

        return carry

    lax.fori_loop(0, 4, last, 0)

    to_c.wait_recv()
    sums = jnp.zeros((SENT_DEV, features), f32)
    counts = jnp.zeros((SENT_DEV, 1), f32)
    for q in range(4):
        rows = pl.ds(q * 64, 64)
        to_b(q).wait_recv()
        summed = tok[0, rows].astype(f32) + (
            acc[0, rows] + part_recv[1, rows].astype(f32) + part_recv[2, rows].astype(f32)
        )
        normed = layer_norm(summed)
        high = normed.astype(bf16)
        low = (normed - high.astype(f32)).astype(bf16)
        ids = sid_ref[:, q * 64:(q + 1) * 64]
        members = (ids == lax.broadcasted_iota(jnp.int32, (SENT_DEV, 64), 0)).astype(f32)
        counts = counts + jnp.sum(members, axis=1, keepdims=True)
        members = members.astype(bf16)
        sums = sums + (
            jnp.dot(members, high, preferred_element_type=f32)
            + jnp.dot(members, low, preferred_element_type=f32)
        )
    unit = unit_rows(sums / counts)
    grid = grid_ref[...]
    order_key = grid // 128 * 8 + lax.rem(grid, 8)
    reorder = (order_key == lax.broadcasted_iota(jnp.int32, (SENT_DEV, SENT_DEV), 0)).astype(f32)
    ordered = jnp.dot(reorder.astype(bf16), unit, preferred_element_type=f32)
    for b in range(4):
        su[b] = ordered[b * 8:(b + 1) * 8].astype(bf16)

    me = s * 4 + z

    def unit_copy(a, to):
        n = a * 4 + lax.rem(to - z + 4, 4)
        return remote(
            su.at[lax.rem(s + a, 4)], blk.at[me], unit_ssem.at[n], unit_rsem.at[n],
            src=lax.rem(s + a, 4), tgt=to,
        )

    across = 3 - z
    near_end = jnp.where(z < 2, 0, 3)
    inward = jnp.where(z == 0, 1, 2)

    def unit_copies(method):
        for a in range(4):
            method(unit_copy(a, jnp.where(mid, across, inward)))
        for a in range(4):
            method(unit_copy(a, jnp.where(mid, near_end, across)))
        for a in range(1, 4):
            method(unit_copy(a, z))

    def unit_wait(a, b):
        origin = lax.rem(s + 4 - a, 4) * 4 + lax.rem(z + 4 - b, 4)
        remote(
            su.at[0], blk.at[origin], unit_ssem.at[a * 4 + b], unit_rsem.at[a * 4 + b],
            groups=1 - g,
        ).wait_recv()

    def unit_relay(k, a):
        origin = lax.rem(s + 4 - a, 4) * 4 + (across if k == 0 else near_end)
        return remote(
            blk.at[origin], blk.at[origin], relay_ssem.at[k * 4 + a], unit_rsem.at[a * 4 + 2],
            tgt=near_end if k == 0 else across,
        )

    unit_copies(lambda copy: copy.start())
    blk[me] = su[s]

    @pl.when(mid)
    def _():
        for k in range(2):
            for a in range(4):
                unit_wait(a, lax.rem(z + 4 - (across if k == 0 else near_end), 4))
                unit_relay(k, a).start()
        for a in range(4):
            unit_wait(a, 2)

    @pl.when(end)
    def _():
        for a in range(4):
            for b in range(1, 4):
                unit_wait(a, b)

    for a in range(1, 4):
        unit_wait(a, 0)

    block = jnp.concatenate([blk[d].astype(f32) for d in range(16)], axis=0).astype(bf16)
    row_ids = lax.broadcasted_iota(jnp.int32, (column_blocks, TBLK), 0)
    expos = []
    row_part = jnp.zeros((128, 1), f32)
    dense = jnp.zeros((column_blocks, TBLK), f32)
    for m in range(MOST):
        scores = lax.dot_general(
            block, tu[m * TBLK:(m + 1) * TBLK, :], (((1,), (1,)), ((), ())),
            preferred_element_type=f32,
        )
        expo = jnp.exp(SCORE_SCALE * scores) * valids[m].astype(f32)
        expos.append(expo)
        row_part = row_part + jnp.sum(expo, axis=1, keepdims=True)
        dense = dense + jnp.where(row_ids == slots[m], jnp.sum(expo, axis=0, keepdims=True), 0.0)
    col_send[...] = dense

    def col_copy(a):
        return remote(
            col_send, col_recv.at[a - 1], col_ssem.at[a - 1], col_rsem.at[a - 1],
            src=lax.rem(s + a, 4),
        )

    for a in range(1, 4):
        col_copy(a).start()
    for a in range(1, 4):
        col_copy(a).wait_recv()
    total = dense + col_recv[0] + col_recv[1] + col_recv[2]
    numer = jnp.zeros((128, features), f32)
    mass = jnp.zeros((128, 1), f32)
    for m in range(MOST):
        picked = jnp.sum(jnp.where(row_ids == slots[m], total, 0.0), axis=0, keepdims=True)
        divisor = jnp.where(valids[m] > 0, picked, 1.0)
        mutual = expos[m] * (expos[m] / divisor)
        mass = mass + jnp.sum(mutual, axis=1, keepdims=True)
        numer = numer + jnp.dot(
            mutual.astype(bf16), tu[m * TBLK:(m + 1) * TBLK, :], preferred_element_type=f32
        )
    square_eye = lax.broadcasted_iota(jnp.int32, (128, 128), 0) == lax.broadcasted_iota(
        jnp.int32, (128, 128), 1
    )

    def as_row(column):
        return jnp.sum(jnp.where(square_eye, column, 0.0), axis=0, keepdims=True)

    eights = lax.broadcasted_iota(jnp.int32, (8, 128), 0)
    stat_send[...] = jnp.where(
        eights == 0, as_row(mass), jnp.where(eights == 1, as_row(row_part), 0.0)
    )
    for t in range(4):
        num_send[t] = numer[t * 32:(t + 1) * 32].astype(bf16)

    def owner(k):
        order = ((3, 2, 1), (0, 3, 2), (0, 1, 3), (0, 1, 2))
        return jnp.where(
            z == 0, order[0][k],
            jnp.where(z == 1, order[1][k], jnp.where(z == 2, order[2][k], order[3][k])),
        )

    def num_copies(k):
        to = owner(k)
        b = lax.rem(to - z + 4, 4) - 1
        return (
            remote(stat_send, stat_recv.at[b], stat_ssem.at[k], stat_rsem.at[b], tgt=to),
            remote(num_send.at[to], num_recv.at[b], num_ssem.at[k], num_rsem.at[b], tgt=to),
        )

    for k in range(3):
        for copy in num_copies(k):
            copy.start()
    for b in range(3):
        remote(
            num_send.at[0], num_recv.at[b], num_ssem.at[0], num_rsem.at[b], groups=1 - g
        ).wait_recv()
        remote(
            stat_send, stat_recv.at[b], stat_ssem.at[0], stat_rsem.at[b], groups=1 - g
        ).wait_recv()
    rows = num_send[z].astype(f32)
    stat = stat_send[...]
    for b in range(3):
        rows = rows + num_recv[b].astype(f32)
        stat = stat + stat_recv[b]
    square = jnp.mean(rows * rows, axis=-1, keepdims=True)
    matched_ref[...] = (rows * lax.rsqrt(square + 1e-06)).astype(bf16)
    logs = jnp.log(stat[0:1] / stat[1:2])
    chosen = (
        lax.broadcasted_iota(jnp.int32, (128, 32), 0)
        == z * 32 + lax.broadcasted_iota(jnp.int32, (128, 32), 1)
    )
    log_ref[...] = jnp.sum(
        jnp.where(chosen, jnp.sum(jnp.where(square_eye, logs, 0.0), axis=1, keepdims=True), 0.0),
        axis=0, keepdims=True,
    )

    own_copies(lambda copy: copy.wait_send())
    to_mate.wait_send()
    to_peer.wait_send()
    to_diag.wait_send()

    def drain(i, carry):
        j = i // NP + 1
        p = lax.rem(i, NP)
        forward, valid = z_copy(j, p)
        pl.when(valid)(forward.wait_send)
        pl.when(has_y(j, p))(lambda: y_copy(j, p).wait_send())
        return carry

    lax.fori_loop(0, 3 * NP, drain, 0)
    for j in (2, 3):
        forward, valid = z_copy(j, NP)
        pl.when(valid & (mid if j == 2 else True))(forward.wait_send)
    to_a(0).wait_send()
    to_a(1).wait_send()
    to_c.wait_send()
    for q in range(4):
        to_b(q).wait_send()
    unit_copies(lambda copy: copy.wait_send())
    pl.when(mid)(
        lambda: [unit_relay(k, a).wait_send() for k in range(2) for a in range(4)] and None
    )
    for a in range(1, 4):
        col_copy(a).wait_send()

    for k in range(3):
        for copy in num_copies(k):
            copy.wait_send()


def out_kernel(matched_in, log_in, matched_out, log_out, sems):
    copies = [
        pltpu.make_async_copy(matched_in, matched_out, sems.at[0]),
        pltpu.make_async_copy(log_in, log_out, sems.at[1]),
    ]
    for copy in copies:
        copy.start()
    for copy in copies:
        copy.wait()


def fused(tokens, sentence_ids, inner_weight, outer_weight, grid_rows, candidates, targets):
    f32, bf16 = jnp.float32, jnp.bfloat16
    features = tokens.shape[1]
    dma = pltpu.SemaphoreType.DMA
    any_spec = pl.BlockSpec(memory_space=pltpu.HBM)
    vmem = pl.BlockSpec(memory_space=pltpu.VMEM)
    matched, logs = pl.pallas_call(
        fused_kernel,
        out_shape=(
            jax.ShapeDtypeStruct((SENT_DEV, features), bf16),
            jax.ShapeDtypeStruct((1, SENT_DEV), f32),
        ),
        in_specs=[
            any_spec,
        ] * 7,
        out_specs=(vmem, vmem),
        scratch_shapes=[
            pltpu.VMEM((1, 256), jnp.int32),
            pltpu.VMEM((1, SENT_DEV), jnp.int32),
            pltpu.SMEM(candidates.shape, jnp.int32),
            pltpu.VMEM((4, 256, features), bf16),
            pltpu.VMEM((2, 4, 256, features), bf16),
            pltpu.VMEM((4, 256, features), f32),
            pltpu.VMEM((4, 256, 256), bf16),
            pltpu.VMEM(targets.shape, bf16),
            pltpu.VMEM((MOST * TBLK, features), bf16),
            pltpu.VMEM((3, 256, features), bf16),
            pltpu.VMEM((3, 256, features), bf16),
            pltpu.VMEM((4, 8, features), bf16),
            pltpu.VMEM((16, 8, features), bf16),
            pltpu.VMEM((4, 32, features), bf16),
            pltpu.VMEM((3, 32, features), bf16),
            pltpu.VMEM((8, 128), f32),
            pltpu.VMEM((3, 8, 128), f32),
            pltpu.VMEM((targets.shape[0] // TBLK, TBLK), f32),
            pltpu.VMEM((3, targets.shape[0] // TBLK, TBLK), f32),
            dma((7,)),
            dma((2, NP + 1)),
            dma((3, NP + 1)),
            dma((3, NP)),
            dma((4, NP + 1)),
            dma((4, NP)),
            dma((3,)),
            dma((4,)),
            dma((7,)),
            dma((7,)),
            dma((16,)),
            dma((16,)),
            dma((8,)),
            dma((3,)),
            dma((3,)),
            dma((3,)),
            dma((3,)),
            dma((3,)),
            dma((3,)),
        ],
        compiler_params=pltpu.CompilerParams(
            collective_id=0, has_side_effects=True, vmem_limit_bytes=64 * 1024 * 1024 - 65536
        ),
    )(
        tokens, sentence_ids, inner_weight, outer_weight,
        grid_rows.reshape(1, SENT_DEV), candidates, targets,
    )
    anywhere = pl.BlockSpec(memory_space=pl.ANY)
    matched, logs = pl.pallas_call(
        out_kernel,
        out_shape=(
            jax.ShapeDtypeStruct((SENT_DEV, features), bf16),
            jax.ShapeDtypeStruct((1, SENT_DEV), f32),
        ),
        in_specs=[anywhere] * 2,
        out_specs=(anywhere, anywhere),
        scratch_shapes=[dma((2,))],
    )(matched, logs)
    return matched, logs.reshape(SENT_DEV)


def solution(mesh):
    in_specs = (
        P(("groups", "src", "tgt"), None),
        P(("groups", "src", "tgt"), None),
        P(("src", "tgt"), None),
        P(("src", "tgt"), None),
        P(("groups", "src", "tgt")),
        P(("groups", "src"), None),
        P(("groups", "tgt"), None),
    )
    out_specs = (P(("groups", "src", "tgt"), None), P(("groups", "src", "tgt")))
    sizes = tuple(mesh.shape[name] for name in ("groups", "src", "tgt"))
    body = fused if sizes == (2, 4, 4) else on_device
    return jax.shard_map(
        body, mesh=mesh, in_specs=in_specs, out_specs=out_specs, check_vma=False
    )
```

```python
import math

import jax
import jax.numpy as jnp
from jax import lax
from jax.experimental import pallas as pl
from jax.experimental.pallas import tpu as pltpu
from jax.sharding import PartitionSpec as P

SENT_DEV = 32
TBLK = 256
MOST = 4


SCORE_SCALE = 32.0


def unit_rows(values):
    floats = values.astype(jnp.float32)
    square = jnp.mean(floats * floats, axis=-1, keepdims=True)
    return (floats * lax.rsqrt(square + 1e-06) * (1.0 / math.sqrt(values.shape[-1]))).astype(
        jnp.bfloat16
    )


def inner_units(rows, inner):
    product = lax.dot_general(
        rows, inner, (((1,), (1,)), ((), ())), preferred_element_type=jnp.float32
    )
    return jax.nn.gelu(product, approximate=False).astype(jnp.bfloat16)


def layer_norm(summed):
    center = jnp.mean(summed, axis=-1, keepdims=True)
    spread = jnp.mean((summed - center) * (summed - center), axis=-1, keepdims=True)
    return (summed - center) * lax.rsqrt(spread + 1e-05)


def on_device(tokens, sentence_ids, inner_weight, outer_weight, grid_rows, candidates, targets):
    features = tokens.shape[1]
    projected = jnp.dot(
        inner_units(tokens, lax.all_gather(inner_weight, ("src", "tgt"), axis=0, tiled=True)),
        lax.all_gather(outer_weight, ("src", "tgt"), axis=0, tiled=True),
        preferred_element_type=jnp.float32,
    )
    normed = layer_norm(tokens.astype(jnp.float32) + projected)
    members = (sentence_ids[0][None, :] == jnp.arange(SENT_DEV, dtype=jnp.int32)[:, None]).astype(
        jnp.float32
    )
    sums = jnp.dot(members, normed, precision=lax.Precision.HIGHEST)
    unit = unit_rows(sums / jnp.sum(members, axis=1, keepdims=True))
    src_count = lax.axis_size("src")
    tgt_count = lax.axis_size("tgt")
    per_block = SENT_DEV // src_count
    block_rows = tgt_count * SENT_DEV
    order_key = grid_rows // block_rows * per_block + grid_rows % per_block
    reorder = (order_key[None, :] == jnp.arange(SENT_DEV, dtype=jnp.int32)[:, None]).astype(
        jnp.bfloat16
    )
    sorted_units = jnp.dot(reorder, unit, preferred_element_type=jnp.float32).astype(jnp.bfloat16)
    relayed = lax.all_to_all(
        sorted_units.reshape(src_count, per_block, features),
        "src",
        split_axis=0,
        concat_axis=0,
        tiled=True,
    )
    block = lax.all_gather(relayed, "tgt", axis=1, tiled=True).reshape(block_rows, features)
    column_index = lax.axis_index("tgt")
    column_blocks = targets.shape[0] // TBLK
    cand_row = candidates[0]
    listed = (cand_row // column_blocks == column_index).astype(jnp.int32)
    places = jnp.arange(cand_row.shape[0], dtype=jnp.int32)
    ranks = jnp.sum(listed[None, :] * (places[None, :] <= places[:, None]), axis=1) - 1
    chosen = (
        (listed[None, :] == 1) & (ranks[None, :] == jnp.arange(MOST, dtype=jnp.int32)[:, None])
    ).astype(jnp.int32)
    slot_block = jnp.sum(chosen * (cand_row % column_blocks)[None, :], axis=1)
    valid = jnp.sum(chosen, axis=1).astype(jnp.float32)
    tiles = jnp.stack(
        [lax.dynamic_slice_in_dim(targets, slot_block[m] * TBLK, TBLK) for m in range(MOST)]
    )
    target_units = unit_rows(tiles).reshape(MOST * TBLK, features)
    scores = lax.dot_general(
        block, target_units, (((1,), (1,)), ((), ())), preferred_element_type=jnp.float32
    )
    column_valid = jnp.repeat(valid, TBLK)
    expo = jnp.exp(SCORE_SCALE * scores) * column_valid[None, :]
    row_part = jnp.sum(expo, axis=1)
    column_part = jnp.sum(expo, axis=0).reshape(MOST, TBLK)
    picker = (slot_block[:, None] == jnp.arange(column_blocks, dtype=jnp.int32)[None, :]).astype(
        jnp.float32
    )
    column_local = jnp.dot(
        (picker * valid[:, None]).T, column_part, precision=lax.Precision.HIGHEST
    )
    column_total = lax.psum(column_local, "src")
    picked = jnp.dot(picker, column_total, precision=lax.Precision.HIGHEST)
    divisor = jnp.where(valid[:, None] > 0, picked, 1.0).reshape(-1)
    mutual = expo * (expo / divisor[None, :])
    numer = jnp.dot(mutual.astype(jnp.bfloat16), target_units, preferred_element_type=jnp.float32)
    mass_part = jnp.sum(mutual, axis=1)
    row_total = lax.psum(row_part, "tgt")
    numer_rows, mass_rows = (
        lax.psum_scatter(numer, "tgt", scatter_dimension=0, tiled=True),
        lax.psum_scatter(mass_part, "tgt", scatter_dimension=0, tiled=True),
    )
    total_rows = lax.dynamic_slice_in_dim(row_total, column_index * SENT_DEV, SENT_DEV)
    square = jnp.mean(numer_rows * numer_rows, axis=-1, keepdims=True)
    matched = (numer_rows * lax.rsqrt(square + 1e-06)).astype(jnp.bfloat16)
    log_mass = jnp.log(mass_rows / total_rows)
    return (matched, log_mass)


PIECES = ((0, 0), (0, 64), (1, 0), (1, 64))
PROWS = 64
NP = len(PIECES)
HALF = 0.7071067811865476


def remote(source, target, send, recv, /, **device):
    return pltpu.make_async_remote_copy(
        src_ref=source,
        dst_ref=target,
        send_sem=send,
        recv_sem=recv,
        device_id=device,
        device_id_type=pl.DeviceIdType.MESH,
    )


def gelu(product):
    return (0.5 * product * (1.0 + lax.erf(product * HALF))).astype(jnp.bfloat16)


def fused_kernel(
    tok_any, sid_any, win_any, wout_any, grid_any, cand_any, tgt_any,
    matched_ref, log_ref,
    sid_ref, grid_ref, cand_ref, tok, w, acc, hid, tgt, tu, part_send, part_recv, su, blk,
    num_send, num_recv, stat_send, stat_recv, col_send, col_recv,
    local_sem, own_send, fwd_send, y_send, z_recv, y_recv, tok_send, tok_recv,
    part_ssem, part_rsem, unit_ssem, unit_rsem, relay_ssem, col_ssem, col_rsem,
    num_ssem, num_rsem, stat_ssem, stat_rsem,
):
    g = lax.axis_index("groups")
    s = lax.axis_index("src")
    z = lax.axis_index("tgt")
    f32, bf16 = jnp.float32, jnp.bfloat16
    features = tok.shape[2]
    mate = s + 1 - 2 * lax.rem(s, 2)
    peer = lax.rem(s + 2, 4)
    mid = (z == 1) | (z == 2)
    end = (z == 0) | (z == 3)

    locals_ = [
        pltpu.make_async_copy(tok_any, tok.at[0], local_sem.at[0]),
        pltpu.make_async_copy(win_any, w.at[0, z], local_sem.at[1]),
        pltpu.make_async_copy(wout_any, w.at[1, z], local_sem.at[2]),
        pltpu.make_async_copy(tgt_any, tgt, local_sem.at[3]),
        pltpu.make_async_copy(sid_any, sid_ref, local_sem.at[4]),
        pltpu.make_async_copy(grid_any, grid_ref, local_sem.at[5]),
        pltpu.make_async_copy(cand_any, cand_ref, local_sem.at[6]),
    ]

    barrier = pltpu.get_barrier_semaphore()

    def greet(**device):
        pl.semaphore_signal(
            barrier, inc=1, device_id=device, device_id_type=pl.DeviceIdType.MESH
        )

    pl.when(z > 0)(lambda: greet(tgt=z - 1))
    pl.when(z < 3)(lambda: greet(tgt=z + 1))
    greet(groups=1 - g)
    greet(src=mate)
    greet(src=peer)
    for copy in locals_[:3]:
        copy.start()
    pl.semaphore_wait(barrier, 4 + mid.astype(jnp.int32))

    def place(u, half):
        if isinstance(u, int):
            matrix, row = PIECES[u]
        else:
            matrix, row = u // 2, lax.rem(u, 2) * PROWS
        return matrix, pl.multiple_of(half * 128 + row, PROWS)

    def piece(origin, u, half):
        matrix, row = place(u, half)
        return w.at[matrix, origin, pl.ds(row, PROWS)]

    def unit_of(origin, u):
        if isinstance(u, int) and u == NP:
            return piece(origin, NP - 1, 1 - g)
        return piece(origin, u, g)

    def own_copy(direction, u):
        half = 1 - g if u == NP else g
        matrix, row = place(min(u, NP - 1), half)
        return remote(
            (win_any, wout_any)[matrix].at[pl.ds(row, PROWS)], unit_of(z, u),
            own_send.at[direction, u], z_recv.at[z, u],
            tgt=z + 1 if direction == 0 else z - 1,
        )

    def own_copies(method):
        for u in range(NP + 1):
            pl.when(z < 3 if u < NP else z == 0)(lambda u=u: method(own_copy(0, u)))
            pl.when(z > 0 if u < NP else z == 3)(lambda u=u: method(own_copy(1, u)))

    own_copies(lambda copy: copy.start())

    to_mate = remote(tok_any, tok.at[1], tok_send.at[0], tok_recv.at[1], src=mate)
    to_peer = remote(tok_any, tok.at[2], tok_send.at[1], tok_recv.at[2], src=peer)
    to_diag = remote(tok.at[2], tok.at[3], tok_send.at[2], tok_recv.at[3], src=mate)
    to_mate.start()
    to_peer.start()
    for copy in locals_[3:]:
        copy.start()

    first = 1 + lax.rem(z, 2)
    third = jnp.where(z < 2, 3, 0)
    second = 6 - z - first - third

    def origin_of(j):
        return jnp.where(j == 0, z, jnp.where(j == 1, first, jnp.where(j == 2, second, third)))

    def z_copy(j, u):
        origin = origin_of(j)
        ref = unit_of(origin, u)
        from_left = origin < z
        following = jnp.where(from_left, z + 1, z - 1)
        valid = jnp.where(from_left, (z < 3).astype(jnp.int32), (z > 0).astype(jnp.int32)) == 1
        return (
            remote(ref, ref, fwd_send.at[j - 1, u], z_recv.at[origin, u], tgt=following),
            valid,
        )

    def y_copy(j, u):
        origin = origin_of(j)
        ref = piece(origin, u, g)
        return remote(ref, ref, y_send.at[j - 1, u], y_recv.at[origin, u], groups=1 - g)

    def has_y(j, u):
        return (u < NP - 1) | (j == 1) | ((j == 2) & end)

    def y_wait(j, us=range(NP)):
        origin = origin_of(j)
        for u in us:
            ref = piece(origin, u, 1 - g)

            def wait(u=u, ref=ref):
                remote(ref, ref, y_send.at[0, u], y_recv.at[origin, u], groups=1 - g).wait_recv()

            if j == 2 and u == NP - 1:
                pl.when(end)(wait)
            elif j < 3 or u < NP - 1:
                wait()

    def take(j, u):
        ref = unit_of(origin_of(j), u)
        remote(
            ref, ref, own_send.at[0, u], z_recv.at[origin_of(j), u], groups=1 - g
        ).wait_recv()
        forward, valid = z_copy(j, u)
        pl.when(valid)(forward.start)

    for copy in locals_[:3] + locals_[4:]:
        copy.wait()

    def hidden_of(j, r):
        product = lax.dot_general(
            tok[r], w[0, origin_of(j)], (((1,), (1,)), ((), ())), preferred_element_type=f32
        )
        return gelu(product)

    def compute(j, r):
        term = jnp.dot(hidden_of(j, r), w[1, origin_of(j)], preferred_element_type=f32)

        @pl.when(j == 0)
        def _():
            acc[r] = term

        @pl.when(j > 0)
        def _():
            acc[r] += term

    count = jnp.int32(0)
    slots = [jnp.int32(0)] * MOST
    valids = [jnp.int32(0)] * MOST
    column_blocks = tgt.shape[0] // TBLK
    for k in range(cand_ref.shape[1]):
        c = cand_ref[0, k]
        hit = (c // column_blocks == z).astype(jnp.int32)
        for m in range(MOST):
            take_it = hit * (count == m).astype(jnp.int32) == 1
            slots[m] = jnp.where(take_it, lax.rem(c, column_blocks), slots[m])
            valids[m] = jnp.where(take_it, 1, valids[m])
        count = count + hit

    def target_unit(p):
        def some(i, carry):
            row = pl.multiple_of(p * 64 + i * 16, 16)
            tiles = [jnp.zeros((16, features), bf16)] * MOST
            for b in range(column_blocks):
                values = tgt[pl.ds(b * TBLK + row, 16), :]
                for m in range(MOST):
                    keep = jnp.full((16, features), (slots[m] == b).astype(f32), f32)
                    tiles[m] = tiles[m] + values * keep.astype(bf16)
            for m in range(MOST):
                tu[pl.ds(m * TBLK + row, 16), :] = unit_rows(tiles[m])
            return carry

        lax.fori_loop(0, 4, some, 0)

    def step(i, carry):
        j = i // NP + 1
        p = lax.rem(i, NP)
        take(j, p)
        pl.when(has_y(j, p))(lambda: y_copy(j, p).start())
        pl.when((p == NP - 1) & (j > 1) & mid)(lambda: take(j, NP))

        @pl.when(i == 1)
        def _():
            to_mate.wait_recv()

        @pl.when(i == 2)
        def _():
            locals_[3].wait()

        @pl.when((i >= 2) & (i < 6))
        def _():
            target_unit(i - 2)

        @pl.when(i == 6)
        def _():
            to_peer.wait_recv()
            to_diag.start()

        @pl.when(i == 7)
        def _():
            to_diag.wait_recv()

        @pl.when(i == 8)
        def _():
            y_wait(1)

        @pl.when(i == 10)
        def _():
            y_wait(2)

        start = jnp.where(i < 2, i, jnp.where(i < 8, i - 4, 2 * i - 12))
        number = jnp.where(i < 2, 1, jnp.where(i < 6, 0, jnp.where(i < 8, 1, 2)))

        def block(k, carry):
            compute((start + k) // 4, lax.rem(start + k, 4))
            return carry

        lax.fori_loop(0, number, block, 0)
        return carry

    lax.fori_loop(0, 3 * NP, step, 0)

    y_wait(3, (0, 1))

    def inner(r, carry):
        hid[r] = hidden_of(3, r)
        return carry

    lax.fori_loop(0, 4, inner, 0)
    pl.when(end)(lambda: take(3, NP))
    y_wait(3, (2,))

    def to_a(h):
        rows = pl.ds(h * 128, 128)
        return remote(
            part_send.at[0, rows], part_recv.at[0, rows], part_ssem.at[h], part_rsem.at[h],
            src=mate,
        )

    to_c = remote(part_send.at[1], part_recv.at[1], part_ssem.at[2], part_rsem.at[2], src=mate)

    def to_b(q):
        rows = pl.ds(q * 64, 64)
        return remote(
            part_send.at[2, rows], part_recv.at[2, rows],
            part_ssem.at[3 + q], part_rsem.at[3 + q], src=peer,
        )

    def last(i, carry):
        r = 3 - i
        acc[r] += jnp.dot(hid[r], w[1, third], preferred_element_type=f32)

        @pl.when(i == 0)
        def _():
            for h in range(2):
                rows = pl.ds(h * 128, 128)
                part_send[0, rows] = acc[3, rows].astype(bf16)
                to_a(h).start()

        @pl.when(i == 1)
        def _():
            for q in range(4):
                if q % 2 == 0:
                    to_a(q // 2).wait_recv()
                rows = pl.ds(q * 64, 64)
                part_send[2, rows] = (acc[2, rows] + part_recv[0, rows].astype(f32)).astype(bf16)
                to_b(q).start()

        @pl.when(i == 2)
        def _():
            part_send[1] = acc[1].astype(bf16)
            to_c.start()

        return carry

    lax.fori_loop(0, 4, last, 0)

    to_c.wait_recv()
    sums = jnp.zeros((SENT_DEV, features), f32)
    counts = jnp.zeros((SENT_DEV, 1), f32)
    for q in range(4):
        rows = pl.ds(q * 64, 64)
        to_b(q).wait_recv()
        summed = tok[0, rows].astype(f32) + (
            acc[0, rows] + part_recv[1, rows].astype(f32) + part_recv[2, rows].astype(f32)
        )
        normed = layer_norm(summed)
        high = normed.astype(bf16)
        low = (normed - high.astype(f32)).astype(bf16)
        ids = sid_ref[:, q * 64:(q + 1) * 64]
        members = (ids == lax.broadcasted_iota(jnp.int32, (SENT_DEV, 64), 0)).astype(f32)
        counts = counts + jnp.sum(members, axis=1, keepdims=True)
        members = members.astype(bf16)
        sums = sums + (
            jnp.dot(members, high, preferred_element_type=f32)
            + jnp.dot(members, low, preferred_element_type=f32)
        )
    unit = unit_rows(sums / counts)
    grid = grid_ref[...]
    order_key = grid // 128 * 8 + lax.rem(grid, 8)
    reorder = (order_key == lax.broadcasted_iota(jnp.int32, (SENT_DEV, SENT_DEV), 0)).astype(f32)
    ordered = jnp.dot(reorder.astype(bf16), unit, preferred_element_type=f32)
    for b in range(4):
        su[b] = ordered[b * 8:(b + 1) * 8].astype(bf16)

    me = s * 4 + z

    def unit_copy(a, to):
        n = a * 4 + lax.rem(to - z + 4, 4)
        return remote(
            su.at[lax.rem(s + a, 4)], blk.at[me], unit_ssem.at[n], unit_rsem.at[n],
            src=lax.rem(s + a, 4), tgt=to,
        )

    across = 3 - z
    near_end = jnp.where(z < 2, 0, 3)
    next_one = jnp.where(mid, near_end, jnp.where(z == 0, 2, 1))
    inward = jnp.where(z == 0, 1, 2)

    def unit_copies(method):
        for a in range(4):
            method(unit_copy(a, across))
        for a in range(4):
            method(unit_copy(a, next_one))
        pl.when(end)(lambda: [method(unit_copy(a, inward)) for a in range(4)] and None)
        for a in range(1, 4):
            method(unit_copy(a, z))

    def unit_wait(a, b):
        origin = lax.rem(s + 4 - a, 4) * 4 + lax.rem(z + 4 - b, 4)
        remote(
            su.at[0], blk.at[origin], unit_ssem.at[a * 4 + b], unit_rsem.at[a * 4 + b],
            groups=1 - g,
        ).wait_recv()

    def unit_relay(a):
        origin = lax.rem(s + 4 - a, 4) * 4 + across
        return remote(
            blk.at[origin], blk.at[origin], relay_ssem.at[a], unit_rsem.at[a * 4 + 2],
            tgt=near_end,
        )

    unit_copies(lambda copy: copy.start())
    blk[me] = su[s]
    back = lax.rem(4 + z - across, 4)

    @pl.when(mid)
    def _():
        for a in range(4):
            unit_wait(a, back)
            unit_relay(a).start()
        for a in range(4):
            unit_wait(a, lax.rem(back + 2, 4))
            unit_wait(a, 2)

    @pl.when(end)
    def _():
        for a in range(4):
            for b in range(1, 4):
                unit_wait(a, b)

    for a in range(1, 4):
        unit_wait(a, 0)

    block = jnp.concatenate([blk[d].astype(f32) for d in range(16)], axis=0).astype(bf16)
    row_ids = lax.broadcasted_iota(jnp.int32, (column_blocks, TBLK), 0)
    expos = []
    row_part = jnp.zeros((128, 1), f32)
    dense = jnp.zeros((column_blocks, TBLK), f32)
    for m in range(MOST):
        scores = lax.dot_general(
            block, tu[m * TBLK:(m + 1) * TBLK, :], (((1,), (1,)), ((), ())),
            preferred_element_type=f32,
        )
        expo = jnp.exp(SCORE_SCALE * scores) * valids[m].astype(f32)
        expos.append(expo)
        row_part = row_part + jnp.sum(expo, axis=1, keepdims=True)
        dense = dense + jnp.where(row_ids == slots[m], jnp.sum(expo, axis=0, keepdims=True), 0.0)
    col_send[...] = dense

    def col_copy(a):
        return remote(
            col_send, col_recv.at[a - 1], col_ssem.at[a - 1], col_rsem.at[a - 1],
            src=lax.rem(s + a, 4),
        )

    for a in range(1, 4):
        col_copy(a).start()
    for a in range(1, 4):
        col_copy(a).wait_recv()
    total = dense + col_recv[0] + col_recv[1] + col_recv[2]
    numer = jnp.zeros((128, features), f32)
    mass = jnp.zeros((128, 1), f32)
    for m in range(MOST):
        picked = jnp.sum(jnp.where(row_ids == slots[m], total, 0.0), axis=0, keepdims=True)
        divisor = jnp.where(valids[m] > 0, picked, 1.0)
        mutual = expos[m] * (expos[m] / divisor)
        mass = mass + jnp.sum(mutual, axis=1, keepdims=True)
        numer = numer + jnp.dot(
            mutual.astype(bf16), tu[m * TBLK:(m + 1) * TBLK, :], preferred_element_type=f32
        )
    square_eye = lax.broadcasted_iota(jnp.int32, (128, 128), 0) == lax.broadcasted_iota(
        jnp.int32, (128, 128), 1
    )

    def as_row(column):
        return jnp.sum(jnp.where(square_eye, column, 0.0), axis=0, keepdims=True)

    eights = lax.broadcasted_iota(jnp.int32, (8, 128), 0)
    stat_send[...] = jnp.where(
        eights == 0, as_row(mass), jnp.where(eights == 1, as_row(row_part), 0.0)
    )
    for t in range(4):
        num_send[t] = numer[t * 32:(t + 1) * 32].astype(bf16)

    def owner(k):
        order = ((3, 2, 1), (0, 3, 2), (0, 1, 3), (0, 1, 2))
        return jnp.where(
            z == 0, order[0][k],
            jnp.where(z == 1, order[1][k], jnp.where(z == 2, order[2][k], order[3][k])),
        )

    def num_copies(k):
        to = owner(k)
        b = lax.rem(to - z + 4, 4) - 1
        return (
            remote(stat_send, stat_recv.at[b], stat_ssem.at[k], stat_rsem.at[b], tgt=to),
            remote(num_send.at[to], num_recv.at[b], num_ssem.at[k], num_rsem.at[b], tgt=to),
        )

    for k in range(3):
        for copy in num_copies(k):
            copy.start()
    for b in range(3):
        remote(
            num_send.at[0], num_recv.at[b], num_ssem.at[0], num_rsem.at[b], groups=1 - g
        ).wait_recv()
        remote(
            stat_send, stat_recv.at[b], stat_ssem.at[0], stat_rsem.at[b], groups=1 - g
        ).wait_recv()
    rows = num_send[z].astype(f32)
    stat = stat_send[...]
    for b in range(3):
        rows = rows + num_recv[b].astype(f32)
        stat = stat + stat_recv[b]
    square = jnp.mean(rows * rows, axis=-1, keepdims=True)
    matched_ref[...] = (rows * lax.rsqrt(square + 1e-06)).astype(bf16)
    logs = jnp.log(stat[0:1] / stat[1:2])
    chosen = (
        lax.broadcasted_iota(jnp.int32, (128, 32), 0)
        == z * 32 + lax.broadcasted_iota(jnp.int32, (128, 32), 1)
    )
    log_ref[...] = jnp.sum(
        jnp.where(chosen, jnp.sum(jnp.where(square_eye, logs, 0.0), axis=1, keepdims=True), 0.0),
        axis=0, keepdims=True,
    )

    own_copies(lambda copy: copy.wait_send())
    to_mate.wait_send()
    to_peer.wait_send()
    to_diag.wait_send()

    def drain(i, carry):
        j = i // NP + 1
        p = lax.rem(i, NP)
        forward, valid = z_copy(j, p)
        pl.when(valid)(forward.wait_send)
        pl.when(has_y(j, p))(lambda: y_copy(j, p).wait_send())
        return carry

    lax.fori_loop(0, 3 * NP, drain, 0)
    for j in (2, 3):
        forward, valid = z_copy(j, NP)
        pl.when(valid & (mid if j == 2 else True))(forward.wait_send)
    to_a(0).wait_send()
    to_a(1).wait_send()
    to_c.wait_send()
    for q in range(4):
        to_b(q).wait_send()
    unit_copies(lambda copy: copy.wait_send())
    pl.when(mid)(lambda: [unit_relay(a).wait_send() for a in range(4)] and None)
    for a in range(1, 4):
        col_copy(a).wait_send()

    for k in range(3):
        for copy in num_copies(k):
            copy.wait_send()


def fused(tokens, sentence_ids, inner_weight, outer_weight, grid_rows, candidates, targets):
    f32, bf16 = jnp.float32, jnp.bfloat16
    features = tokens.shape[1]
    dma = pltpu.SemaphoreType.DMA
    any_spec = pl.BlockSpec(memory_space=pltpu.HBM)
    vmem = pl.BlockSpec(memory_space=pltpu.VMEM)
    matched, logs = pl.pallas_call(
        fused_kernel,
        out_shape=(pltpu.VMEM((SENT_DEV, features), bf16), pltpu.VMEM((1, SENT_DEV), f32)),
        in_specs=[
            any_spec,
        ] * 7,
        out_specs=(vmem, vmem),
        scratch_shapes=[
            pltpu.VMEM((1, 256), jnp.int32),
            pltpu.VMEM((1, SENT_DEV), jnp.int32),
            pltpu.SMEM(candidates.shape, jnp.int32),
            pltpu.VMEM((4, 256, features), bf16),
            pltpu.VMEM((2, 4, 256, features), bf16),
            pltpu.VMEM((4, 256, features), f32),
            pltpu.VMEM((4, 256, 256), bf16),
            pltpu.VMEM(targets.shape, bf16),
            pltpu.VMEM((MOST * TBLK, features), bf16),
            pltpu.VMEM((3, 256, features), bf16),
            pltpu.VMEM((3, 256, features), bf16),
            pltpu.VMEM((4, 8, features), bf16),
            pltpu.VMEM((16, 8, features), bf16),
            pltpu.VMEM((4, 32, features), bf16),
            pltpu.VMEM((3, 32, features), bf16),
            pltpu.VMEM((8, 128), f32),
            pltpu.VMEM((3, 8, 128), f32),
            pltpu.VMEM((targets.shape[0] // TBLK, TBLK), f32),
            pltpu.VMEM((3, targets.shape[0] // TBLK, TBLK), f32),
            dma((7,)),
            dma((2, NP + 1)),
            dma((3, NP + 1)),
            dma((3, NP)),
            dma((4, NP + 1)),
            dma((4, NP)),
            dma((3,)),
            dma((4,)),
            dma((7,)),
            dma((7,)),
            dma((16,)),
            dma((16,)),
            dma((4,)),
            dma((3,)),
            dma((3,)),
            dma((3,)),
            dma((3,)),
            dma((3,)),
            dma((3,)),
        ],
        compiler_params=pltpu.CompilerParams(
            collective_id=0, has_side_effects=True, vmem_limit_bytes=64 * 1024 * 1024 - 163840
        ),
    )(
        tokens, sentence_ids, inner_weight, outer_weight,
        grid_rows.reshape(1, SENT_DEV), candidates, targets,
    )
    return matched, logs.reshape(SENT_DEV)


def solution(mesh):
    in_specs = (
        P(("groups", "src", "tgt"), None),
        P(("groups", "src", "tgt"), None),
        P(("src", "tgt"), None),
        P(("src", "tgt"), None),
        P(("groups", "src", "tgt")),
        P(("groups", "src"), None),
        P(("groups", "tgt"), None),
    )
    out_specs = (P(("groups", "src", "tgt"), None), P(("groups", "src", "tgt")))
    sizes = tuple(mesh.shape[name] for name in ("groups", "src", "tgt"))
    body = fused if sizes == (2, 4, 4) else on_device
    return jax.shard_map(
        body, mesh=mesh, in_specs=in_specs, out_specs=out_specs, check_vma=False
    )
```

```python
import math

import jax
import jax.numpy as jnp
from jax import lax
from jax.experimental import pallas as pl
from jax.experimental.pallas import tpu as pltpu
from jax.sharding import PartitionSpec as P

SENT_DEV = 32
TBLK = 256
MOST = 4


SCORE_SCALE = 32.0


def unit_rows(values):
    floats = values.astype(jnp.float32)
    square = jnp.mean(floats * floats, axis=-1, keepdims=True)
    return (floats * lax.rsqrt(square + 1e-06) * (1.0 / math.sqrt(values.shape[-1]))).astype(
        jnp.bfloat16
    )


def inner_units(rows, inner):
    product = lax.dot_general(
        rows, inner, (((1,), (1,)), ((), ())), preferred_element_type=jnp.float32
    )
    return jax.nn.gelu(product, approximate=False).astype(jnp.bfloat16)


def layer_norm(summed):
    center = jnp.mean(summed, axis=-1, keepdims=True)
    spread = jnp.mean((summed - center) * (summed - center), axis=-1, keepdims=True)
    return (summed - center) * lax.rsqrt(spread + 1e-05)


def on_device(tokens, sentence_ids, inner_weight, outer_weight, grid_rows, candidates, targets):
    features = tokens.shape[1]
    projected = jnp.dot(
        inner_units(tokens, lax.all_gather(inner_weight, ("src", "tgt"), axis=0, tiled=True)),
        lax.all_gather(outer_weight, ("src", "tgt"), axis=0, tiled=True),
        preferred_element_type=jnp.float32,
    )
    normed = layer_norm(tokens.astype(jnp.float32) + projected)
    members = (sentence_ids[0][None, :] == jnp.arange(SENT_DEV, dtype=jnp.int32)[:, None]).astype(
        jnp.float32
    )
    sums = jnp.dot(members, normed, precision=lax.Precision.HIGHEST)
    unit = unit_rows(sums / jnp.sum(members, axis=1, keepdims=True))
    src_count = lax.axis_size("src")
    tgt_count = lax.axis_size("tgt")
    per_block = SENT_DEV // src_count
    block_rows = tgt_count * SENT_DEV
    order_key = grid_rows // block_rows * per_block + grid_rows % per_block
    reorder = (order_key[None, :] == jnp.arange(SENT_DEV, dtype=jnp.int32)[:, None]).astype(
        jnp.bfloat16
    )
    sorted_units = jnp.dot(reorder, unit, preferred_element_type=jnp.float32).astype(jnp.bfloat16)
    relayed = lax.all_to_all(
        sorted_units.reshape(src_count, per_block, features),
        "src",
        split_axis=0,
        concat_axis=0,
        tiled=True,
    )
    block = lax.all_gather(relayed, "tgt", axis=1, tiled=True).reshape(block_rows, features)
    column_index = lax.axis_index("tgt")
    column_blocks = targets.shape[0] // TBLK
    cand_row = candidates[0]
    listed = (cand_row // column_blocks == column_index).astype(jnp.int32)
    places = jnp.arange(cand_row.shape[0], dtype=jnp.int32)
    ranks = jnp.sum(listed[None, :] * (places[None, :] <= places[:, None]), axis=1) - 1
    chosen = (
        (listed[None, :] == 1) & (ranks[None, :] == jnp.arange(MOST, dtype=jnp.int32)[:, None])
    ).astype(jnp.int32)
    slot_block = jnp.sum(chosen * (cand_row % column_blocks)[None, :], axis=1)
    valid = jnp.sum(chosen, axis=1).astype(jnp.float32)
    tiles = jnp.stack(
        [lax.dynamic_slice_in_dim(targets, slot_block[m] * TBLK, TBLK) for m in range(MOST)]
    )
    target_units = unit_rows(tiles).reshape(MOST * TBLK, features)
    scores = lax.dot_general(
        block, target_units, (((1,), (1,)), ((), ())), preferred_element_type=jnp.float32
    )
    column_valid = jnp.repeat(valid, TBLK)
    expo = jnp.exp(SCORE_SCALE * scores) * column_valid[None, :]
    row_part = jnp.sum(expo, axis=1)
    column_part = jnp.sum(expo, axis=0).reshape(MOST, TBLK)
    picker = (slot_block[:, None] == jnp.arange(column_blocks, dtype=jnp.int32)[None, :]).astype(
        jnp.float32
    )
    column_local = jnp.dot(
        (picker * valid[:, None]).T, column_part, precision=lax.Precision.HIGHEST
    )
    column_total = lax.psum(column_local, "src")
    picked = jnp.dot(picker, column_total, precision=lax.Precision.HIGHEST)
    divisor = jnp.where(valid[:, None] > 0, picked, 1.0).reshape(-1)
    mutual = expo * (expo / divisor[None, :])
    numer = jnp.dot(mutual.astype(jnp.bfloat16), target_units, preferred_element_type=jnp.float32)
    mass_part = jnp.sum(mutual, axis=1)
    row_total = lax.psum(row_part, "tgt")
    numer_rows, mass_rows = (
        lax.psum_scatter(numer, "tgt", scatter_dimension=0, tiled=True),
        lax.psum_scatter(mass_part, "tgt", scatter_dimension=0, tiled=True),
    )
    total_rows = lax.dynamic_slice_in_dim(row_total, column_index * SENT_DEV, SENT_DEV)
    square = jnp.mean(numer_rows * numer_rows, axis=-1, keepdims=True)
    matched = (numer_rows * lax.rsqrt(square + 1e-06)).astype(jnp.bfloat16)
    log_mass = jnp.log(mass_rows / total_rows)
    return (matched, log_mass)


PIECES = ((0, 0), (0, 64), (1, 0), (1, 64))
PROWS = 64
CHUNKS = ((0, 64), (64, 64), (128, 64), (192, 32), (224, 32))
NP = len(PIECES)
HALF = 0.7071067811865476


def remote(source, target, send, recv, /, **device):
    return pltpu.make_async_remote_copy(
        src_ref=source,
        dst_ref=target,
        send_sem=send,
        recv_sem=recv,
        device_id=device,
        device_id_type=pl.DeviceIdType.MESH,
    )


def gelu(product):
    return (0.5 * product * (1.0 + lax.erf(product * HALF))).astype(jnp.bfloat16)


def fused_kernel(
    tok_any, sid_any, win_any, wout_any, grid_any, cand_any, tgt_any,
    matched_ref, log_ref,
    sid_ref, grid_ref, cand_ref, tok, w, acc, hid, tgt, tu, part_send, part_recv, routed, su, blk,
    num_send, num_recv, num_relay, stat_send, stat_recv, col_send, col_recv,
    local_sem, own_send, fwd_send, y_send, z_recv, y_recv, tok_send, tok_recv,
    part_ssem, part_rsem, route_sem, unit_ssem, unit_rsem, relay_ssem, col_ssem, col_rsem,
    num_ssem, num_rsem, relay_rsem, stat_ssem, stat_rsem,
):
    g = lax.axis_index("groups")
    s = lax.axis_index("src")
    z = lax.axis_index("tgt")
    f32, bf16 = jnp.float32, jnp.bfloat16
    features = tok.shape[2]
    mate = s + 1 - 2 * lax.rem(s, 2)
    peer = lax.rem(s + 2, 4)
    mid = (z == 1) | (z == 2)
    end = (z == 0) | (z == 3)
    across = 3 - z
    near_end = jnp.where(z < 2, 0, 3)
    inward = jnp.where(z == 0, 1, 2)

    locals_ = [
        pltpu.make_async_copy(tok_any, tok.at[0], local_sem.at[0]),
        pltpu.make_async_copy(win_any, w.at[0, z], local_sem.at[1]),
        pltpu.make_async_copy(wout_any, w.at[1, z], local_sem.at[2]),
        pltpu.make_async_copy(tgt_any, tgt, local_sem.at[3]),
        pltpu.make_async_copy(sid_any, sid_ref, local_sem.at[4]),
        pltpu.make_async_copy(grid_any, grid_ref, local_sem.at[5]),
        pltpu.make_async_copy(cand_any, cand_ref, local_sem.at[6]),
    ]

    barrier = pltpu.get_barrier_semaphore()

    def greet(**device):
        pl.semaphore_signal(
            barrier, inc=1, device_id=device, device_id_type=pl.DeviceIdType.MESH
        )

    pl.when(z > 0)(lambda: greet(tgt=z - 1))
    pl.when(z < 3)(lambda: greet(tgt=z + 1))
    greet(groups=1 - g)
    greet(src=mate)
    greet(src=peer)
    for copy in locals_[:3]:
        copy.start()
    pl.semaphore_wait(barrier, 4 + mid.astype(jnp.int32))

    def place(u, half):
        if isinstance(u, int):
            matrix, row = PIECES[u]
        else:
            matrix, row = u // 2, lax.rem(u, 2) * PROWS
        return matrix, pl.multiple_of(half * 128 + row, PROWS)

    def piece(origin, u, half):
        matrix, row = place(u, half)
        return w.at[matrix, origin, pl.ds(row, PROWS)]

    def unit_of(origin, u):
        if isinstance(u, int) and u == NP:
            return piece(origin, NP - 1, 1 - g)
        return piece(origin, u, g)

    def own_copy(direction, u):
        half = 1 - g if u == NP else g
        matrix, row = place(min(u, NP - 1), half)
        return remote(
            (win_any, wout_any)[matrix].at[pl.ds(row, PROWS)], unit_of(z, u),
            own_send.at[direction, u], z_recv.at[z, u],
            tgt=z + 1 if direction == 0 else z - 1,
        )

    def own_copies(method):
        for u in range(NP + 1):
            pl.when(z < 3 if u < NP else z == 0)(lambda u=u: method(own_copy(0, u)))
            pl.when(z > 0 if u < NP else z == 3)(lambda u=u: method(own_copy(1, u)))

    own_copies(lambda copy: copy.start())

    to_mate = remote(tok_any, tok.at[1], tok_send.at[0], tok_recv.at[1], src=mate)
    to_peer = remote(tok_any, tok.at[2], tok_send.at[1], tok_recv.at[2], src=peer)
    to_diag = remote(tok.at[2], tok.at[3], tok_send.at[2], tok_recv.at[3], src=mate)
    to_mate.start()
    to_peer.start()
    for copy in locals_[3:]:
        copy.start()

    first = 1 + lax.rem(z, 2)
    third = jnp.where(z < 2, 3, 0)
    second = 6 - z - first - third

    def origin_of(j):
        return jnp.where(j == 0, z, jnp.where(j == 1, first, jnp.where(j == 2, second, third)))

    def z_copy(j, u):
        origin = origin_of(j)
        ref = unit_of(origin, u)
        from_left = origin < z
        following = jnp.where(from_left, z + 1, z - 1)
        valid = jnp.where(from_left, (z < 3).astype(jnp.int32), (z > 0).astype(jnp.int32)) == 1
        return (
            remote(ref, ref, fwd_send.at[j - 1, u], z_recv.at[origin, u], tgt=following),
            valid,
        )

    def y_copy(j, u):
        origin = origin_of(j)
        ref = piece(origin, u, g)
        return remote(ref, ref, y_send.at[j - 1, u], y_recv.at[origin, u], groups=1 - g)

    def has_y(j, u):
        return (u < NP - 1) | (j == 1) | ((j == 2) & end)

    def y_wait(j, us=range(NP)):
        origin = origin_of(j)
        for u in us:
            ref = piece(origin, u, 1 - g)

            def wait(u=u, ref=ref):
                remote(ref, ref, y_send.at[0, u], y_recv.at[origin, u], groups=1 - g).wait_recv()

            if j == 2 and u == NP - 1:
                pl.when(end)(wait)
            elif j < 3 or u < NP - 1:
                wait()

    def take(j, u):
        ref = unit_of(origin_of(j), u)
        remote(
            ref, ref, own_send.at[0, u], z_recv.at[origin_of(j), u], groups=1 - g
        ).wait_recv()
        forward, valid = z_copy(j, u)
        pl.when(valid)(forward.start)

    for copy in locals_[:3] + locals_[4:]:
        copy.wait()

    def hidden_of(j, r):
        product = lax.dot_general(
            tok[r], w[0, origin_of(j)], (((1,), (1,)), ((), ())), preferred_element_type=f32
        )
        return gelu(product)

    def compute(j, r):
        term = jnp.dot(hidden_of(j, r), w[1, origin_of(j)], preferred_element_type=f32)

        @pl.when(j == 0)
        def _():
            acc[r] = term

        @pl.when(j > 0)
        def _():
            acc[r] += term

    count = jnp.int32(0)
    slots = [jnp.int32(0)] * MOST
    valids = [jnp.int32(0)] * MOST
    column_blocks = tgt.shape[0] // TBLK
    for k in range(cand_ref.shape[1]):
        c = cand_ref[0, k]
        hit = (c // column_blocks == z).astype(jnp.int32)
        for m in range(MOST):
            take_it = hit * (count == m).astype(jnp.int32) == 1
            slots[m] = jnp.where(take_it, lax.rem(c, column_blocks), slots[m])
            valids[m] = jnp.where(take_it, 1, valids[m])
        count = count + hit

    for m in range(MOST):
        col_send[MOST + m:MOST + m + 1] = jnp.full(
            (1, TBLK), jnp.where(valids[m] > 0, slots[m], -1).astype(f32), f32
        )

    def target_unit(p):
        def some(i, carry):
            row = pl.multiple_of(p * 64 + i * 16, 16)
            tiles = [jnp.zeros((16, features), bf16)] * MOST
            for b in range(column_blocks):
                values = tgt[pl.ds(b * TBLK + row, 16), :]
                for m in range(MOST):
                    keep = jnp.full((16, features), (slots[m] == b).astype(f32), f32)
                    tiles[m] = tiles[m] + values * keep.astype(bf16)
            for m in range(MOST):
                tu[pl.ds(m * TBLK + row, 16), :] = unit_rows(tiles[m])
            return carry

        lax.fori_loop(0, 4, some, 0)

    def step(i, carry):
        j = i // NP + 1
        p = lax.rem(i, NP)
        take(j, p)
        pl.when(has_y(j, p))(lambda: y_copy(j, p).start())
        pl.when((p == NP - 1) & (j > 1) & mid)(lambda: take(j, NP))

        @pl.when(i == 1)
        def _():
            to_mate.wait_recv()

        @pl.when(i == 2)
        def _():
            locals_[3].wait()

        @pl.when((i >= 2) & (i < 6))
        def _():
            target_unit(i - 2)

        @pl.when(i == 6)
        def _():
            to_peer.wait_recv()
            to_diag.start()

        @pl.when(i == 7)
        def _():
            to_diag.wait_recv()

        @pl.when(i == 8)
        def _():
            y_wait(1)

        @pl.when(i == 10)
        def _():
            y_wait(2)

        start = jnp.where(i < 2, i, jnp.where(i < 8, i - 4, 2 * i - 12))
        number = jnp.where(i < 2, 1, jnp.where(i < 6, 0, jnp.where(i < 8, 1, 2)))

        def block(k, carry):
            compute((start + k) // 4, lax.rem(start + k, 4))
            return carry

        lax.fori_loop(0, number, block, 0)
        return carry

    lax.fori_loop(0, 3 * NP, step, 0)

    y_wait(3, (0, 1))

    def inner(k, carry):
        hid[3 - k] = hidden_of(3, 3 - k)
        return carry

    lax.fori_loop(0, 2, inner, 0)
    pl.when(end)(lambda: take(3, NP))
    y_wait(3, (2,))

    def quarter(q):
        return pl.ds(pl.multiple_of(q * 64, 64), 64)

    def to_a(q):
        rows = quarter(q)
        return remote(
            part_send.at[0, rows], part_recv.at[0, rows], part_ssem.at[q], part_rsem.at[q],
            src=mate,
        )

    to_c = remote(part_send.at[1], part_recv.at[1], part_ssem.at[4], part_rsem.at[4], src=mate)

    def to_b(k):
        rows = pl.ds(*CHUNKS[k])
        return remote(
            part_send.at[2, rows], part_recv.at[2, rows],
            part_ssem.at[5 + k], part_rsem.at[5 + k], src=peer,
        )

    def to_route(**device):
        return remote(
            part_send.at[2, pl.ds(*CHUNKS[0])], routed, part_ssem.at[5], route_sem.at[0], **device
        )

    hand_on = remote(
        routed, part_recv.at[2, pl.ds(*CHUNKS[0])], route_sem.at[1], part_rsem.at[5], tgt=near_end
    )

    def outer(r, rows):
        return acc[r, rows] + jnp.dot(hid[r, rows], w[1, third], preferred_element_type=f32)

    def for_diag(q, carry):
        rows = quarter(q)
        part_send[0, rows] = outer(3, rows).astype(bf16)
        to_a(q).start()
        return carry

    lax.fori_loop(0, 4, for_diag, 0)

    def for_peer(q, carry):
        rows = quarter(q)
        mine = outer(2, rows)
        to_a(q).wait_recv()
        part_send[2, rows] = (mine + part_recv[0, rows].astype(f32)).astype(bf16)
        for k in range(len(CHUNKS)):
            ready = q == (CHUNKS[k][0] + CHUNKS[k][1] - 1) // 64
            pl.when(ready if k else ready & mid)(to_b(k).start)
        pl.when((q == (CHUNKS[0][1] - 1) // 64) & end)(to_route(src=peer, tgt=inward).start)
        return carry

    lax.fori_loop(0, 4, for_peer, 0)

    def for_chip(k, carry):
        r = 1 - k
        hid[r] = hidden_of(3, r)
        acc[r] += jnp.dot(hid[r], w[1, third], preferred_element_type=f32)

        @pl.when(k == 0)
        def _():
            part_send[1] = acc[1].astype(bf16)
            to_c.start()

        return carry

    lax.fori_loop(0, 2, for_chip, 0)

    @pl.when(mid)
    def _():
        num_recv[:, 1] = jnp.zeros((2, 32, features // 2), bf16)
        to_route(groups=1 - g).wait_recv()
        hand_on.start()

    members = (
        sid_ref[...] == lax.broadcasted_iota(jnp.int32, (SENT_DEV, 256), 0)
    ).astype(f32)
    counts = jnp.sum(members, axis=1, keepdims=True)
    members = members.astype(bf16)
    grid = grid_ref[...]
    order_key = grid // 128 * 8 + lax.rem(grid, 8)
    reorder = (
        order_key == lax.broadcasted_iota(jnp.int32, (SENT_DEV, SENT_DEV), 0)
    ).astype(f32).astype(bf16)
    own_copies(lambda copy: copy.wait_send())
    to_mate.wait_send()
    to_peer.wait_send()
    to_diag.wait_send()

    def drain(i, carry):
        j = i // NP + 1
        p = lax.rem(i, NP)
        forward, valid = z_copy(j, p)
        pl.when(valid)(forward.wait_send)
        pl.when(has_y(j, p))(lambda: y_copy(j, p).wait_send())
        return carry

    lax.fori_loop(0, 3 * NP, drain, 0)
    for j in (2, 3):
        forward, valid = z_copy(j, NP)
        pl.when(valid & (mid if j == 2 else True))(forward.wait_send)
    to_c.wait_recv()
    acc[0] = tok[0].astype(f32) + (acc[0] + part_recv[1].astype(f32))
    sums = jnp.zeros((SENT_DEV, features), f32)
    for k in (1, 2, 0, 3, 4):
        start, size = CHUNKS[k]
        rows = pl.ds(start, size)
        to_b(k).wait_recv()
        normed = layer_norm(acc[0, rows] + part_recv[2, rows].astype(f32))
        high = normed.astype(bf16)
        low = (normed - high.astype(f32)).astype(bf16)
        here = members[:, start:start + size]
        sums = sums + (
            jnp.dot(here, high, preferred_element_type=f32)
            + jnp.dot(here, low, preferred_element_type=f32)
        )
    unit = unit_rows(sums / counts)
    ordered = jnp.dot(reorder, unit, preferred_element_type=f32)
    for b in range(4):
        su[b] = ordered[b * 8:(b + 1) * 8].astype(bf16)

    me = s * 4 + z

    def unit_copy(to_s, to):
        n = lax.rem(to_s - s + 4, 4) * 4 + lax.rem(to - z + 4, 4)
        return remote(
            su.at[to_s], blk.at[me], unit_ssem.at[n], unit_rsem.at[n], src=to_s, tgt=to
        )

    diag = lax.rem(mate + 2, 4)
    far = jnp.where(z < 2, 3, 0)
    middle = jnp.where(z < 2, 2, 1)
    beside = jnp.where(mid, near_end, inward)

    def unit_copies(method):
        for to in (far, middle, beside, z):
            for to_s in (peer, diag):
                method(unit_copy(to_s, to))
        for to in (far, middle, beside):
            for to_s in (mate, s):
                method(unit_copy(to_s, to))
        method(unit_copy(mate, z))

    def unit_wait(a, b):
        origin = lax.rem(s + 4 - a, 4) * 4 + lax.rem(z + 4 - b, 4)
        remote(
            su.at[0], blk.at[origin], unit_ssem.at[a * 4 + b], unit_rsem.at[a * 4 + b],
            groups=1 - g,
        ).wait_recv()

    unit_copies(lambda copy: copy.start())
    blk[me] = su[s]
    for q in range(4):
        to_a(q).wait_send()
    to_c.wait_send()
    for k in range(len(CHUNKS)):
        to_b(k).wait_send()
    pl.when(mid)(hand_on.wait_send)
    for a in range(4):
        for b in range(4):
            if a or b:
                unit_wait(a, b)

    block = jnp.concatenate([blk[d].astype(f32) for d in range(16)], axis=0).astype(bf16)
    square_eye = lax.broadcasted_iota(jnp.int32, (128, 128), 0) == lax.broadcasted_iota(
        jnp.int32, (128, 128), 1
    )

    def as_row(column):
        return jnp.sum(jnp.where(square_eye, column, 0.0), axis=0, keepdims=True)

    expos = []
    row_part = jnp.zeros((128, 1), f32)
    for m in range(MOST):
        scores = lax.dot_general(
            block, tu[m * TBLK:(m + 1) * TBLK, :], (((1,), (1,)), ((), ())),
            preferred_element_type=f32,
        )
        expo = jnp.exp(SCORE_SCALE * scores) * valids[m].astype(f32)
        expos.append(expo)
        row_part = row_part + jnp.sum(expo, axis=1, keepdims=True)
        col_send[m:m + 1] = jnp.sum(expo, axis=0, keepdims=True)

    def col_copy(a):
        return remote(
            col_send, col_recv.at[a - 1], col_ssem.at[a - 1], col_rsem.at[a - 1],
            src=lax.rem(s + a, 4),
        )

    for a in (2, 1, 3):
        col_copy(a).start()
    row_row = as_row(row_part)
    unit_copies(lambda copy: copy.wait_send())
    for a in range(1, 4):
        col_copy(a).wait_recv()
    mass = jnp.zeros((128, 1), f32)
    mutuals = []
    for m in range(MOST):
        mine = slots[m].astype(f32)
        total = col_send[m:m + 1]
        for a in range(3):
            total = total + jnp.sum(
                jnp.where(col_recv[a, MOST:] == mine, col_recv[a, :MOST], 0.0),
                axis=0, keepdims=True,
            )
        inverse = 1.0 / jnp.where(valids[m] > 0, total, 1.0)
        mutual = expos[m] * (expos[m] * inverse)
        mass = mass + jnp.sum(mutual, axis=1, keepdims=True)
        mutuals.append(mutual.astype(bf16))
    half = features // 2

    def numer_half(f):
        numer = jnp.zeros((128, half), f32)
        for m in range(MOST):
            numer = numer + jnp.dot(
                mutuals[m], tu[m * TBLK:(m + 1) * TBLK, f * half:(f + 1) * half],
                preferred_element_type=f32,
            )
        for t in range(4):
            num_send[f, t] = numer[t * 32:(t + 1) * 32].astype(bf16)

    eights = lax.broadcasted_iota(jnp.int32, (8, 128), 0)
    stat_send[...] = jnp.where(
        eights == 0, as_row(mass), jnp.where(eights == 1, row_row, 0.0)
    )
    def owner(k):
        return (far, middle, beside)[k]

    def stat_copy(k):
        b = lax.rem(owner(k) - z + 4, 4) - 1
        return remote(stat_send, stat_recv.at[b], stat_ssem.at[k], stat_rsem.at[b], tgt=owner(k))

    def num_copy(f, k):
        b = lax.rem(owner(k) - z + 4, 4) - 1
        return remote(
            num_send.at[f, owner(k)], num_recv.at[f, b], num_ssem.at[f, k], num_rsem.at[f, b],
            tgt=owner(k),
        )

    def to_relay(f, **device):
        return remote(
            num_send.at[f, middle], num_relay.at[f], num_ssem.at[f, 1], relay_rsem.at[f], **device
        )

    def relayed(f):
        b = lax.rem(across - z + 4, 4) - 1
        return remote(
            num_relay.at[f], num_recv.at[f, b], num_ssem.at[f, 1], num_rsem.at[f, b], tgt=across
        )

    for f in range(2):
        numer_half(f)
        pl.when(end)(to_relay(f, tgt=inward).start)
        num_copy(f, 0).start()
        num_copy(f, 2).start()
        if f == 0:
            for k in range(3):
                stat_copy(k).start()

    @pl.when(mid)
    def _():
        for f in range(2):
            to_relay(f, groups=1 - g).wait_recv()
            num_relay[f] = (num_relay[f].astype(f32) + num_send[f, across].astype(f32)).astype(bf16)
            relayed(f).start()

    def num_wait(f, b):
        remote(
            num_send.at[0, 0], num_recv.at[f, b], num_ssem.at[0, 0], num_rsem.at[f, b],
            groups=1 - g,
        ).wait_recv()

    for a in range(1, 4):
        col_copy(a).wait_send()

    stat = stat_send[...]
    for b in range(3):
        remote(
            stat_send, stat_recv.at[b], stat_ssem.at[0], stat_rsem.at[b], groups=1 - g
        ).wait_recv()
        stat = stat + stat_recv[b]
    logs = jnp.log(stat[0:1] / stat[1:2])
    chosen = (
        lax.broadcasted_iota(jnp.int32, (128, 32), 0)
        == z * 32 + lax.broadcasted_iota(jnp.int32, (128, 32), 1)
    )
    log_ref[...] = jnp.sum(
        jnp.where(chosen, jnp.sum(jnp.where(square_eye, logs, 0.0), axis=1, keepdims=True), 0.0),
        axis=0, keepdims=True,
    )
    parts = []
    for f in range(2):
        part = num_send[f, z].astype(f32)
        for b in (2, 1, 0):
            if b == 1:
                pl.when(end)(lambda f=f: num_wait(f, 1))
                part = part + jnp.where(end, num_recv[f, 1].astype(f32), 0.0)
            else:
                num_wait(f, b)
                part = part + num_recv[f, b].astype(f32)
        parts.append(part)
    square = (
        jnp.sum(parts[0] * parts[0], axis=-1, keepdims=True)
        + jnp.sum(parts[1] * parts[1], axis=-1, keepdims=True)
    ) / features
    scale = lax.rsqrt(square + 1e-06)
    for f in range(2):
        matched_ref[:, f * half:(f + 1) * half] = (parts[f] * scale).astype(bf16)

    for k in range(3):
        stat_copy(k).wait_send()
    for f in range(2):
        num_copy(f, 0).wait_send()
        num_copy(f, 2).wait_send()
        pl.when(end)(to_relay(f, tgt=inward).wait_send)
        pl.when(mid)(relayed(f).wait_send)


def fused(tokens, sentence_ids, inner_weight, outer_weight, grid_rows, candidates, targets):
    f32, bf16 = jnp.float32, jnp.bfloat16
    features = tokens.shape[1]
    dma = pltpu.SemaphoreType.DMA
    any_spec = pl.BlockSpec(memory_space=pltpu.HBM)
    vmem = pl.BlockSpec(memory_space=pltpu.VMEM)
    matched, logs = pl.pallas_call(
        fused_kernel,
        out_shape=(pltpu.VMEM((SENT_DEV, features), bf16), pltpu.VMEM((1, SENT_DEV), f32)),
        in_specs=[
            any_spec,
        ] * 7,
        out_specs=(vmem, vmem),
        scratch_shapes=[
            pltpu.VMEM((1, 256), jnp.int32),
            pltpu.VMEM((1, SENT_DEV), jnp.int32),
            pltpu.SMEM(candidates.shape, jnp.int32),
            pltpu.VMEM((4, 256, features), bf16),
            pltpu.VMEM((2, 4, 256, features), bf16),
            pltpu.VMEM((4, 256, features), f32),
            pltpu.VMEM((4, 256, 256), bf16),
            pltpu.VMEM(targets.shape, bf16),
            pltpu.VMEM((MOST * TBLK, features), bf16),
            pltpu.VMEM((3, 256, features), bf16),
            pltpu.VMEM((3, 256, features), bf16),
            pltpu.VMEM((CHUNKS[0][1], features), bf16),
            pltpu.VMEM((4, 8, features), bf16),
            pltpu.VMEM((16, 8, features), bf16),
            pltpu.VMEM((2, 4, 32, features // 2), bf16),
            pltpu.VMEM((2, 3, 32, features // 2), bf16),
            pltpu.VMEM((2, 32, features // 2), bf16),
            pltpu.VMEM((8, 128), f32),
            pltpu.VMEM((3, 8, 128), f32),
            pltpu.VMEM((2 * MOST, TBLK), f32),
            pltpu.VMEM((3, 2 * MOST, TBLK), f32),
            dma((7,)),
            dma((2, NP + 1)),
            dma((3, NP + 1)),
            dma((3, NP)),
            dma((4, NP + 1)),
            dma((4, NP)),
            dma((3,)),
            dma((4,)),
            dma((5 + len(CHUNKS),)),
            dma((5 + len(CHUNKS),)),
            dma((2,)),
            dma((16,)),
            dma((16,)),
            dma((4,)),
            dma((3,)),
            dma((3,)),
            dma((2, 3)),
            dma((2, 3)),
            dma((2,)),
            dma((3,)),
            dma((3,)),
        ],
        compiler_params=pltpu.CompilerParams(
            collective_id=0, has_side_effects=True, vmem_limit_bytes=64 * 1024 * 1024 - 163840
        ),
    )(
        tokens, sentence_ids, inner_weight, outer_weight,
        grid_rows.reshape(1, SENT_DEV), candidates, targets,
    )
    return matched, logs.reshape(SENT_DEV)


def solution(mesh):
    in_specs = (
        P(("groups", "src", "tgt"), None),
        P(("groups", "src", "tgt"), None),
        P(("src", "tgt"), None),
        P(("src", "tgt"), None),
        P(("groups", "src", "tgt")),
        P(("groups", "src"), None),
        P(("groups", "tgt"), None),
    )
    out_specs = (P(("groups", "src", "tgt"), None), P(("groups", "src", "tgt")))
    sizes = tuple(mesh.shape[name] for name in ("groups", "src", "tgt"))
    body = fused if sizes == (2, 4, 4) else on_device
    return jax.shard_map(
        body, mesh=mesh, in_specs=in_specs, out_specs=out_specs, check_vma=False
    )
```

```python
import math

import jax
import jax.numpy as jnp
from jax import lax
from jax.experimental import pallas as pl
from jax.experimental.pallas import tpu as pltpu
from jax.sharding import PartitionSpec as P

SENT_DEV = 32
TBLK = 256
MOST = 4


SCORE_SCALE = 32.0


def unit_rows(values):
    floats = values.astype(jnp.float32)
    square = jnp.mean(floats * floats, axis=-1, keepdims=True)
    return (floats * lax.rsqrt(square + 1e-06) * (1.0 / math.sqrt(values.shape[-1]))).astype(
        jnp.bfloat16
    )


def inner_units(rows, inner):
    product = lax.dot_general(
        rows, inner, (((1,), (1,)), ((), ())), preferred_element_type=jnp.float32
    )
    return jax.nn.gelu(product, approximate=False).astype(jnp.bfloat16)


def layer_norm(summed):
    center = jnp.mean(summed, axis=-1, keepdims=True)
    spread = jnp.mean((summed - center) * (summed - center), axis=-1, keepdims=True)
    return (summed - center) * lax.rsqrt(spread + 1e-05)


def on_device(tokens, sentence_ids, inner_weight, outer_weight, grid_rows, candidates, targets):
    features = tokens.shape[1]
    projected = jnp.dot(
        inner_units(tokens, lax.all_gather(inner_weight, ("src", "tgt"), axis=0, tiled=True)),
        lax.all_gather(outer_weight, ("src", "tgt"), axis=0, tiled=True),
        preferred_element_type=jnp.float32,
    )
    normed = layer_norm(tokens.astype(jnp.float32) + projected)
    members = (sentence_ids[0][None, :] == jnp.arange(SENT_DEV, dtype=jnp.int32)[:, None]).astype(
        jnp.float32
    )
    sums = jnp.dot(members, normed, precision=lax.Precision.HIGHEST)
    unit = unit_rows(sums / jnp.sum(members, axis=1, keepdims=True))
    src_count = lax.axis_size("src")
    tgt_count = lax.axis_size("tgt")
    per_block = SENT_DEV // src_count
    block_rows = tgt_count * SENT_DEV
    order_key = grid_rows // block_rows * per_block + grid_rows % per_block
    reorder = (order_key[None, :] == jnp.arange(SENT_DEV, dtype=jnp.int32)[:, None]).astype(
        jnp.bfloat16
    )
    sorted_units = jnp.dot(reorder, unit, preferred_element_type=jnp.float32).astype(jnp.bfloat16)
    relayed = lax.all_to_all(
        sorted_units.reshape(src_count, per_block, features),
        "src",
        split_axis=0,
        concat_axis=0,
        tiled=True,
    )
    block = lax.all_gather(relayed, "tgt", axis=1, tiled=True).reshape(block_rows, features)
    column_index = lax.axis_index("tgt")
    column_blocks = targets.shape[0] // TBLK
    cand_row = candidates[0]
    listed = (cand_row // column_blocks == column_index).astype(jnp.int32)
    places = jnp.arange(cand_row.shape[0], dtype=jnp.int32)
    ranks = jnp.sum(listed[None, :] * (places[None, :] <= places[:, None]), axis=1) - 1
    chosen = (
        (listed[None, :] == 1) & (ranks[None, :] == jnp.arange(MOST, dtype=jnp.int32)[:, None])
    ).astype(jnp.int32)
    slot_block = jnp.sum(chosen * (cand_row % column_blocks)[None, :], axis=1)
    valid = jnp.sum(chosen, axis=1).astype(jnp.float32)
    tiles = jnp.stack(
        [lax.dynamic_slice_in_dim(targets, slot_block[m] * TBLK, TBLK) for m in range(MOST)]
    )
    target_units = unit_rows(tiles).reshape(MOST * TBLK, features)
    scores = lax.dot_general(
        block, target_units, (((1,), (1,)), ((), ())), preferred_element_type=jnp.float32
    )
    column_valid = jnp.repeat(valid, TBLK)
    expo = jnp.exp(SCORE_SCALE * scores) * column_valid[None, :]
    row_part = jnp.sum(expo, axis=1)
    column_part = jnp.sum(expo, axis=0).reshape(MOST, TBLK)
    picker = (slot_block[:, None] == jnp.arange(column_blocks, dtype=jnp.int32)[None, :]).astype(
        jnp.float32
    )
    column_local = jnp.dot(
        (picker * valid[:, None]).T, column_part, precision=lax.Precision.HIGHEST
    )
    column_total = lax.psum(column_local, "src")
    picked = jnp.dot(picker, column_total, precision=lax.Precision.HIGHEST)
    divisor = jnp.where(valid[:, None] > 0, picked, 1.0).reshape(-1)
    mutual = expo * (expo / divisor[None, :])
    numer = jnp.dot(mutual.astype(jnp.bfloat16), target_units, preferred_element_type=jnp.float32)
    mass_part = jnp.sum(mutual, axis=1)
    row_total = lax.psum(row_part, "tgt")
    numer_rows, mass_rows = (
        lax.psum_scatter(numer, "tgt", scatter_dimension=0, tiled=True),
        lax.psum_scatter(mass_part, "tgt", scatter_dimension=0, tiled=True),
    )
    total_rows = lax.dynamic_slice_in_dim(row_total, column_index * SENT_DEV, SENT_DEV)
    square = jnp.mean(numer_rows * numer_rows, axis=-1, keepdims=True)
    matched = (numer_rows * lax.rsqrt(square + 1e-06)).astype(jnp.bfloat16)
    log_mass = jnp.log(mass_rows / total_rows)
    return (matched, log_mass)


PIECES = ((0, 0), (0, 64), (1, 0), (1, 64))
PROWS = 64
CHUNKS = ((0, 64), (64, 64), (128, 64), (192, 32), (224, 32))
NP = len(PIECES)
HALF = 0.7071067811865476


def remote(source, target, send, recv, /, **device):
    return pltpu.make_async_remote_copy(
        src_ref=source,
        dst_ref=target,
        send_sem=send,
        recv_sem=recv,
        device_id=device,
        device_id_type=pl.DeviceIdType.MESH,
    )


def gelu(product):
    return (0.5 * product * (1.0 + lax.erf(product * HALF))).astype(jnp.bfloat16)


def fused_kernel(
    tok_any, sid_any, win_any, wout_any, grid_any, cand_any, tgt_any,
    matched_ref, log_ref,
    sid_ref, grid_ref, cand_ref, tok, w, acc, hid, tgt, tu, part_send, part_recv, routed, su, blk,
    num_send, num_recv, num_relay, stat_send, stat_recv, col_send, col_recv,
    local_sem, own_send, fwd_send, y_send, z_recv, y_recv, tok_send, tok_recv,
    part_ssem, part_rsem, route_sem, unit_ssem, unit_rsem, relay_ssem, col_ssem, col_rsem,
    num_ssem, num_rsem, relay_rsem, stat_ssem, stat_rsem,
):
    g = lax.axis_index("groups")
    s = lax.axis_index("src")
    z = lax.axis_index("tgt")
    f32, bf16 = jnp.float32, jnp.bfloat16
    features = tok.shape[2]
    mate = s + 1 - 2 * lax.rem(s, 2)
    peer = lax.rem(s + 2, 4)
    mid = (z == 1) | (z == 2)
    end = (z == 0) | (z == 3)
    across = 3 - z
    near_end = jnp.where(z < 2, 0, 3)
    inward = jnp.where(z == 0, 1, 2)

    locals_ = [
        pltpu.make_async_copy(tok_any, tok.at[0], local_sem.at[0]),
        pltpu.make_async_copy(win_any, w.at[0, z], local_sem.at[1]),
        pltpu.make_async_copy(wout_any, w.at[1, z], local_sem.at[2]),
        pltpu.make_async_copy(tgt_any, tgt, local_sem.at[3]),
        pltpu.make_async_copy(sid_any, sid_ref, local_sem.at[4]),
        pltpu.make_async_copy(grid_any, grid_ref, local_sem.at[5]),
        pltpu.make_async_copy(cand_any, cand_ref, local_sem.at[6]),
    ]

    barrier = pltpu.get_barrier_semaphore()

    def greet(**device):
        pl.semaphore_signal(
            barrier, inc=1, device_id=device, device_id_type=pl.DeviceIdType.MESH
        )

    pl.when(z > 0)(lambda: greet(tgt=z - 1))
    pl.when(z < 3)(lambda: greet(tgt=z + 1))
    greet(groups=1 - g)
    greet(src=mate)
    greet(src=peer)
    for copy in locals_[:3]:
        copy.start()
    pl.semaphore_wait(barrier, 4 + mid.astype(jnp.int32))

    def place(u, half):
        if isinstance(u, int):
            matrix, row = PIECES[u]
        else:
            matrix, row = u // 2, lax.rem(u, 2) * PROWS
        return matrix, pl.multiple_of(half * 128 + row, PROWS)

    def piece(origin, u, half):
        matrix, row = place(u, half)
        return w.at[matrix, origin, pl.ds(row, PROWS)]

    def unit_of(origin, u):
        if isinstance(u, int) and u == NP:
            return piece(origin, NP - 1, 1 - g)
        return piece(origin, u, g)

    def own_copy(direction, u):
        half = 1 - g if u == NP else g
        matrix, row = place(min(u, NP - 1), half)
        return remote(
            (win_any, wout_any)[matrix].at[pl.ds(row, PROWS)], unit_of(z, u),
            own_send.at[direction, u], z_recv.at[z, u],
            tgt=z + 1 if direction == 0 else z - 1,
        )

    def own_copies(method):
        for u in range(NP + 1):
            pl.when(z < 3 if u < NP else z == 0)(lambda u=u: method(own_copy(0, u)))
            pl.when(z > 0 if u < NP else z == 3)(lambda u=u: method(own_copy(1, u)))

    own_copies(lambda copy: copy.start())

    to_mate = remote(tok_any, tok.at[1], tok_send.at[0], tok_recv.at[1], src=mate)
    to_peer = remote(tok_any, tok.at[2], tok_send.at[1], tok_recv.at[2], src=peer)
    to_diag = remote(tok.at[2], tok.at[3], tok_send.at[2], tok_recv.at[3], src=mate)
    to_mate.start()
    to_peer.start()
    for copy in locals_[3:]:
        copy.start()

    first = 1 + lax.rem(z, 2)
    third = jnp.where(z < 2, 3, 0)
    second = 6 - z - first - third

    def origin_of(j):
        return jnp.where(j == 0, z, jnp.where(j == 1, first, jnp.where(j == 2, second, third)))

    def z_copy(j, u):
        origin = origin_of(j)
        ref = unit_of(origin, u)
        from_left = origin < z
        following = jnp.where(from_left, z + 1, z - 1)
        valid = jnp.where(from_left, (z < 3).astype(jnp.int32), (z > 0).astype(jnp.int32)) == 1
        return (
            remote(ref, ref, fwd_send.at[j - 1, u], z_recv.at[origin, u], tgt=following),
            valid,
        )

    def y_copy(j, u):
        origin = origin_of(j)
        ref = piece(origin, u, g)
        return remote(ref, ref, y_send.at[j - 1, u], y_recv.at[origin, u], groups=1 - g)

    def has_y(j, u):
        return (u < NP - 1) | (j == 1) | ((j == 2) & end)

    def y_wait(j, us=range(NP)):
        origin = origin_of(j)
        for u in us:
            ref = piece(origin, u, 1 - g)

            def wait(u=u, ref=ref):
                remote(ref, ref, y_send.at[0, u], y_recv.at[origin, u], groups=1 - g).wait_recv()

            if j == 2 and u == NP - 1:
                pl.when(end)(wait)
            elif j < 3 or u < NP - 1:
                wait()

    def take(j, u):
        ref = unit_of(origin_of(j), u)
        remote(
            ref, ref, own_send.at[0, u], z_recv.at[origin_of(j), u], groups=1 - g
        ).wait_recv()
        forward, valid = z_copy(j, u)
        pl.when(valid)(forward.start)

    for copy in locals_[:3] + locals_[4:]:
        copy.wait()

    def hidden_of(j, r):
        product = lax.dot_general(
            tok[r], w[0, origin_of(j)], (((1,), (1,)), ((), ())), preferred_element_type=f32
        )
        return gelu(product)

    def compute(j, r):
        term = jnp.dot(hidden_of(j, r), w[1, origin_of(j)], preferred_element_type=f32)

        @pl.when(j == 0)
        def _():
            acc[r] = term

        @pl.when(j > 0)
        def _():
            acc[r] += term

    count = jnp.int32(0)
    slots = [jnp.int32(0)] * MOST
    valids = [jnp.int32(0)] * MOST
    column_blocks = tgt.shape[0] // TBLK
    for k in range(cand_ref.shape[1]):
        c = cand_ref[0, k]
        hit = (c // column_blocks == z).astype(jnp.int32)
        for m in range(MOST):
            take_it = hit * (count == m).astype(jnp.int32) == 1
            slots[m] = jnp.where(take_it, lax.rem(c, column_blocks), slots[m])
            valids[m] = jnp.where(take_it, 1, valids[m])
        count = count + hit

    for m in range(MOST):
        col_send[MOST + m:MOST + m + 1] = jnp.full(
            (1, TBLK), jnp.where(valids[m] > 0, slots[m], -1).astype(f32), f32
        )

    def target_unit(p):
        def some(i, carry):
            row = pl.multiple_of(p * 64 + i * 16, 16)
            tiles = [jnp.zeros((16, features), bf16)] * MOST
            for b in range(column_blocks):
                values = tgt[pl.ds(b * TBLK + row, 16), :]
                for m in range(MOST):
                    keep = jnp.full((16, features), (slots[m] == b).astype(f32), f32)
                    tiles[m] = tiles[m] + values * keep.astype(bf16)
            for m in range(MOST):
                tu[pl.ds(m * TBLK + row, 16), :] = unit_rows(tiles[m])
            return carry

        lax.fori_loop(0, 4, some, 0)

    def step(i, carry):
        j = i // NP + 1
        p = lax.rem(i, NP)
        take(j, p)
        pl.when(has_y(j, p))(lambda: y_copy(j, p).start())
        pl.when((p == NP - 1) & (j > 1) & mid)(lambda: take(j, NP))

        @pl.when(i == 1)
        def _():
            to_mate.wait_recv()

        @pl.when(i == 2)
        def _():
            locals_[3].wait()

        @pl.when((i >= 2) & (i < 6))
        def _():
            target_unit(i - 2)

        @pl.when(i == 6)
        def _():
            to_peer.wait_recv()
            to_diag.start()

        @pl.when(i == 7)
        def _():
            to_diag.wait_recv()

        @pl.when(i == 8)
        def _():
            y_wait(1)

        @pl.when(i == 10)
        def _():
            y_wait(2)

        start = jnp.where(i < 2, i, jnp.where(i < 8, i - 4, 2 * i - 12))
        number = jnp.where(i < 2, 1, jnp.where(i < 6, 0, jnp.where(i < 8, 1, 2)))

        def block(k, carry):
            compute((start + k) // 4, lax.rem(start + k, 4))
            return carry

        lax.fori_loop(0, number, block, 0)
        return carry

    lax.fori_loop(0, 3 * NP, step, 0)

    y_wait(3, (0, 1))

    def inner(k, carry):
        hid[3 - k] = hidden_of(3, 3 - k)
        return carry

    lax.fori_loop(0, 1, inner, 0)
    pl.when(end)(lambda: take(3, NP))
    y_wait(3, (2,))

    def quarter(q):
        return pl.ds(pl.multiple_of(q * 64, 64), 64)

    def to_a(q):
        rows = quarter(q)
        return remote(
            part_send.at[0, rows], part_recv.at[0, rows], part_ssem.at[q], part_rsem.at[q],
            src=mate,
        )

    to_c = remote(part_send.at[1], part_recv.at[1], part_ssem.at[4], part_rsem.at[4], src=mate)

    def to_b(k):
        rows = pl.ds(*CHUNKS[k])
        return remote(
            part_send.at[2, rows], part_recv.at[2, rows],
            part_ssem.at[5 + k], part_rsem.at[5 + k], src=peer,
        )

    def to_route(**device):
        return remote(
            part_send.at[2, pl.ds(*CHUNKS[0])], routed, part_ssem.at[5], route_sem.at[0], **device
        )

    hand_on = remote(
        routed, part_recv.at[2, pl.ds(*CHUNKS[0])], route_sem.at[1], part_rsem.at[5], tgt=near_end
    )

    def outer(r, rows):
        return acc[r, rows] + jnp.dot(hid[r, rows], w[1, third], preferred_element_type=f32)

    def for_diag(q, carry):
        rows = quarter(q)
        part_send[0, rows] = outer(3, rows).astype(bf16)
        to_a(q).start()
        return carry

    lax.fori_loop(0, 4, for_diag, 0)

    def for_peer(q, carry):
        rows = quarter(q)
        mine = outer(2, rows)
        to_a(q).wait_recv()
        part_send[2, rows] = (mine + part_recv[0, rows].astype(f32)).astype(bf16)
        for k in range(len(CHUNKS)):
            ready = q == (CHUNKS[k][0] + CHUNKS[k][1] - 1) // 64
            pl.when(ready if k else ready & mid)(to_b(k).start)
        pl.when((q == (CHUNKS[0][1] - 1) // 64) & end)(to_route(src=peer, tgt=inward).start)
        return carry

    hid[2] = hidden_of(3, 2)
    lax.fori_loop(0, 4, for_peer, 0)

    def for_chip(k, carry):
        r = 1 - k
        hid[r] = hidden_of(3, r)
        acc[r] += jnp.dot(hid[r], w[1, third], preferred_element_type=f32)

        @pl.when(k == 0)
        def _():
            part_send[1] = acc[1].astype(bf16)
            to_c.start()

        return carry

    lax.fori_loop(0, 2, for_chip, 0)

    @pl.when(mid)
    def _():
        num_recv[:, 1] = jnp.zeros((2, 32, features // 2), bf16)
        to_route(groups=1 - g).wait_recv()
        hand_on.start()

    members = (
        sid_ref[...] == lax.broadcasted_iota(jnp.int32, (SENT_DEV, 256), 0)
    ).astype(f32)
    counts = jnp.sum(members, axis=1, keepdims=True)
    members = members.astype(bf16)
    grid = grid_ref[...]
    order_key = grid // 128 * 8 + lax.rem(grid, 8)
    reorder = (
        order_key == lax.broadcasted_iota(jnp.int32, (SENT_DEV, SENT_DEV), 0)
    ).astype(f32).astype(bf16)
    own_copies(lambda copy: copy.wait_send())
    to_mate.wait_send()
    to_peer.wait_send()
    to_diag.wait_send()

    def drain(i, carry):
        j = i // NP + 1
        p = lax.rem(i, NP)
        forward, valid = z_copy(j, p)
        pl.when(valid)(forward.wait_send)
        pl.when(has_y(j, p))(lambda: y_copy(j, p).wait_send())
        return carry

    lax.fori_loop(0, 3 * NP, drain, 0)
    for j in (2, 3):
        forward, valid = z_copy(j, NP)
        pl.when(valid & (mid if j == 2 else True))(forward.wait_send)
    to_c.wait_recv()
    acc[0] = tok[0].astype(f32) + (acc[0] + part_recv[1].astype(f32))
    sums = jnp.zeros((SENT_DEV, features), f32)
    for k in (1, 2, 0, 3, 4):
        start, size = CHUNKS[k]
        rows = pl.ds(start, size)
        to_b(k).wait_recv()
        normed = layer_norm(acc[0, rows] + part_recv[2, rows].astype(f32))
        high = normed.astype(bf16)
        low = (normed - high.astype(f32)).astype(bf16)
        here = members[:, start:start + size]
        sums = sums + (
            jnp.dot(here, high, preferred_element_type=f32)
            + jnp.dot(here, low, preferred_element_type=f32)
        )
    unit = unit_rows(sums / counts)
    ordered = jnp.dot(reorder, unit, preferred_element_type=f32)
    for b in range(4):
        su[b] = ordered[b * 8:(b + 1) * 8].astype(bf16)

    me = s * 4 + z

    def unit_copy(to_s, to):
        n = lax.rem(to_s - s + 4, 4) * 4 + lax.rem(to - z + 4, 4)
        return remote(
            su.at[to_s], blk.at[me], unit_ssem.at[n], unit_rsem.at[n], src=to_s, tgt=to
        )

    diag = lax.rem(mate + 2, 4)
    far = jnp.where(z < 2, 3, 0)
    middle = jnp.where(z < 2, 2, 1)
    beside = jnp.where(mid, near_end, inward)

    def unit_copies(method):
        for to in (far, middle, beside, z):
            for to_s in (peer, diag):
                method(unit_copy(to_s, to))
        for to in (far, middle, beside):
            for to_s in (mate, s):
                method(unit_copy(to_s, to))
        method(unit_copy(mate, z))

    def unit_wait(a, b):
        origin = lax.rem(s + 4 - a, 4) * 4 + lax.rem(z + 4 - b, 4)
        remote(
            su.at[0], blk.at[origin], unit_ssem.at[a * 4 + b], unit_rsem.at[a * 4 + b],
            groups=1 - g,
        ).wait_recv()

    unit_copies(lambda copy: copy.start())
    blk[me] = su[s]
    for q in range(4):
        to_a(q).wait_send()
    to_c.wait_send()
    for k in range(len(CHUNKS)):
        to_b(k).wait_send()
    pl.when(mid)(hand_on.wait_send)
    for a in range(4):
        for b in range(4):
            if a or b:
                unit_wait(a, b)

    block = jnp.concatenate([blk[d].astype(f32) for d in range(16)], axis=0).astype(bf16)
    square_eye = lax.broadcasted_iota(jnp.int32, (128, 128), 0) == lax.broadcasted_iota(
        jnp.int32, (128, 128), 1
    )

    def as_row(column):
        return jnp.sum(jnp.where(square_eye, column, 0.0), axis=0, keepdims=True)

    expos = []
    row_part = jnp.zeros((128, 1), f32)
    for m in range(MOST):
        scores = lax.dot_general(
            block, tu[m * TBLK:(m + 1) * TBLK, :], (((1,), (1,)), ((), ())),
            preferred_element_type=f32,
        )
        expo = jnp.exp(SCORE_SCALE * scores) * valids[m].astype(f32)
        expos.append(expo)
        row_part = row_part + jnp.sum(expo, axis=1, keepdims=True)
        col_send[m:m + 1] = jnp.sum(expo, axis=0, keepdims=True)

    def col_copy(a):
        return remote(
            col_send, col_recv.at[a - 1], col_ssem.at[a - 1], col_rsem.at[a - 1],
            src=lax.rem(s + a, 4),
        )

    for a in (2, 1, 3):
        col_copy(a).start()
    row_row = as_row(row_part)
    unit_copies(lambda copy: copy.wait_send())
    for a in range(1, 4):
        col_copy(a).wait_recv()
    mass = jnp.zeros((128, 1), f32)
    mutuals = []
    for m in range(MOST):
        mine = slots[m].astype(f32)
        total = col_send[m:m + 1]
        for a in range(3):
            total = total + jnp.sum(
                jnp.where(col_recv[a, MOST:] == mine, col_recv[a, :MOST], 0.0),
                axis=0, keepdims=True,
            )
        inverse = 1.0 / jnp.where(valids[m] > 0, total, 1.0)
        mutual = expos[m] * (expos[m] * inverse)
        mass = mass + jnp.sum(mutual, axis=1, keepdims=True)
        mutuals.append(mutual.astype(bf16))
    half = features // 2

    def numer_half(f):
        numer = jnp.zeros((128, half), f32)
        for m in range(MOST):
            numer = numer + jnp.dot(
                mutuals[m], tu[m * TBLK:(m + 1) * TBLK, f * half:(f + 1) * half],
                preferred_element_type=f32,
            )
        for t in range(4):
            num_send[f, t] = numer[t * 32:(t + 1) * 32].astype(bf16)

    eights = lax.broadcasted_iota(jnp.int32, (8, 128), 0)
    stat_send[...] = jnp.where(
        eights == 0, as_row(mass), jnp.where(eights == 1, row_row, 0.0)
    )
    def owner(k):
        return (far, middle, beside)[k]

    def stat_copy(k):
        b = lax.rem(owner(k) - z + 4, 4) - 1
        return remote(stat_send, stat_recv.at[b], stat_ssem.at[k], stat_rsem.at[b], tgt=owner(k))

    def num_copy(f, k):
        b = lax.rem(owner(k) - z + 4, 4) - 1
        return remote(
            num_send.at[f, owner(k)], num_recv.at[f, b], num_ssem.at[f, k], num_rsem.at[f, b],
            tgt=owner(k),
        )

    def to_relay(f, **device):
        return remote(
            num_send.at[f, middle], num_relay.at[f], num_ssem.at[f, 1], relay_rsem.at[f], **device
        )

    def relayed(f):
        b = lax.rem(across - z + 4, 4) - 1
        return remote(
            num_relay.at[f], num_recv.at[f, b], num_ssem.at[f, 1], num_rsem.at[f, b], tgt=across
        )

    for f in range(2):
        numer_half(f)
        pl.when(end)(to_relay(f, tgt=inward).start)
        num_copy(f, 0).start()
        num_copy(f, 2).start()
        if f == 0:
            for k in range(3):
                stat_copy(k).start()

    @pl.when(mid)
    def _():
        for f in range(2):
            to_relay(f, groups=1 - g).wait_recv()
            num_relay[f] = (num_relay[f].astype(f32) + num_send[f, across].astype(f32)).astype(bf16)
            relayed(f).start()

    def num_wait(f, b):
        remote(
            num_send.at[0, 0], num_recv.at[f, b], num_ssem.at[0, 0], num_rsem.at[f, b],
            groups=1 - g,
        ).wait_recv()

    for a in range(1, 4):
        col_copy(a).wait_send()

    stat = stat_send[...]
    for b in range(3):
        remote(
            stat_send, stat_recv.at[b], stat_ssem.at[0], stat_rsem.at[b], groups=1 - g
        ).wait_recv()
        stat = stat + stat_recv[b]
    logs = jnp.log(stat[0:1] / stat[1:2])
    chosen = (
        lax.broadcasted_iota(jnp.int32, (128, 32), 0)
        == z * 32 + lax.broadcasted_iota(jnp.int32, (128, 32), 1)
    )
    log_ref[...] = jnp.sum(
        jnp.where(chosen, jnp.sum(jnp.where(square_eye, logs, 0.0), axis=1, keepdims=True), 0.0),
        axis=0, keepdims=True,
    )
    parts = []
    for f in range(2):
        part = num_send[f, z].astype(f32)
        for b in (2, 1, 0):
            if b == 1:
                pl.when(end)(lambda f=f: num_wait(f, 1))
                part = part + jnp.where(end, num_recv[f, 1].astype(f32), 0.0)
            else:
                num_wait(f, b)
                part = part + num_recv[f, b].astype(f32)
        parts.append(part)
    square = (
        jnp.sum(parts[0] * parts[0], axis=-1, keepdims=True)
        + jnp.sum(parts[1] * parts[1], axis=-1, keepdims=True)
    ) / features
    scale = lax.rsqrt(square + 1e-06)
    for f in range(2):
        matched_ref[:, f * half:(f + 1) * half] = (parts[f] * scale).astype(bf16)

    for k in range(3):
        stat_copy(k).wait_send()
    for f in range(2):
        num_copy(f, 0).wait_send()
        num_copy(f, 2).wait_send()
        pl.when(end)(to_relay(f, tgt=inward).wait_send)
        pl.when(mid)(relayed(f).wait_send)


def fused(tokens, sentence_ids, inner_weight, outer_weight, grid_rows, candidates, targets):
    f32, bf16 = jnp.float32, jnp.bfloat16
    features = tokens.shape[1]
    dma = pltpu.SemaphoreType.DMA
    any_spec = pl.BlockSpec(memory_space=pltpu.HBM)
    vmem = pl.BlockSpec(memory_space=pltpu.VMEM)
    matched, logs = pl.pallas_call(
        fused_kernel,
        out_shape=(pltpu.VMEM((SENT_DEV, features), bf16), pltpu.VMEM((1, SENT_DEV), f32)),
        in_specs=[
            any_spec,
        ] * 7,
        out_specs=(vmem, vmem),
        scratch_shapes=[
            pltpu.VMEM((1, 256), jnp.int32),
            pltpu.VMEM((1, SENT_DEV), jnp.int32),
            pltpu.SMEM(candidates.shape, jnp.int32),
            pltpu.VMEM((4, 256, features), bf16),
            pltpu.VMEM((2, 4, 256, features), bf16),
            pltpu.VMEM((4, 256, features), f32),
            pltpu.VMEM((4, 256, 256), bf16),
            pltpu.VMEM(targets.shape, bf16),
            pltpu.VMEM((MOST * TBLK, features), bf16),
            pltpu.VMEM((3, 256, features), bf16),
            pltpu.VMEM((3, 256, features), bf16),
            pltpu.VMEM((CHUNKS[0][1], features), bf16),
            pltpu.VMEM((4, 8, features), bf16),
            pltpu.VMEM((16, 8, features), bf16),
            pltpu.VMEM((2, 4, 32, features // 2), bf16),
            pltpu.VMEM((2, 3, 32, features // 2), bf16),
            pltpu.VMEM((2, 32, features // 2), bf16),
            pltpu.VMEM((8, 128), f32),
            pltpu.VMEM((3, 8, 128), f32),
            pltpu.VMEM((2 * MOST, TBLK), f32),
            pltpu.VMEM((3, 2 * MOST, TBLK), f32),
            dma((7,)),
            dma((2, NP + 1)),
            dma((3, NP + 1)),
            dma((3, NP)),
            dma((4, NP + 1)),
            dma((4, NP)),
            dma((3,)),
            dma((4,)),
            dma((5 + len(CHUNKS),)),
            dma((5 + len(CHUNKS),)),
            dma((2,)),
            dma((16,)),
            dma((16,)),
            dma((4,)),
            dma((3,)),
            dma((3,)),
            dma((2, 3)),
            dma((2, 3)),
            dma((2,)),
            dma((3,)),
            dma((3,)),
        ],
        compiler_params=pltpu.CompilerParams(
            collective_id=0, has_side_effects=True, vmem_limit_bytes=64 * 1024 * 1024 - 163840
        ),
    )(
        tokens, sentence_ids, inner_weight, outer_weight,
        grid_rows.reshape(1, SENT_DEV), candidates, targets,
    )
    return matched, logs.reshape(SENT_DEV)


def solution(mesh):
    in_specs = (
        P(("groups", "src", "tgt"), None),
        P(("groups", "src", "tgt"), None),
        P(("src", "tgt"), None),
        P(("src", "tgt"), None),
        P(("groups", "src", "tgt")),
        P(("groups", "src"), None),
        P(("groups", "tgt"), None),
    )
    out_specs = (P(("groups", "src", "tgt"), None), P(("groups", "src", "tgt")))
    sizes = tuple(mesh.shape[name] for name in ("groups", "src", "tgt"))
    body = fused if sizes == (2, 4, 4) else on_device
    return jax.shard_map(
        body, mesh=mesh, in_specs=in_specs, out_specs=out_specs, check_vma=False
    )
```

```python
import math

import jax
import jax.numpy as jnp
from jax import lax
from jax.experimental import pallas as pl
from jax.experimental.pallas import tpu as pltpu
from jax.sharding import PartitionSpec as P

SENT_DEV = 32
TBLK = 256
MOST = 4


SCORE_SCALE = 32.0


def unit_rows(values):
    floats = values.astype(jnp.float32)
    square = jnp.mean(floats * floats, axis=-1, keepdims=True)
    return (floats * lax.rsqrt(square + 1e-06) * (1.0 / math.sqrt(values.shape[-1]))).astype(
        jnp.bfloat16
    )


def inner_units(rows, inner):
    product = lax.dot_general(
        rows, inner, (((1,), (1,)), ((), ())), preferred_element_type=jnp.float32
    )
    return jax.nn.gelu(product, approximate=False).astype(jnp.bfloat16)


def layer_norm(summed):
    center = jnp.mean(summed, axis=-1, keepdims=True)
    spread = jnp.mean((summed - center) * (summed - center), axis=-1, keepdims=True)
    return (summed - center) * lax.rsqrt(spread + 1e-05)


def on_device(tokens, sentence_ids, inner_weight, outer_weight, grid_rows, candidates, targets):
    features = tokens.shape[1]
    projected = jnp.dot(
        inner_units(tokens, lax.all_gather(inner_weight, ("src", "tgt"), axis=0, tiled=True)),
        lax.all_gather(outer_weight, ("src", "tgt"), axis=0, tiled=True),
        preferred_element_type=jnp.float32,
    )
    normed = layer_norm(tokens.astype(jnp.float32) + projected)
    members = (sentence_ids[0][None, :] == jnp.arange(SENT_DEV, dtype=jnp.int32)[:, None]).astype(
        jnp.float32
    )
    sums = jnp.dot(members, normed, precision=lax.Precision.HIGHEST)
    unit = unit_rows(sums / jnp.sum(members, axis=1, keepdims=True))
    src_count = lax.axis_size("src")
    tgt_count = lax.axis_size("tgt")
    per_block = SENT_DEV // src_count
    block_rows = tgt_count * SENT_DEV
    order_key = grid_rows // block_rows * per_block + grid_rows % per_block
    reorder = (order_key[None, :] == jnp.arange(SENT_DEV, dtype=jnp.int32)[:, None]).astype(
        jnp.bfloat16
    )
    sorted_units = jnp.dot(reorder, unit, preferred_element_type=jnp.float32).astype(jnp.bfloat16)
    relayed = lax.all_to_all(
        sorted_units.reshape(src_count, per_block, features),
        "src",
        split_axis=0,
        concat_axis=0,
        tiled=True,
    )
    block = lax.all_gather(relayed, "tgt", axis=1, tiled=True).reshape(block_rows, features)
    column_index = lax.axis_index("tgt")
    column_blocks = targets.shape[0] // TBLK
    cand_row = candidates[0]
    listed = (cand_row // column_blocks == column_index).astype(jnp.int32)
    places = jnp.arange(cand_row.shape[0], dtype=jnp.int32)
    ranks = jnp.sum(listed[None, :] * (places[None, :] <= places[:, None]), axis=1) - 1
    chosen = (
        (listed[None, :] == 1) & (ranks[None, :] == jnp.arange(MOST, dtype=jnp.int32)[:, None])
    ).astype(jnp.int32)
    slot_block = jnp.sum(chosen * (cand_row % column_blocks)[None, :], axis=1)
    valid = jnp.sum(chosen, axis=1).astype(jnp.float32)
    tiles = jnp.stack(
        [lax.dynamic_slice_in_dim(targets, slot_block[m] * TBLK, TBLK) for m in range(MOST)]
    )
    target_units = unit_rows(tiles).reshape(MOST * TBLK, features)
    scores = lax.dot_general(
        block, target_units, (((1,), (1,)), ((), ())), preferred_element_type=jnp.float32
    )
    column_valid = jnp.repeat(valid, TBLK)
    expo = jnp.exp(SCORE_SCALE * scores) * column_valid[None, :]
    row_part = jnp.sum(expo, axis=1)
    column_part = jnp.sum(expo, axis=0).reshape(MOST, TBLK)
    picker = (slot_block[:, None] == jnp.arange(column_blocks, dtype=jnp.int32)[None, :]).astype(
        jnp.float32
    )
    column_local = jnp.dot(
        (picker * valid[:, None]).T, column_part, precision=lax.Precision.HIGHEST
    )
    column_total = lax.psum(column_local, "src")
    picked = jnp.dot(picker, column_total, precision=lax.Precision.HIGHEST)
    divisor = jnp.where(valid[:, None] > 0, picked, 1.0).reshape(-1)
    mutual = expo * (expo / divisor[None, :])
    numer = jnp.dot(mutual.astype(jnp.bfloat16), target_units, preferred_element_type=jnp.float32)
    mass_part = jnp.sum(mutual, axis=1)
    row_total = lax.psum(row_part, "tgt")
    numer_rows, mass_rows = (
        lax.psum_scatter(numer, "tgt", scatter_dimension=0, tiled=True),
        lax.psum_scatter(mass_part, "tgt", scatter_dimension=0, tiled=True),
    )
    total_rows = lax.dynamic_slice_in_dim(row_total, column_index * SENT_DEV, SENT_DEV)
    square = jnp.mean(numer_rows * numer_rows, axis=-1, keepdims=True)
    matched = (numer_rows * lax.rsqrt(square + 1e-06)).astype(jnp.bfloat16)
    log_mass = jnp.log(mass_rows / total_rows)
    return (matched, log_mass)


PIECES = ((0, 0), (0, 64), (1, 0), (1, 64))
PROWS = 64
CHUNKS = ((64, 64), (0, 64), (128, 64), (192, 32), (224, 32))
NP = len(PIECES)
HALF = 0.7071067811865476


def remote(source, target, send, recv, /, **device):
    return pltpu.make_async_remote_copy(
        src_ref=source,
        dst_ref=target,
        send_sem=send,
        recv_sem=recv,
        device_id=device,
        device_id_type=pl.DeviceIdType.MESH,
    )


def gelu(product):
    return (0.5 * product * (1.0 + lax.erf(product * HALF))).astype(jnp.bfloat16)


def fused_kernel(
    tok_any, sid_any, win_any, wout_any, grid_any, cand_any, tgt_any,
    matched_ref, log_ref,
    sid_ref, grid_ref, cand_ref, tok, w, acc, hid, tgt, tu, part_send, part_recv, routed, su, blk,
    num_send, num_recv, num_relay, stat_send, stat_recv, col_send, col_recv,
    local_sem, own_send, fwd_send, y_send, z_recv, y_recv, tok_send, tok_recv,
    part_ssem, part_rsem, route_sem, unit_ssem, unit_rsem, relay_ssem, col_ssem, col_rsem,
    num_ssem, num_rsem, relay_rsem, stat_ssem, stat_rsem,
):
    g = lax.axis_index("groups")
    s = lax.axis_index("src")
    z = lax.axis_index("tgt")
    f32, bf16 = jnp.float32, jnp.bfloat16
    features = tok.shape[2]
    mate = s + 1 - 2 * lax.rem(s, 2)
    peer = lax.rem(s + 2, 4)
    mid = (z == 1) | (z == 2)
    end = (z == 0) | (z == 3)
    across = 3 - z
    near_end = jnp.where(z < 2, 0, 3)
    inward = jnp.where(z == 0, 1, 2)

    locals_ = [
        pltpu.make_async_copy(tok_any, tok.at[0], local_sem.at[0]),
        pltpu.make_async_copy(win_any, w.at[0, z], local_sem.at[1]),
        pltpu.make_async_copy(wout_any, w.at[1, z], local_sem.at[2]),
        pltpu.make_async_copy(tgt_any, tgt, local_sem.at[3]),
        pltpu.make_async_copy(sid_any, sid_ref, local_sem.at[4]),
        pltpu.make_async_copy(grid_any, grid_ref, local_sem.at[5]),
        pltpu.make_async_copy(cand_any, cand_ref, local_sem.at[6]),
    ]

    barrier = pltpu.get_barrier_semaphore()

    def greet(**device):
        pl.semaphore_signal(
            barrier, inc=1, device_id=device, device_id_type=pl.DeviceIdType.MESH
        )

    pl.when(z > 0)(lambda: greet(tgt=z - 1))
    pl.when(z < 3)(lambda: greet(tgt=z + 1))
    greet(groups=1 - g)
    greet(src=mate)
    greet(src=peer)
    for copy in locals_[:3]:
        copy.start()
    pl.semaphore_wait(barrier, 4 + mid.astype(jnp.int32))

    def place(u, half):
        if isinstance(u, int):
            matrix, row = PIECES[u]
        else:
            matrix, row = u // 2, lax.rem(u, 2) * PROWS
        return matrix, pl.multiple_of(half * 128 + row, PROWS)

    def piece(origin, u, half):
        matrix, row = place(u, half)
        return w.at[matrix, origin, pl.ds(row, PROWS)]

    def unit_of(origin, u):
        if isinstance(u, int) and u == NP:
            return piece(origin, NP - 1, 1 - g)
        return piece(origin, u, g)

    def own_copy(direction, u):
        half = 1 - g if u == NP else g
        matrix, row = place(min(u, NP - 1), half)
        return remote(
            (win_any, wout_any)[matrix].at[pl.ds(row, PROWS)], unit_of(z, u),
            own_send.at[direction, u], z_recv.at[z, u],
            tgt=z + 1 if direction == 0 else z - 1,
        )

    def own_copies(method):
        for u in range(NP + 1):
            pl.when(z < 3 if u < NP else z == 0)(lambda u=u: method(own_copy(0, u)))
            pl.when(z > 0 if u < NP else z == 3)(lambda u=u: method(own_copy(1, u)))

    own_copies(lambda copy: copy.start())

    to_mate = remote(tok_any, tok.at[1], tok_send.at[0], tok_recv.at[1], src=mate)
    to_peer = remote(tok_any, tok.at[2], tok_send.at[1], tok_recv.at[2], src=peer)
    to_diag = remote(tok.at[2], tok.at[3], tok_send.at[2], tok_recv.at[3], src=mate)
    to_mate.start()
    to_peer.start()
    for copy in locals_[3:]:
        copy.start()

    first = 1 + lax.rem(z, 2)
    third = jnp.where(z < 2, 3, 0)
    second = 6 - z - first - third

    def origin_of(j):
        return jnp.where(j == 0, z, jnp.where(j == 1, first, jnp.where(j == 2, second, third)))

    def z_copy(j, u):
        origin = origin_of(j)
        ref = unit_of(origin, u)
        from_left = origin < z
        following = jnp.where(from_left, z + 1, z - 1)
        valid = jnp.where(from_left, (z < 3).astype(jnp.int32), (z > 0).astype(jnp.int32)) == 1
        return (
            remote(ref, ref, fwd_send.at[j - 1, u], z_recv.at[origin, u], tgt=following),
            valid,
        )

    def y_copy(j, u):
        origin = origin_of(j)
        ref = piece(origin, u, g)
        return remote(ref, ref, y_send.at[j - 1, u], y_recv.at[origin, u], groups=1 - g)

    def has_y(j, u):
        return (u < NP - 1) | (j == 1) | ((j == 2) & end)

    def y_wait(j, us=range(NP)):
        origin = origin_of(j)
        for u in us:
            ref = piece(origin, u, 1 - g)

            def wait(u=u, ref=ref):
                remote(ref, ref, y_send.at[0, u], y_recv.at[origin, u], groups=1 - g).wait_recv()

            if j == 2 and u == NP - 1:
                pl.when(end)(wait)
            elif j < 3 or u < NP - 1:
                wait()

    def take(j, u):
        ref = unit_of(origin_of(j), u)
        remote(
            ref, ref, own_send.at[0, u], z_recv.at[origin_of(j), u], groups=1 - g
        ).wait_recv()
        forward, valid = z_copy(j, u)
        pl.when(valid)(forward.start)

    for copy in locals_[:3] + locals_[4:]:
        copy.wait()

    def hidden_of(j, r):
        product = lax.dot_general(
            tok[r], w[0, origin_of(j)], (((1,), (1,)), ((), ())), preferred_element_type=f32
        )
        return gelu(product)

    def compute(j, r):
        term = jnp.dot(hidden_of(j, r), w[1, origin_of(j)], preferred_element_type=f32)

        @pl.when(j == 0)
        def _():
            acc[r] = term

        @pl.when(j > 0)
        def _():
            acc[r] += term

    count = jnp.int32(0)
    slots = [jnp.int32(0)] * MOST
    valids = [jnp.int32(0)] * MOST
    column_blocks = tgt.shape[0] // TBLK
    for k in range(cand_ref.shape[1]):
        c = cand_ref[0, k]
        hit = (c // column_blocks == z).astype(jnp.int32)
        for m in range(MOST):
            take_it = hit * (count == m).astype(jnp.int32) == 1
            slots[m] = jnp.where(take_it, lax.rem(c, column_blocks), slots[m])
            valids[m] = jnp.where(take_it, 1, valids[m])
        count = count + hit

    for m in range(MOST):
        col_send[MOST + m:MOST + m + 1] = jnp.full(
            (1, TBLK), jnp.where(valids[m] > 0, slots[m], -1).astype(f32), f32
        )

    def target_unit(p):
        def some(i, carry):
            row = pl.multiple_of(p * 64 + i * 16, 16)
            tiles = [jnp.zeros((16, features), bf16)] * MOST
            for b in range(column_blocks):
                values = tgt[pl.ds(b * TBLK + row, 16), :]
                for m in range(MOST):
                    keep = jnp.full((16, features), (slots[m] == b).astype(f32), f32)
                    tiles[m] = tiles[m] + values * keep.astype(bf16)
            for m in range(MOST):
                tu[pl.ds(m * TBLK + row, 16), :] = unit_rows(tiles[m])
            return carry

        lax.fori_loop(0, 4, some, 0)

    def step(i, carry):
        j = i // NP + 1
        p = lax.rem(i, NP)
        take(j, p)
        pl.when(has_y(j, p))(lambda: y_copy(j, p).start())
        pl.when((p == NP - 1) & (j > 1) & mid)(lambda: take(j, NP))

        @pl.when(i == 1)
        def _():
            to_mate.wait_recv()

        @pl.when(i == 2)
        def _():
            locals_[3].wait()

        @pl.when((i >= 2) & (i < 6))
        def _():
            target_unit(i - 2)

        @pl.when(i == 6)
        def _():
            to_peer.wait_recv()
            to_diag.start()

        @pl.when(i == 7)
        def _():
            to_diag.wait_recv()

        @pl.when(i == 8)
        def _():
            y_wait(1)

        @pl.when(i == 10)
        def _():
            y_wait(2)

        start = jnp.where(i < 2, i, jnp.where(i < 8, i - 4, 2 * i - 12))
        number = jnp.where(i < 2, 1, jnp.where(i < 6, 0, jnp.where(i < 8, 1, 2)))

        def block(k, carry):
            compute((start + k) // 4, lax.rem(start + k, 4))
            return carry

        lax.fori_loop(0, number, block, 0)
        return carry

    lax.fori_loop(0, 3 * NP, step, 0)

    y_wait(3, (0, 1))

    def inner(k, carry):
        hid[3 - k] = hidden_of(3, 3 - k)
        return carry

    lax.fori_loop(0, 1, inner, 0)
    pl.when(end)(lambda: take(3, NP))
    y_wait(3, (2,))

    def quarter(q):
        return pl.ds(pl.multiple_of(q * 64, 64), 64)

    def to_a(q):
        rows = quarter(q)
        return remote(
            part_send.at[0, rows], part_recv.at[0, rows], part_ssem.at[q], part_rsem.at[q],
            src=mate,
        )

    to_c = remote(part_send.at[1], part_recv.at[1], part_ssem.at[4], part_rsem.at[4], src=mate)

    def to_b(k):
        rows = pl.ds(*CHUNKS[k])
        return remote(
            part_send.at[2, rows], part_recv.at[2, rows],
            part_ssem.at[5 + k], part_rsem.at[5 + k], src=peer,
        )

    def to_route(**device):
        return remote(
            part_send.at[2, pl.ds(*CHUNKS[0])], routed, part_ssem.at[5], route_sem.at[0], **device
        )

    hand_on = remote(
        routed, part_recv.at[2, pl.ds(*CHUNKS[0])], route_sem.at[1], part_rsem.at[5], tgt=near_end
    )

    def outer(r, rows):
        return acc[r, rows] + jnp.dot(hid[r, rows], w[1, third], preferred_element_type=f32)

    def for_diag(q, carry):
        rows = quarter(q)
        part_send[0, rows] = outer(3, rows).astype(bf16)
        to_a(q).start()
        return carry

    lax.fori_loop(0, 4, for_diag, 0)

    def for_peer(q, carry):
        rows = quarter(q)
        mine = outer(2, rows)
        to_a(q).wait_recv()
        part_send[2, rows] = (mine + part_recv[0, rows].astype(f32)).astype(bf16)
        for k in range(len(CHUNKS)):
            ready = q == (CHUNKS[k][0] + CHUNKS[k][1] - 1) // 64
            pl.when(ready if k else ready & mid)(to_b(k).start)
        pl.when((q == (CHUNKS[0][0] + CHUNKS[0][1] - 1) // 64) & end)(to_route(src=peer, tgt=inward).start)
        return carry

    hid[2] = hidden_of(3, 2)
    lax.fori_loop(0, 4, for_peer, 0)

    def for_chip(k, carry):
        r = 1 - k
        hid[r] = hidden_of(3, r)
        acc[r] += jnp.dot(hid[r], w[1, third], preferred_element_type=f32)

        @pl.when(k == 0)
        def _():
            part_send[1] = acc[1].astype(bf16)
            to_c.start()

        return carry

    lax.fori_loop(0, 2, for_chip, 0)

    @pl.when(mid)
    def _():
        num_recv[:, 1] = jnp.zeros((2, 32, features // 2), bf16)
        to_route(groups=1 - g).wait_recv()
        hand_on.start()

    members = (
        sid_ref[...] == lax.broadcasted_iota(jnp.int32, (SENT_DEV, 256), 0)
    ).astype(f32)
    counts = jnp.sum(members, axis=1, keepdims=True)
    members = members.astype(bf16)
    grid = grid_ref[...]
    order_key = grid // 128 * 8 + lax.rem(grid, 8)
    reorder = (
        order_key == lax.broadcasted_iota(jnp.int32, (SENT_DEV, SENT_DEV), 0)
    ).astype(f32).astype(bf16)
    own_copies(lambda copy: copy.wait_send())
    to_mate.wait_send()
    to_peer.wait_send()
    to_diag.wait_send()

    def drain(i, carry):
        j = i // NP + 1
        p = lax.rem(i, NP)
        forward, valid = z_copy(j, p)
        pl.when(valid)(forward.wait_send)
        pl.when(has_y(j, p))(lambda: y_copy(j, p).wait_send())
        return carry

    lax.fori_loop(0, 3 * NP, drain, 0)
    for j in (2, 3):
        forward, valid = z_copy(j, NP)
        pl.when(valid & (mid if j == 2 else True))(forward.wait_send)
    to_c.wait_recv()
    acc[0] = tok[0].astype(f32) + (acc[0] + part_recv[1].astype(f32))
    sums = jnp.zeros((SENT_DEV, features), f32)
    for k in (1, 2, 0, 3, 4):
        start, size = CHUNKS[k]
        rows = pl.ds(start, size)
        to_b(k).wait_recv()
        normed = layer_norm(acc[0, rows] + part_recv[2, rows].astype(f32))
        high = normed.astype(bf16)
        low = (normed - high.astype(f32)).astype(bf16)
        here = members[:, start:start + size]
        sums = sums + (
            jnp.dot(here, high, preferred_element_type=f32)
            + jnp.dot(here, low, preferred_element_type=f32)
        )
    unit = unit_rows(sums / counts)
    ordered = jnp.dot(reorder, unit, preferred_element_type=f32)
    for b in range(4):
        su[b] = ordered[b * 8:(b + 1) * 8].astype(bf16)

    me = s * 4 + z

    def unit_copy(to_s, to):
        n = lax.rem(to_s - s + 4, 4) * 4 + lax.rem(to - z + 4, 4)
        return remote(
            su.at[to_s], blk.at[me], unit_ssem.at[n], unit_rsem.at[n], src=to_s, tgt=to
        )

    diag = lax.rem(mate + 2, 4)
    far = jnp.where(z < 2, 3, 0)
    middle = jnp.where(z < 2, 2, 1)
    beside = jnp.where(mid, near_end, inward)

    def unit_copies(method):
        for to in (far, middle, beside, z):
            for to_s in (peer, diag):
                method(unit_copy(to_s, to))
        for to in (far, middle, beside):
            for to_s in (mate, s):
                method(unit_copy(to_s, to))
        method(unit_copy(mate, z))

    def unit_wait(a, b):
        origin = lax.rem(s + 4 - a, 4) * 4 + lax.rem(z + 4 - b, 4)
        remote(
            su.at[0], blk.at[origin], unit_ssem.at[a * 4 + b], unit_rsem.at[a * 4 + b],
            groups=1 - g,
        ).wait_recv()

    unit_copies(lambda copy: copy.start())
    blk[me] = su[s]
    for q in range(4):
        to_a(q).wait_send()
    to_c.wait_send()
    for k in range(len(CHUNKS)):
        to_b(k).wait_send()
    pl.when(mid)(hand_on.wait_send)
    for a in range(4):
        for b in range(4):
            if a or b:
                unit_wait(a, b)

    block = jnp.concatenate([blk[d].astype(f32) for d in range(16)], axis=0).astype(bf16)
    square_eye = lax.broadcasted_iota(jnp.int32, (128, 128), 0) == lax.broadcasted_iota(
        jnp.int32, (128, 128), 1
    )

    def as_row(column):
        return jnp.sum(jnp.where(square_eye, column, 0.0), axis=0, keepdims=True)

    expos = []
    row_part = jnp.zeros((128, 1), f32)
    for m in range(MOST):
        scores = lax.dot_general(
            block, tu[m * TBLK:(m + 1) * TBLK, :], (((1,), (1,)), ((), ())),
            preferred_element_type=f32,
        )
        expo = jnp.exp(SCORE_SCALE * scores) * valids[m].astype(f32)
        expos.append(expo)
        row_part = row_part + jnp.sum(expo, axis=1, keepdims=True)
        col_send[m:m + 1] = jnp.sum(expo, axis=0, keepdims=True)

    def col_copy(a):
        return remote(
            col_send, col_recv.at[a - 1], col_ssem.at[a - 1], col_rsem.at[a - 1],
            src=lax.rem(s + a, 4),
        )

    for a in (2, 1, 3):
        col_copy(a).start()
    row_row = as_row(row_part)
    unit_copies(lambda copy: copy.wait_send())
    for a in range(1, 4):
        col_copy(a).wait_recv()
    mass = jnp.zeros((128, 1), f32)
    mutuals = []
    for m in range(MOST):
        mine = slots[m].astype(f32)
        total = col_send[m:m + 1]
        for a in range(3):
            total = total + jnp.sum(
                jnp.where(col_recv[a, MOST:] == mine, col_recv[a, :MOST], 0.0),
                axis=0, keepdims=True,
            )
        inverse = 1.0 / jnp.where(valids[m] > 0, total, 1.0)
        mutual = expos[m] * (expos[m] * inverse)
        mass = mass + jnp.sum(mutual, axis=1, keepdims=True)
        mutuals.append(mutual.astype(bf16))
    half = features // 2

    def numer_half(f):
        numer = jnp.zeros((128, half), f32)
        for m in range(MOST):
            numer = numer + jnp.dot(
                mutuals[m], tu[m * TBLK:(m + 1) * TBLK, f * half:(f + 1) * half],
                preferred_element_type=f32,
            )
        for t in range(4):
            num_send[f, t] = numer[t * 32:(t + 1) * 32].astype(bf16)

    eights = lax.broadcasted_iota(jnp.int32, (8, 128), 0)
    stat_send[...] = jnp.where(
        eights == 0, as_row(mass), jnp.where(eights == 1, row_row, 0.0)
    )
    def owner(k):
        return (far, middle, beside)[k]

    def stat_copy(k):
        b = lax.rem(owner(k) - z + 4, 4) - 1
        return remote(stat_send, stat_recv.at[b], stat_ssem.at[k], stat_rsem.at[b], tgt=owner(k))

    def num_copy(f, k):
        b = lax.rem(owner(k) - z + 4, 4) - 1
        return remote(
            num_send.at[f, owner(k)], num_recv.at[f, b], num_ssem.at[f, k], num_rsem.at[f, b],
            tgt=owner(k),
        )

    def to_relay(f, **device):
        return remote(
            num_send.at[f, middle], num_relay.at[f], num_ssem.at[f, 1], relay_rsem.at[f], **device
        )

    def relayed(f):
        b = lax.rem(across - z + 4, 4) - 1
        return remote(
            num_relay.at[f], num_recv.at[f, b], num_ssem.at[f, 1], num_rsem.at[f, b], tgt=across
        )

    for f in range(2):
        numer_half(f)
        pl.when(end)(to_relay(f, tgt=inward).start)
        num_copy(f, 0).start()
        num_copy(f, 2).start()
        if f == 0:
            for k in range(3):
                stat_copy(k).start()

    @pl.when(mid)
    def _():
        for f in range(2):
            to_relay(f, groups=1 - g).wait_recv()
            num_relay[f] = (num_relay[f].astype(f32) + num_send[f, across].astype(f32)).astype(bf16)
            relayed(f).start()

    def num_wait(f, b):
        remote(
            num_send.at[0, 0], num_recv.at[f, b], num_ssem.at[0, 0], num_rsem.at[f, b],
            groups=1 - g,
        ).wait_recv()

    for a in range(1, 4):
        col_copy(a).wait_send()

    stat = stat_send[...]
    for b in range(3):
        remote(
            stat_send, stat_recv.at[b], stat_ssem.at[0], stat_rsem.at[b], groups=1 - g
        ).wait_recv()
        stat = stat + stat_recv[b]
    logs = jnp.log(stat[0:1] / stat[1:2])
    chosen = (
        lax.broadcasted_iota(jnp.int32, (128, 32), 0)
        == z * 32 + lax.broadcasted_iota(jnp.int32, (128, 32), 1)
    )
    log_ref[...] = jnp.sum(
        jnp.where(chosen, jnp.sum(jnp.where(square_eye, logs, 0.0), axis=1, keepdims=True), 0.0),
        axis=0, keepdims=True,
    )
    parts = []
    for f in range(2):
        part = num_send[f, z].astype(f32)
        for b in (2, 1, 0):
            if b == 1:
                pl.when(end)(lambda f=f: num_wait(f, 1))
                part = part + jnp.where(end, num_recv[f, 1].astype(f32), 0.0)
            else:
                num_wait(f, b)
                part = part + num_recv[f, b].astype(f32)
        parts.append(part)
    square = (
        jnp.sum(parts[0] * parts[0], axis=-1, keepdims=True)
        + jnp.sum(parts[1] * parts[1], axis=-1, keepdims=True)
    ) / features
    scale = lax.rsqrt(square + 1e-06)
    for f in range(2):
        matched_ref[:, f * half:(f + 1) * half] = (parts[f] * scale).astype(bf16)

    for k in range(3):
        stat_copy(k).wait_send()
    for f in range(2):
        num_copy(f, 0).wait_send()
        num_copy(f, 2).wait_send()
        pl.when(end)(to_relay(f, tgt=inward).wait_send)
        pl.when(mid)(relayed(f).wait_send)


def fused(tokens, sentence_ids, inner_weight, outer_weight, grid_rows, candidates, targets):
    f32, bf16 = jnp.float32, jnp.bfloat16
    features = tokens.shape[1]
    dma = pltpu.SemaphoreType.DMA
    any_spec = pl.BlockSpec(memory_space=pltpu.HBM)
    vmem = pl.BlockSpec(memory_space=pltpu.VMEM)
    matched, logs = pl.pallas_call(
        fused_kernel,
        out_shape=(pltpu.VMEM((SENT_DEV, features), bf16), pltpu.VMEM((1, SENT_DEV), f32)),
        in_specs=[
            any_spec,
        ] * 7,
        out_specs=(vmem, vmem),
        scratch_shapes=[
            pltpu.VMEM((1, 256), jnp.int32),
            pltpu.VMEM((1, SENT_DEV), jnp.int32),
            pltpu.SMEM(candidates.shape, jnp.int32),
            pltpu.VMEM((4, 256, features), bf16),
            pltpu.VMEM((2, 4, 256, features), bf16),
            pltpu.VMEM((4, 256, features), f32),
            pltpu.VMEM((4, 256, 256), bf16),
            pltpu.VMEM(targets.shape, bf16),
            pltpu.VMEM((MOST * TBLK, features), bf16),
            pltpu.VMEM((3, 256, features), bf16),
            pltpu.VMEM((3, 256, features), bf16),
            pltpu.VMEM((CHUNKS[0][1], features), bf16),
            pltpu.VMEM((4, 8, features), bf16),
            pltpu.VMEM((16, 8, features), bf16),
            pltpu.VMEM((2, 4, 32, features // 2), bf16),
            pltpu.VMEM((2, 3, 32, features // 2), bf16),
            pltpu.VMEM((2, 32, features // 2), bf16),
            pltpu.VMEM((8, 128), f32),
            pltpu.VMEM((3, 8, 128), f32),
            pltpu.VMEM((2 * MOST, TBLK), f32),
            pltpu.VMEM((3, 2 * MOST, TBLK), f32),
            dma((7,)),
            dma((2, NP + 1)),
            dma((3, NP + 1)),
            dma((3, NP)),
            dma((4, NP + 1)),
            dma((4, NP)),
            dma((3,)),
            dma((4,)),
            dma((5 + len(CHUNKS),)),
            dma((5 + len(CHUNKS),)),
            dma((2,)),
            dma((16,)),
            dma((16,)),
            dma((4,)),
            dma((3,)),
            dma((3,)),
            dma((2, 3)),
            dma((2, 3)),
            dma((2,)),
            dma((3,)),
            dma((3,)),
        ],
        compiler_params=pltpu.CompilerParams(
            collective_id=0, has_side_effects=True, vmem_limit_bytes=64 * 1024 * 1024 - 163840
        ),
    )(
        tokens, sentence_ids, inner_weight, outer_weight,
        grid_rows.reshape(1, SENT_DEV), candidates, targets,
    )
    return matched, logs.reshape(SENT_DEV)


def solution(mesh):
    in_specs = (
        P(("groups", "src", "tgt"), None),
        P(("groups", "src", "tgt"), None),
        P(("src", "tgt"), None),
        P(("src", "tgt"), None),
        P(("groups", "src", "tgt")),
        P(("groups", "src"), None),
        P(("groups", "tgt"), None),
    )
    out_specs = (P(("groups", "src", "tgt"), None), P(("groups", "src", "tgt")))
    sizes = tuple(mesh.shape[name] for name in ("groups", "src", "tgt"))
    body = fused if sizes == (2, 4, 4) else on_device
    return jax.shard_map(
        body, mesh=mesh, in_specs=in_specs, out_specs=out_specs, check_vma=False
    )
```

```python
import math

import jax
import jax.numpy as jnp
from jax import lax
from jax.experimental import pallas as pl
from jax.experimental.pallas import tpu as pltpu
from jax.sharding import PartitionSpec as P

SENT_DEV = 32
TBLK = 256
MOST = 4


SCORE_SCALE = 32.0


def unit_rows(values):
    floats = values.astype(jnp.float32)
    square = jnp.mean(floats * floats, axis=-1, keepdims=True)
    return (floats * lax.rsqrt(square + 1e-06) * (1.0 / math.sqrt(values.shape[-1]))).astype(
        jnp.bfloat16
    )


def inner_units(rows, inner):
    product = lax.dot_general(
        rows, inner, (((1,), (1,)), ((), ())), preferred_element_type=jnp.float32
    )
    return jax.nn.gelu(product, approximate=False).astype(jnp.bfloat16)


def layer_norm(summed):
    center = jnp.mean(summed, axis=-1, keepdims=True)
    spread = jnp.mean((summed - center) * (summed - center), axis=-1, keepdims=True)
    return (summed - center) * lax.rsqrt(spread + 1e-05)


def on_device(tokens, sentence_ids, inner_weight, outer_weight, grid_rows, candidates, targets):
    features = tokens.shape[1]
    projected = jnp.dot(
        inner_units(tokens, lax.all_gather(inner_weight, ("src", "tgt"), axis=0, tiled=True)),
        lax.all_gather(outer_weight, ("src", "tgt"), axis=0, tiled=True),
        preferred_element_type=jnp.float32,
    )
    normed = layer_norm(tokens.astype(jnp.float32) + projected)
    members = (sentence_ids[0][None, :] == jnp.arange(SENT_DEV, dtype=jnp.int32)[:, None]).astype(
        jnp.float32
    )
    sums = jnp.dot(members, normed, precision=lax.Precision.HIGHEST)
    unit = unit_rows(sums / jnp.sum(members, axis=1, keepdims=True))
    src_count = lax.axis_size("src")
    tgt_count = lax.axis_size("tgt")
    per_block = SENT_DEV // src_count
    block_rows = tgt_count * SENT_DEV
    order_key = grid_rows // block_rows * per_block + grid_rows % per_block
    reorder = (order_key[None, :] == jnp.arange(SENT_DEV, dtype=jnp.int32)[:, None]).astype(
        jnp.bfloat16
    )
    sorted_units = jnp.dot(reorder, unit, preferred_element_type=jnp.float32).astype(jnp.bfloat16)
    relayed = lax.all_to_all(
        sorted_units.reshape(src_count, per_block, features),
        "src",
        split_axis=0,
        concat_axis=0,
        tiled=True,
    )
    block = lax.all_gather(relayed, "tgt", axis=1, tiled=True).reshape(block_rows, features)
    column_index = lax.axis_index("tgt")
    column_blocks = targets.shape[0] // TBLK
    cand_row = candidates[0]
    listed = (cand_row // column_blocks == column_index).astype(jnp.int32)
    places = jnp.arange(cand_row.shape[0], dtype=jnp.int32)
    ranks = jnp.sum(listed[None, :] * (places[None, :] <= places[:, None]), axis=1) - 1
    chosen = (
        (listed[None, :] == 1) & (ranks[None, :] == jnp.arange(MOST, dtype=jnp.int32)[:, None])
    ).astype(jnp.int32)
    slot_block = jnp.sum(chosen * (cand_row % column_blocks)[None, :], axis=1)
    valid = jnp.sum(chosen, axis=1).astype(jnp.float32)
    tiles = jnp.stack(
        [lax.dynamic_slice_in_dim(targets, slot_block[m] * TBLK, TBLK) for m in range(MOST)]
    )
    target_units = unit_rows(tiles).reshape(MOST * TBLK, features)
    scores = lax.dot_general(
        block, target_units, (((1,), (1,)), ((), ())), preferred_element_type=jnp.float32
    )
    column_valid = jnp.repeat(valid, TBLK)
    expo = jnp.exp(SCORE_SCALE * scores) * column_valid[None, :]
    row_part = jnp.sum(expo, axis=1)
    column_part = jnp.sum(expo, axis=0).reshape(MOST, TBLK)
    picker = (slot_block[:, None] == jnp.arange(column_blocks, dtype=jnp.int32)[None, :]).astype(
        jnp.float32
    )
    column_local = jnp.dot(
        (picker * valid[:, None]).T, column_part, precision=lax.Precision.HIGHEST
    )
    column_total = lax.psum(column_local, "src")
    picked = jnp.dot(picker, column_total, precision=lax.Precision.HIGHEST)
    divisor = jnp.where(valid[:, None] > 0, picked, 1.0).reshape(-1)
    mutual = expo * (expo / divisor[None, :])
    numer = jnp.dot(mutual.astype(jnp.bfloat16), target_units, preferred_element_type=jnp.float32)
    mass_part = jnp.sum(mutual, axis=1)
    row_total = lax.psum(row_part, "tgt")
    numer_rows, mass_rows = (
        lax.psum_scatter(numer, "tgt", scatter_dimension=0, tiled=True),
        lax.psum_scatter(mass_part, "tgt", scatter_dimension=0, tiled=True),
    )
    total_rows = lax.dynamic_slice_in_dim(row_total, column_index * SENT_DEV, SENT_DEV)
    square = jnp.mean(numer_rows * numer_rows, axis=-1, keepdims=True)
    matched = (numer_rows * lax.rsqrt(square + 1e-06)).astype(jnp.bfloat16)
    log_mass = jnp.log(mass_rows / total_rows)
    return (matched, log_mass)


PIECES = ((0, 0), (0, 64), (1, 0), (1, 64))
PROWS = 64
CHUNKS = ((64, 64), (0, 64), (128, 64), (192, 32), (224, 32))
NP = len(PIECES)
HALF = 0.7071067811865476


def remote(source, target, send, recv, /, **device):
    return pltpu.make_async_remote_copy(
        src_ref=source,
        dst_ref=target,
        send_sem=send,
        recv_sem=recv,
        device_id=device,
        device_id_type=pl.DeviceIdType.MESH,
    )


def gelu(product):
    return (0.5 * product * (1.0 + lax.erf(product * HALF))).astype(jnp.bfloat16)


def fused_kernel(
    tok_any, sid_any, win_any, wout_any, grid_any, cand_any, tgt_any,
    matched_ref, log_ref,
    sid_ref, grid_ref, cand_ref, tok, w, acc, hid, tgt, tu, part_send, part_recv, routed, su, blk,
    num_send, num_recv, num_relay, stat_send, stat_recv, col_send, col_recv,
    local_sem, own_send, fwd_send, y_send, z_recv, y_recv, tok_send, tok_recv,
    part_ssem, part_rsem, route_sem, unit_ssem, unit_rsem, relay_ssem, col_ssem, col_rsem,
    num_ssem, num_rsem, relay_rsem, stat_ssem, stat_rsem,
):
    g = lax.axis_index("groups")
    s = lax.axis_index("src")
    z = lax.axis_index("tgt")
    f32, bf16 = jnp.float32, jnp.bfloat16
    features = tok.shape[2]
    mate = s + 1 - 2 * lax.rem(s, 2)
    peer = lax.rem(s + 2, 4)
    mid = (z == 1) | (z == 2)
    end = (z == 0) | (z == 3)
    across = 3 - z
    near_end = jnp.where(z < 2, 0, 3)
    inward = jnp.where(z == 0, 1, 2)

    locals_ = [
        pltpu.make_async_copy(tok_any, tok.at[0], local_sem.at[0]),
        pltpu.make_async_copy(win_any, w.at[0, z], local_sem.at[1]),
        pltpu.make_async_copy(wout_any, w.at[1, z], local_sem.at[2]),
        pltpu.make_async_copy(tgt_any, tgt, local_sem.at[3]),
        pltpu.make_async_copy(sid_any, sid_ref, local_sem.at[4]),
        pltpu.make_async_copy(grid_any, grid_ref, local_sem.at[5]),
        pltpu.make_async_copy(cand_any, cand_ref, local_sem.at[6]),
    ]

    barrier = pltpu.get_barrier_semaphore()

    def greet(**device):
        pl.semaphore_signal(
            barrier, inc=1, device_id=device, device_id_type=pl.DeviceIdType.MESH
        )

    pl.when(z > 0)(lambda: greet(tgt=z - 1))
    pl.when(z < 3)(lambda: greet(tgt=z + 1))
    greet(groups=1 - g)
    greet(src=mate)
    greet(src=peer)
    for copy in locals_[:3]:
        copy.start()
    pl.semaphore_wait(barrier, 4 + mid.astype(jnp.int32))

    def place(u, half):
        if isinstance(u, int):
            matrix, row = PIECES[u]
        else:
            matrix, row = u // 2, lax.rem(u, 2) * PROWS
        return matrix, pl.multiple_of(half * 128 + row, PROWS)

    def piece(origin, u, half):
        matrix, row = place(u, half)
        return w.at[matrix, origin, pl.ds(row, PROWS)]

    def unit_of(origin, u):
        if isinstance(u, int) and u == NP:
            return piece(origin, NP - 1, 1 - g)
        return piece(origin, u, g)

    def own_copy(direction, u):
        half = 1 - g if u == NP else g
        matrix, row = place(min(u, NP - 1), half)
        return remote(
            (win_any, wout_any)[matrix].at[pl.ds(row, PROWS)], unit_of(z, u),
            own_send.at[direction, u], z_recv.at[z, u],
            tgt=z + 1 if direction == 0 else z - 1,
        )

    def own_copies(method):
        for u in range(NP + 1):
            pl.when(z < 3 if u < NP else z == 0)(lambda u=u: method(own_copy(0, u)))
            pl.when(z > 0 if u < NP else z == 3)(lambda u=u: method(own_copy(1, u)))

    own_copies(lambda copy: copy.start())

    to_mate = remote(tok_any, tok.at[1], tok_send.at[0], tok_recv.at[1], src=mate)
    to_peer = remote(tok_any, tok.at[2], tok_send.at[1], tok_recv.at[2], src=peer)
    to_diag = remote(tok.at[2], tok.at[3], tok_send.at[2], tok_recv.at[3], src=mate)
    to_mate.start()
    to_peer.start()
    for copy in locals_[3:]:
        copy.start()

    first = 1 + lax.rem(z, 2)
    third = jnp.where(z < 2, 3, 0)
    second = 6 - z - first - third

    def origin_of(j):
        return jnp.where(j == 0, z, jnp.where(j == 1, first, jnp.where(j == 2, second, third)))

    def z_copy(j, u):
        origin = origin_of(j)
        ref = unit_of(origin, u)
        from_left = origin < z
        following = jnp.where(from_left, z + 1, z - 1)
        valid = jnp.where(from_left, (z < 3).astype(jnp.int32), (z > 0).astype(jnp.int32)) == 1
        return (
            remote(ref, ref, fwd_send.at[j - 1, u], z_recv.at[origin, u], tgt=following),
            valid,
        )

    def y_copy(j, u):
        origin = origin_of(j)
        ref = piece(origin, u, g)
        return remote(ref, ref, y_send.at[j - 1, u], y_recv.at[origin, u], groups=1 - g)

    def has_y(j, u):
        return (u < NP - 1) | (j == 1) | ((j == 2) & end)

    def y_wait(j, us=range(NP)):
        origin = origin_of(j)
        for u in us:
            ref = piece(origin, u, 1 - g)

            def wait(u=u, ref=ref):
                remote(ref, ref, y_send.at[0, u], y_recv.at[origin, u], groups=1 - g).wait_recv()

            if j == 2 and u == NP - 1:
                pl.when(end)(wait)
            elif j < 3 or u < NP - 1:
                wait()

    def take(j, u):
        ref = unit_of(origin_of(j), u)
        remote(
            ref, ref, own_send.at[0, u], z_recv.at[origin_of(j), u], groups=1 - g
        ).wait_recv()
        forward, valid = z_copy(j, u)
        pl.when(valid)(forward.start)

    for copy in locals_[:3] + locals_[4:]:
        copy.wait()

    def hidden_of(j, r):
        product = lax.dot_general(
            tok[r], w[0, origin_of(j)], (((1,), (1,)), ((), ())), preferred_element_type=f32
        )
        return gelu(product)

    def compute(j, r):
        term = jnp.dot(hidden_of(j, r), w[1, origin_of(j)], preferred_element_type=f32)

        @pl.when(j == 0)
        def _():
            acc[r] = term

        @pl.when(j > 0)
        def _():
            acc[r] += term

    count = jnp.int32(0)
    slots = [jnp.int32(0)] * MOST
    valids = [jnp.int32(0)] * MOST
    column_blocks = tgt.shape[0] // TBLK
    for k in range(cand_ref.shape[1]):
        c = cand_ref[0, k]
        hit = (c // column_blocks == z).astype(jnp.int32)
        for m in range(MOST):
            take_it = hit * (count == m).astype(jnp.int32) == 1
            slots[m] = jnp.where(take_it, lax.rem(c, column_blocks), slots[m])
            valids[m] = jnp.where(take_it, 1, valids[m])
        count = count + hit

    for m in range(MOST):
        col_send[MOST + m:MOST + m + 1] = jnp.full(
            (1, TBLK), jnp.where(valids[m] > 0, slots[m], -1).astype(f32), f32
        )

    def target_unit(p):
        def some(i, carry):
            row = pl.multiple_of(p * 64 + i * 16, 16)
            tiles = [jnp.zeros((16, features), bf16)] * MOST
            for b in range(column_blocks):
                values = tgt[pl.ds(b * TBLK + row, 16), :]
                for m in range(MOST):
                    keep = jnp.full((16, features), (slots[m] == b).astype(f32), f32)
                    tiles[m] = tiles[m] + values * keep.astype(bf16)
            for m in range(MOST):
                tu[pl.ds(m * TBLK + row, 16), :] = unit_rows(tiles[m])
            return carry

        lax.fori_loop(0, 4, some, 0)

    def step(i, carry):
        j = i // NP + 1
        p = lax.rem(i, NP)
        take(j, p)
        pl.when(has_y(j, p))(lambda: y_copy(j, p).start())
        pl.when((p == NP - 1) & (j > 1) & mid)(lambda: take(j, NP))

        @pl.when(i == 1)
        def _():
            to_mate.wait_recv()

        @pl.when(i == 2)
        def _():
            locals_[3].wait()

        @pl.when((i >= 2) & (i < 6))
        def _():
            target_unit(i - 2)

        @pl.when(i == 6)
        def _():
            to_peer.wait_recv()
            to_diag.start()

        @pl.when(i == 7)
        def _():
            to_diag.wait_recv()

        @pl.when(i == 8)
        def _():
            y_wait(1)

        @pl.when(i == 10)
        def _():
            y_wait(2)

        start = jnp.where(i < 2, i, jnp.where(i < 8, i - 4, 2 * i - 12))
        number = jnp.where(i < 2, 1, jnp.where(i < 6, 0, jnp.where(i < 8, 1, 2)))

        def block(k, carry):
            compute((start + k) // 4, lax.rem(start + k, 4))
            return carry

        lax.fori_loop(0, number, block, 0)
        return carry

    lax.fori_loop(0, 3 * NP, step, 0)

    y_wait(3, (0, 1))

    def inner(k, carry):
        hid[3 - k] = hidden_of(3, 3 - k)
        return carry

    lax.fori_loop(0, 1, inner, 0)
    pl.when(end)(lambda: take(3, NP))
    y_wait(3, (2,))

    def quarter(q):
        return pl.ds(pl.multiple_of(q * 64, 64), 64)

    def to_a(q):
        rows = quarter(q)
        return remote(
            part_send.at[0, rows], part_recv.at[0, rows], part_ssem.at[q], part_rsem.at[q],
            src=mate,
        )

    to_c = remote(part_send.at[1], part_recv.at[1], part_ssem.at[4], part_rsem.at[4], src=mate)

    def to_b(k):
        rows = pl.ds(*CHUNKS[k])
        return remote(
            part_send.at[2, rows], part_recv.at[2, rows],
            part_ssem.at[5 + k], part_rsem.at[5 + k], src=peer,
        )

    def to_route(**device):
        return remote(
            part_send.at[2, pl.ds(*CHUNKS[0])], routed, part_ssem.at[5], route_sem.at[0], **device
        )

    hand_on = remote(
        routed, part_recv.at[2, pl.ds(*CHUNKS[0])], route_sem.at[1], part_rsem.at[5], tgt=near_end
    )

    def outer(r, rows):
        return acc[r, rows] + jnp.dot(hid[r, rows], w[1, third], preferred_element_type=f32)

    def for_diag(q, carry):
        rows = quarter(q)
        part_send[0, rows] = outer(3, rows).astype(bf16)
        to_a(q).start()
        return carry

    lax.fori_loop(0, 4, for_diag, 0)

    def for_peer(q, carry):
        rows = quarter(q)
        mine = outer(2, rows)
        to_a(q).wait_recv()
        part_send[2, rows] = (mine + part_recv[0, rows].astype(f32)).astype(bf16)
        for k in range(len(CHUNKS)):
            ready = q == (CHUNKS[k][0] + CHUNKS[k][1] - 1) // 64
            pl.when(ready if k else ready & mid)(to_b(k).start)
        pl.when((q == (CHUNKS[0][0] + CHUNKS[0][1] - 1) // 64) & end)(to_route(src=peer, tgt=inward).start)
        return carry

    hid[2] = hidden_of(3, 2)
    lax.fori_loop(0, 4, for_peer, 0)

    def for_chip(k, carry):
        r = 1 - k
        hid[r] = hidden_of(3, r)
        acc[r] += jnp.dot(hid[r], w[1, third], preferred_element_type=f32)

        @pl.when(k == 0)
        def _():
            part_send[1] = acc[1].astype(bf16)
            to_c.start()

        return carry

    lax.fori_loop(0, 2, for_chip, 0)

    @pl.when(mid)
    def _():
        num_recv[:, 1] = jnp.zeros((2, 32, features // 2), bf16)
        to_route(groups=1 - g).wait_recv()
        hand_on.start()

    members = (
        sid_ref[...] == lax.broadcasted_iota(jnp.int32, (SENT_DEV, 256), 0)
    ).astype(f32)
    counts = jnp.sum(members, axis=1, keepdims=True)
    members = members.astype(bf16)
    grid = grid_ref[...]
    order_key = grid // 128 * 8 + lax.rem(grid, 8)
    reorder = (
        order_key == lax.broadcasted_iota(jnp.int32, (SENT_DEV, SENT_DEV), 0)
    ).astype(f32).astype(bf16)
    own_copies(lambda copy: copy.wait_send())
    to_mate.wait_send()
    to_peer.wait_send()
    to_diag.wait_send()

    def drain(i, carry):
        j = i // NP + 1
        p = lax.rem(i, NP)
        forward, valid = z_copy(j, p)
        pl.when(valid)(forward.wait_send)
        pl.when(has_y(j, p))(lambda: y_copy(j, p).wait_send())
        return carry

    lax.fori_loop(0, 3 * NP, drain, 0)
    for j in (2, 3):
        forward, valid = z_copy(j, NP)
        pl.when(valid & (mid if j == 2 else True))(forward.wait_send)
    to_c.wait_recv()
    acc[0] = tok[0].astype(f32) + (acc[0] + part_recv[1].astype(f32))
    sums = jnp.zeros((SENT_DEV, features), f32)
    for k in (1, 2, 0, 3, 4):
        start, size = CHUNKS[k]
        rows = pl.ds(start, size)
        to_b(k).wait_recv()
        normed = layer_norm(acc[0, rows] + part_recv[2, rows].astype(f32))
        high = normed.astype(bf16)
        low = (normed - high.astype(f32)).astype(bf16)
        here = members[:, start:start + size]
        sums = sums + (
            jnp.dot(here, high, preferred_element_type=f32)
            + jnp.dot(here, low, preferred_element_type=f32)
        )
    unit = unit_rows(sums / counts)
    ordered = jnp.dot(reorder, unit, preferred_element_type=f32)
    for b in range(4):
        su[b] = ordered[b * 8:(b + 1) * 8].astype(bf16)

    me = s * 4 + z

    def unit_copy(to_s, to):
        n = lax.rem(to_s - s + 4, 4) * 4 + lax.rem(to - z + 4, 4)
        return remote(
            su.at[to_s], blk.at[me], unit_ssem.at[n], unit_rsem.at[n], src=to_s, tgt=to
        )

    diag = lax.rem(mate + 2, 4)
    far = jnp.where(z < 2, 3, 0)
    middle = jnp.where(z < 2, 2, 1)
    beside = jnp.where(mid, near_end, inward)

    def unit_copies(method):
        for to in (far, middle, beside, z):
            for to_s in (peer, diag):
                method(unit_copy(to_s, to))
        for to in (far, middle, beside):
            for to_s in (mate, s):
                method(unit_copy(to_s, to))
        method(unit_copy(mate, z))

    def unit_wait(a, b):
        origin = lax.rem(s + 4 - a, 4) * 4 + lax.rem(z + 4 - b, 4)
        remote(
            su.at[0], blk.at[origin], unit_ssem.at[a * 4 + b], unit_rsem.at[a * 4 + b],
            groups=1 - g,
        ).wait_recv()

    unit_copies(lambda copy: copy.start())
    blk[me] = su[s]
    for q in range(4):
        to_a(q).wait_send()
    to_c.wait_send()
    for k in range(len(CHUNKS)):
        to_b(k).wait_send()
    pl.when(mid)(hand_on.wait_send)
    for a in range(4):
        for b in range(4):
            if a or b:
                unit_wait(a, b)

    block = jnp.concatenate([blk[d].astype(f32) for d in range(16)], axis=0).astype(bf16)
    square_eye = lax.broadcasted_iota(jnp.int32, (128, 128), 0) == lax.broadcasted_iota(
        jnp.int32, (128, 128), 1
    )

    def as_row(column):
        return jnp.sum(jnp.where(square_eye, column, 0.0), axis=0, keepdims=True)

    expos = []
    row_lanes = jnp.zeros((128, TBLK), f32)
    for m in range(MOST):
        scores = lax.dot_general(
            block, tu[m * TBLK:(m + 1) * TBLK, :], (((1,), (1,)), ((), ())),
            preferred_element_type=f32,
        )
        expo = jnp.exp(SCORE_SCALE * scores) * valids[m].astype(f32)
        expos.append(expo)
        row_lanes = row_lanes + expo
        col_send[m:m + 1] = jnp.sum(expo, axis=0, keepdims=True)

    def col_copy(a):
        return remote(
            col_send, col_recv.at[a - 1], col_ssem.at[a - 1], col_rsem.at[a - 1],
            src=lax.rem(s + a, 4),
        )

    for a in (2, 1, 3):
        col_copy(a).start()
    row_row = as_row(jnp.sum(row_lanes, axis=1, keepdims=True))
    unit_copies(lambda copy: copy.wait_send())
    for a in range(1, 4):
        col_copy(a).wait_recv()
    mass_lanes = jnp.zeros((128, TBLK), f32)
    mutuals = []
    for m in range(MOST):
        mine = slots[m].astype(f32)
        total = col_send[m:m + 1]
        for a in range(3):
            total = total + jnp.sum(
                jnp.where(col_recv[a, MOST:] == mine, col_recv[a, :MOST], 0.0),
                axis=0, keepdims=True,
            )
        inverse = 1.0 / jnp.where(valids[m] > 0, total, 1.0)
        mutual = expos[m] * (expos[m] * inverse)
        mass_lanes = mass_lanes + mutual
        mutuals.append(mutual.astype(bf16))
    half = features // 2

    def numer_half(f):
        numer = jnp.zeros((128, half), f32)
        for m in range(MOST):
            numer = numer + jnp.dot(
                mutuals[m], tu[m * TBLK:(m + 1) * TBLK, f * half:(f + 1) * half],
                preferred_element_type=f32,
            )
        for t in range(4):
            num_send[f, t] = numer[t * 32:(t + 1) * 32].astype(bf16)

    def owner(k):
        return (far, middle, beside)[k]

    def stat_copy(k):
        b = lax.rem(owner(k) - z + 4, 4) - 1
        return remote(stat_send, stat_recv.at[b], stat_ssem.at[k], stat_rsem.at[b], tgt=owner(k))

    def num_copy(f, k):
        b = lax.rem(owner(k) - z + 4, 4) - 1
        return remote(
            num_send.at[f, owner(k)], num_recv.at[f, b], num_ssem.at[f, k], num_rsem.at[f, b],
            tgt=owner(k),
        )

    def to_relay(f, **device):
        return remote(
            num_send.at[f, middle], num_relay.at[f], num_ssem.at[f, 1], relay_rsem.at[f], **device
        )

    def relayed(f):
        b = lax.rem(across - z + 4, 4) - 1
        return remote(
            num_relay.at[f], num_recv.at[f, b], num_ssem.at[f, 1], num_rsem.at[f, b], tgt=across
        )

    for f in range(2):
        numer_half(f)
        pl.when(end)(to_relay(f, tgt=inward).start)
        num_copy(f, 0).start()
        num_copy(f, 2).start()
        if f == 0:
            mass = jnp.sum(mass_lanes, axis=1, keepdims=True)
            eights = lax.broadcasted_iota(jnp.int32, (8, 128), 0)
            stat_send[...] = jnp.where(
                eights == 0, as_row(mass), jnp.where(eights == 1, row_row, 0.0)
            )
            for k in range(3):
                stat_copy(k).start()

    @pl.when(mid)
    def _():
        for f in range(2):
            to_relay(f, groups=1 - g).wait_recv()
            num_relay[f] = (num_relay[f].astype(f32) + num_send[f, across].astype(f32)).astype(bf16)
            relayed(f).start()

    def num_wait(f, b):
        remote(
            num_send.at[0, 0], num_recv.at[f, b], num_ssem.at[0, 0], num_rsem.at[f, b],
            groups=1 - g,
        ).wait_recv()

    for a in range(1, 4):
        col_copy(a).wait_send()

    stat = stat_send[...]
    for b in range(3):
        remote(
            stat_send, stat_recv.at[b], stat_ssem.at[0], stat_rsem.at[b], groups=1 - g
        ).wait_recv()
        stat = stat + stat_recv[b]
    logs = jnp.log(stat[0:1] / stat[1:2])
    chosen = (
        lax.broadcasted_iota(jnp.int32, (128, 32), 0)
        == z * 32 + lax.broadcasted_iota(jnp.int32, (128, 32), 1)
    )
    log_ref[...] = jnp.sum(
        jnp.where(chosen, jnp.sum(jnp.where(square_eye, logs, 0.0), axis=1, keepdims=True), 0.0),
        axis=0, keepdims=True,
    )
    parts = []
    for f in range(2):
        part = num_send[f, z].astype(f32)
        for b in (2, 1, 0):
            if b == 1:
                pl.when(end)(lambda f=f: num_wait(f, 1))
                part = part + jnp.where(end, num_recv[f, 1].astype(f32), 0.0)
            else:
                num_wait(f, b)
                part = part + num_recv[f, b].astype(f32)
        parts.append(part)
    square = (
        jnp.sum(parts[0] * parts[0], axis=-1, keepdims=True)
        + jnp.sum(parts[1] * parts[1], axis=-1, keepdims=True)
    ) / features
    scale = lax.rsqrt(square + 1e-06)
    for f in range(2):
        matched_ref[:, f * half:(f + 1) * half] = (parts[f] * scale).astype(bf16)

    for k in range(3):
        stat_copy(k).wait_send()
    for f in range(2):
        num_copy(f, 0).wait_send()
        num_copy(f, 2).wait_send()
        pl.when(end)(to_relay(f, tgt=inward).wait_send)
        pl.when(mid)(relayed(f).wait_send)


def fused(tokens, sentence_ids, inner_weight, outer_weight, grid_rows, candidates, targets):
    f32, bf16 = jnp.float32, jnp.bfloat16
    features = tokens.shape[1]
    dma = pltpu.SemaphoreType.DMA
    any_spec = pl.BlockSpec(memory_space=pltpu.HBM)
    vmem = pl.BlockSpec(memory_space=pltpu.VMEM)
    matched, logs = pl.pallas_call(
        fused_kernel,
        out_shape=(pltpu.VMEM((SENT_DEV, features), bf16), pltpu.VMEM((1, SENT_DEV), f32)),
        in_specs=[
            any_spec,
        ] * 7,
        out_specs=(vmem, vmem),
        scratch_shapes=[
            pltpu.VMEM((1, 256), jnp.int32),
            pltpu.VMEM((1, SENT_DEV), jnp.int32),
            pltpu.SMEM(candidates.shape, jnp.int32),
            pltpu.VMEM((4, 256, features), bf16),
            pltpu.VMEM((2, 4, 256, features), bf16),
            pltpu.VMEM((4, 256, features), f32),
            pltpu.VMEM((4, 256, 256), bf16),
            pltpu.VMEM(targets.shape, bf16),
            pltpu.VMEM((MOST * TBLK, features), bf16),
            pltpu.VMEM((3, 256, features), bf16),
            pltpu.VMEM((3, 256, features), bf16),
            pltpu.VMEM((CHUNKS[0][1], features), bf16),
            pltpu.VMEM((4, 8, features), bf16),
            pltpu.VMEM((16, 8, features), bf16),
            pltpu.VMEM((2, 4, 32, features // 2), bf16),
            pltpu.VMEM((2, 3, 32, features // 2), bf16),
            pltpu.VMEM((2, 32, features // 2), bf16),
            pltpu.VMEM((8, 128), f32),
            pltpu.VMEM((3, 8, 128), f32),
            pltpu.VMEM((2 * MOST, TBLK), f32),
            pltpu.VMEM((3, 2 * MOST, TBLK), f32),
            dma((7,)),
            dma((2, NP + 1)),
            dma((3, NP + 1)),
            dma((3, NP)),
            dma((4, NP + 1)),
            dma((4, NP)),
            dma((3,)),
            dma((4,)),
            dma((5 + len(CHUNKS),)),
            dma((5 + len(CHUNKS),)),
            dma((2,)),
            dma((16,)),
            dma((16,)),
            dma((4,)),
            dma((3,)),
            dma((3,)),
            dma((2, 3)),
            dma((2, 3)),
            dma((2,)),
            dma((3,)),
            dma((3,)),
        ],
        compiler_params=pltpu.CompilerParams(
            collective_id=0, has_side_effects=True, vmem_limit_bytes=64 * 1024 * 1024 - 163840
        ),
    )(
        tokens, sentence_ids, inner_weight, outer_weight,
        grid_rows.reshape(1, SENT_DEV), candidates, targets,
    )
    return matched, logs.reshape(SENT_DEV)


def solution(mesh):
    in_specs = (
        P(("groups", "src", "tgt"), None),
        P(("groups", "src", "tgt"), None),
        P(("src", "tgt"), None),
        P(("src", "tgt"), None),
        P(("groups", "src", "tgt")),
        P(("groups", "src"), None),
        P(("groups", "tgt"), None),
    )
    out_specs = (P(("groups", "src", "tgt"), None), P(("groups", "src", "tgt")))
    sizes = tuple(mesh.shape[name] for name in ("groups", "src", "tgt"))
    body = fused if sizes == (2, 4, 4) else on_device
    return jax.shard_map(
        body, mesh=mesh, in_specs=in_specs, out_specs=out_specs, check_vma=False
    )
```
